32 devices in a mesh: head: 4 (over x, core), seq: 8 (over z, y).
Axes of the slice: x: 2, y: 2, z: 4, core: 2. Of those that a mesh axis runs over, the one named last changes fastest.
Arguments:
- layer_input: bfloat16 [4, 4096, 768], P('head', 'seq'), may hold values from -6 to 6
- document_start: int32 [16384], P('seq'), may hold values from 0 to 16383, as said below
- ln1_gain: float32 [768], replicated, may hold values from 0.25 to 1.75
- w_qkv: bfloat16 [3, 768, 768], P(None, None, 'head'), may hold values from -0.21875 to 0.21875
- sub_gain_attn: float32 [768], P('head'), may hold values from 0.25 to 1.75
- w_out: bfloat16 [768, 768], P('head'), may hold values from -0.21875 to 0.21875
- ln2_gain: float32 [768], replicated, may hold values from 0.25 to 1.75
- w_in: bfloat16 [768, 3072], P(None, 'head'), may hold values from -0.21875 to 0.21875
- sub_gain_ffn: float32 [3072], P('head'), may hold values from 0.25 to 1.75
- w_ffo: bfloat16 [3072, 768], P('head'), may hold values from -0.109375 to 0.109375
- dy: bfloat16 [16384, 768], P('seq'), may hold values from -6 to 6
Outputs:
- layer_output: bfloat16 [4, 4096, 768], P('head', 'seq')
- dx: float32 [4, 4096, 768], P('head', 'seq')
- g_ln1: float32 [768], replicated
- g_qkv: float32 [3, 768, 768], P(None, None, 'head')
- g_sub_attn: float32 [768], P('head')
- g_out: float32 [768, 768], P('head')
- g_ln2: float32 [768], replicated
- g_in: float32 [768, 3072], P(None, 'head')
- g_sub_ffn: float32 [3072], P('head')
- g_ffo: float32 [3072, 768], P('head')
- denom_means: float32 [2], replicated
The draws below stay inside these ranges and needn't reach their ends.
Inputs may be any that keep to these rules, and one draw needn't show every extreme that they name: document_start[p] is the first position of the sequence that holds position p: document_start[p] <= p, it never falls, and it equals p or document_start[p - 1]. The first sequence holds the first 12288 positions; every later one holds at least 256.
All inputs are finite; a program needn't handle non-finite values.
Results may differ from the reference program's by a relative error of at most 0.015.
Values may be sent and summed in bfloat16 or wider, within the bound.
No kernel may reach another device: no remote copies, remote signals or barrier semaphores. Data moves between devices by JAX's collectives and lax.ppermute only.
A program may use at most 192 MiB of HBM per device.

```python
from functools import partial
import jax
import jax.numpy as jnp
from jax import lax

D = 768
HEAD_NUMBER = 12
HEAD_SIZE = 64
FF = 3072
TOK_DEV = 2048
DILATION_RATE = 16
TOKEN_TOTAL = 16384
QROWS = 512
SEG = 2048
N_HEAD = 4
N_SEQ = 8


def draw_document_start(key, part):
    position_list = jnp.arange(TOKEN_TOTAL, dtype=jnp.int32)
    long_len = 3 * TOKEN_TOTAL // 4
    block_count = (TOKEN_TOTAL - long_len) // TOK_DEV
    shifts = jax.random.randint(key, (block_count,), TOK_DEV // 8, 7 * TOK_DEV // 8, dtype=jnp.int32)
    breaks = long_len + jnp.arange(block_count, dtype=jnp.int32) * TOK_DEV + shifts
    earlier = jnp.concatenate([jnp.full((1,), long_len, jnp.int32), breaks[:-1]])
    block_ids = jnp.clip((position_list - long_len) // TOK_DEV, 0, block_count - 1)
    own_break = breaks[block_ids]
    tail_start = jnp.where(position_list >= own_break, own_break, earlier[block_ids])
    return jnp.where(position_list < long_len, 0, tail_start).astype(jnp.int32)


def steps_of(rng, dims, cuts, smallest, largest):
    def one(dim, shards_of):
        draws = jax.random.uniform(jax.random.fold_in(jax.random.fold_in(rng, 6), dim), (shards_of,), jnp.float32, smallest / len(cuts), largest / len(cuts))
        return jnp.repeat(jnp.exp(draws), dims[dim] // shards_of).reshape((-1,) + (1,) * (len(dims) - dim - 1))

    level = one(*cuts[0])
    for cut in cuts[1:]:
        level = level * one(*cut)
    return level


def bell_draw(rng, dims, width, reach, cuts=(), held_as=jnp.bfloat16):
    result = jax.random.normal(rng, dims, jnp.float32) * width
    if len(cuts) > 0:
        result = steps_of(rng, dims, cuts, -0.22, 0.18) * result
    return jnp.clip(result, min=-reach, max=reach).astype(held_as)


def setup_inputs(seed: int = 0) -> dict:
    key_of = jax.random.split(jax.random.key(seed), 12)
    return {
        "layer_input": bell_draw(key_of[0], (N_HEAD, N_SEQ * QROWS, D), 1.0, 6.0, ((0, 4), (1, 8))),
        "document_start": draw_document_start(jax.random.fold_in(key_of[11], 71), 0),
        "ln1_gain": jnp.clip(1.0 + 0.15 * jax.random.normal(key_of[2], (D,), jnp.float32), 0.25, 1.75),
        "w_qkv": bell_draw(key_of[3], (3, D, D), D ** -0.5, 0.21875, ((2, 4),)),
        "sub_gain_attn": jnp.clip(1.0 + 0.15 * jax.random.normal(key_of[4], (D,), jnp.float32), 0.25, 1.75),
        "w_out": bell_draw(key_of[5], (D, D), D ** -0.5, 0.21875, ((0, 4),)),
        "ln2_gain": jnp.clip(1.0 + 0.15 * jax.random.normal(key_of[6], (D,), jnp.float32), 0.25, 1.75),
        "w_in": bell_draw(key_of[7], (D, FF), D ** -0.5, 0.21875, ((1, 4),)),
        "sub_gain_ffn": jnp.clip(1.0 + 0.15 * jax.random.normal(key_of[8], (FF,), jnp.float32), 0.25, 1.75),
        "w_ffo": bell_draw(key_of[9], (FF, D), FF ** -0.5, 0.109375, ((0, 4),)),
        "dy": bell_draw(key_of[10], (TOKEN_TOTAL, D), 1.0, 6.0, ((0, 8),)),
    }


EPSILON = 1e-05
NEGATIVE = -1e+30
PRECISION_EXACT = lax.Precision.HIGHEST

@jax.custom_vjp
def lower_result(v):
    return lax.optimization_barrier(v.astype(jnp.bfloat16)).astype(jnp.float32)

@jax.custom_vjp
def lower_backward(v):
    return v

def low_keep(v):
    return (lower_result(v), None)

def low_pass(kept, grad):
    return (grad,)

def back_keep(v):
    return (v, None)

def back_low(kept, grad):
    return (lower_result(grad),)
lower_result.defvjp(low_keep, low_pass)
lower_backward.defvjp(back_keep, back_low)

def full_norm(value_matrix, gain):
    mean_row = lax.optimization_barrier(jnp.mean(value_matrix, axis=-1, keepdims=True))
    centred = value_matrix - mean_row
    return centred * lax.rsqrt(lax.optimization_barrier(jnp.mean(centred * centred, axis=-1, keepdims=True)) + EPSILON) * gain

def split_norm(value_matrix, gain):
    mean_row = lax.optimization_barrier(jnp.mean(value_matrix, axis=-1, keepdims=True))
    power = lax.optimization_barrier(jnp.mean(value_matrix * value_matrix, axis=-1, keepdims=True))
    return (value_matrix - mean_row) * lax.rsqrt(power - mean_row * mean_row + EPSILON) * gain

def head_attend(pieces, document_start):
    single_query, single_key, single_value, shift_amount = pieces
    scale_of_scores = HEAD_SIZE ** (-0.5)
    position_list = jnp.arange(TOKEN_TOTAL, dtype=jnp.int32)
    seg_count = TOKEN_TOTAL // SEG
    query_seg = single_query.reshape(seg_count, SEG, HEAD_SIZE)
    key_seg = single_key.reshape(seg_count, SEG, HEAD_SIZE)
    value_seg = single_value.reshape(seg_count, SEG, HEAD_SIZE)
    pos_seg = position_list.reshape(seg_count, SEG)
    start_seg = document_start.reshape(seg_count, SEG)
    mask_near = (pos_seg[:, None, :] <= pos_seg[:, :, None]) & (pos_seg[:, None, :] >= start_seg[:, :, None])
    scores_near = lower_backward(jnp.einsum('sqh,skh->sqk', query_seg, key_seg, precision=PRECISION_EXACT) * scale_of_scores)
    scores_near = jnp.where(mask_near, scores_near, NEGATIVE)
    lse_near = jax.nn.logsumexp(scores_near, axis=-1).reshape(TOKEN_TOTAL)
    dilated_count = TOKEN_TOTAL // DILATION_RATE

    def selection(value_matrix):
        return lax.dynamic_index_in_dim(value_matrix.reshape(dilated_count, DILATION_RATE, -1), shift_amount, axis=1, keepdims=False)
    dilated_query = selection(single_query)
    dilated_key = selection(single_key)
    dilated_value = selection(single_value)
    dilated_positions = jnp.arange(dilated_count, dtype=jnp.int32) * DILATION_RATE + shift_amount
    dilated_start = selection(document_start[:, None])[:, 0]
    distant_mask = (dilated_positions[None, :] <= dilated_positions[:, None]) & (dilated_positions[None, :] >= dilated_start[:, None])
    distant_scores = lower_backward(jnp.dot(dilated_query, dilated_key.T, precision=PRECISION_EXACT) * scale_of_scores)
    distant_scores = jnp.where(distant_mask, distant_scores, NEGATIVE)
    distant_log_sum = jax.nn.logsumexp(distant_scores, axis=-1)
    dilated_flag = position_list % DILATION_RATE == shift_amount
    distant_rows = jnp.repeat(distant_log_sum, DILATION_RATE)
    row_overall = jnp.where(dilated_flag, jnp.logaddexp(lse_near, distant_rows), lse_near)
    total_seg = row_overall.reshape(seg_count, SEG)
    dilated_total = selection(row_overall[:, None])[:, 0]
    prob_near = lower_result(jnp.exp(scores_near - total_seg[:, :, None]))
    nearby_output = jnp.einsum('sqk,skh->sqh', prob_near, value_seg, precision=PRECISION_EXACT).reshape(TOKEN_TOTAL, HEAD_SIZE)
    distant_probability = lower_result(jnp.exp(distant_scores - dilated_total[:, None]))
    distant_output = jnp.dot(distant_probability, dilated_value, precision=PRECISION_EXACT)
    output_rows = nearby_output + jnp.repeat(distant_output, DILATION_RATE, axis=0) * dilated_flag.astype(jnp.float32)[:, None]
    return (output_rows, lse_near, distant_log_sum)

def layer(tokens_seq, ln1_gain, w_qkv, sub_gain_attn, w_out, ln2_gain, w_in, sub_gain_ffn, w_ffo, document_start):
    normed_one = lower_result(full_norm(tokens_seq, ln1_gain))
    project = lower_result(lower_backward(jnp.einsum('td,cde->cte', normed_one, w_qkv, precision=PRECISION_EXACT)))
    per_head = project.reshape(3, TOKEN_TOTAL, HEAD_NUMBER, HEAD_SIZE).transpose(0, 2, 1, 3)
    shift_amounts = jnp.arange(HEAD_NUMBER, dtype=jnp.int32) % DILATION_RATE
    attend = jax.checkpoint(partial(head_attend, document_start=document_start))
    out_heads, lse_near, distant_log_sum = lax.map(attend, (per_head[0], per_head[1], per_head[2], shift_amounts))
    attn_rows = lower_backward(out_heads.transpose(1, 0, 2).reshape(TOKEN_TOTAL, D))
    attn_low = lower_result(split_norm(attn_rows, sub_gain_attn))
    branch = lower_backward(jnp.dot(attn_low, w_out, precision=PRECISION_EXACT))
    resid = tokens_seq + branch
    ffn_input = lower_result(full_norm(resid, ln2_gain))
    hidden_pre = lower_backward(jnp.dot(ffn_input, w_in, precision=PRECISION_EXACT))
    hidden_low = lower_result(split_norm(jax.nn.gelu(hidden_pre, approximate=False), sub_gain_ffn))
    output_seq = resid + jnp.dot(hidden_low, w_ffo, precision=PRECISION_EXACT)
    return (output_seq, (lse_near, distant_log_sum))

def reference(layer_input, document_start, ln1_gain, w_qkv, sub_gain_attn, w_out, ln2_gain, w_in, sub_gain_ffn, w_ffo, dy):
    tokens_seq = layer_input.astype(jnp.float32).reshape(N_HEAD, N_SEQ, QROWS, D).transpose(1, 0, 2, 3).reshape(TOKEN_TOTAL, D)
    params = (tokens_seq, ln1_gain, w_qkv.astype(jnp.float32), sub_gain_attn, w_out.astype(jnp.float32), ln2_gain, w_in.astype(jnp.float32), sub_gain_ffn, w_ffo.astype(jnp.float32))
    output_seq, pullback, logged = jax.vjp(partial(layer, document_start=document_start), *params, has_aux=True)
    grads = pullback(dy.astype(jnp.float32))

    def unorder(value_matrix):
        return value_matrix.reshape(N_SEQ, N_HEAD, QROWS, D).transpose(1, 0, 2, 3).reshape(N_HEAD, N_SEQ * QROWS, D)
    means = jnp.stack([jnp.mean(logged[0]), jnp.mean(logged[1])])
    return (unorder(output_seq).astype(jnp.bfloat16), unorder(grads[0]), grads[1], grads[2], grads[3], grads[4], grads[5], grads[6], grads[7], grads[8], means)
```

```python
import math

import jax
import jax.numpy as jnp
from jax import lax
from jax.experimental import pallas as pl
from jax.experimental.pallas import tpu as pltpu
from jax.sharding import PartitionSpec as P

HEAD_SIZE = 64
DILATION_RATE = 16
EPSILON = 1e-05
NEGATIVE = -1e30
APART = -(2.0**30)
DOC_MIN = 256
GAUSS_NORM = 1.0 / math.sqrt(2.0 * math.pi)
BLOCK = 256
LANES = 256
BF = jnp.bfloat16
F32 = jnp.float32
ERF_P = 0.3275911
ERF_C = (0.254829592, -0.284496736, 1.421413741, -1.453152027, 1.061405429)
SPLIT = 3


def dot(a, b):
    return lax.dot_general(a, b, (((1,), (0,)), ((), ())), preferred_element_type=F32)


def dot_nt(a, b):
    return lax.dot_general(a, b, (((1,), (1,)), ((), ())), preferred_element_type=F32)


def iota(shape, axis):
    return lax.broadcasted_iota(jnp.int32, shape, axis)


def halves(value):
    high = value.astype(BF)
    return high, (value - high.astype(F32)).astype(BF)


def thirds(value):
    high = value.astype(BF)
    rest = value - high.astype(F32)
    middle = rest.astype(BF)
    return high, middle, (rest - middle.astype(F32)).astype(BF)


def fence(value, *before):
    return lax.optimization_barrier((value, *before))[0]


def turned(value):
    return value.astype(F32).T


def room(shape, dtype):
    shape = (1,) * (2 - len(shape)) + tuple(shape)
    size = jnp.dtype(dtype).itemsize
    lanes = (shape[-1] + 127) // 128 * 128
    rows = (shape[-2] + 15) // 16 * 16
    return math.prod(shape[:-2]) * rows * lanes * size


def call(kernel, ins, outs, scratch=(), margin=6, name=None, aliases=None):
    n_in, n_out = len(ins), len(outs)
    spaces = {"s": pltpu.SMEM, "v": pltpu.VMEM, "p": pltpu.VMEM}
    far_in = [i for i, (kind, _) in enumerate(ins) if kind not in spaces]
    far_out = [i for i, (kind, _) in enumerate(outs) if kind not in spaces]
    n_far = len(far_in) + len(far_out)
    far = [ins[i] for i in far_in] + [outs[i] for i in far_out]
    buffers = [pltpu.VMEM(a.shape, a.dtype) for _, a in far]
    counts = [a.shape[0] if kind == "b" else 1 for kind, a in far]

    def wrapped(*refs):
        given, results, rest = list(refs[:n_in]), list(refs[n_in : n_in + n_out]), refs[n_in + n_out :]
        arriving, leaving, started = {}, {}, []

        def copies(kind, n, source, target):
            semaphores = rest[n_far]
            first = sum(counts[:n])
            if kind != "b":
                return {0: pltpu.make_async_copy(source, target, semaphores.at[first])}
            return {
                m: pltpu.make_async_copy(source.at[m], target.at[m], semaphores.at[first + m])
                for m in range(counts[n])
            }

        for n, i in enumerate(far_in):
            arriving[i] = copies(ins[i][0], n, given[i], rest[n])
            for copy in arriving[i].values():
                copy.start()
            given[i] = rest[n]
        for n, i in enumerate(far_out, len(far_in)):
            leaving[i] = copies(outs[i][0], n, rest[n], results[i])
            results[i] = rest[n]

        def need(i, m=0):
            arriving[i].pop(m).wait()

        def done(i, m=0):
            copy = leaving[i].pop(m)
            copy.start()
            started.append(copy)

        for i in far_in:
            if ins[i][0] == "h":
                need(i)
        own = rest[n_far + 1 :] if n_far else rest
        kernel(need, done, *given, *results, *own)
        for i in far_in:
            for m in list(arriving[i]):
                need(i, m)
        for i in far_out:
            for m in list(leaving[i]):
                done(i, m)
        for copy in started:
            copy.wait()

    held = [(a.shape, a.dtype) for kind, a in ins if kind not in "sp"]
    held += [(a.shape, a.dtype) for kind, a in outs if kind != "p"]
    held += [(a.shape, a.dtype) for a in scratch]
    limit = sum(room(*a) for a in held) + (margin << 20)

    def placed(kind, a):
        if kind in "sv":
            return a
        return pltpu.with_memory_space_constraint(a, spaces.get(kind, pltpu.HBM))

    def shape_of(kind, a):
        if kind == "v":
            return a
        return spaces.get(kind, pltpu.HBM)(a.shape, a.dtype)

    return pl.pallas_call(
        wrapped,
        out_shape=tuple(shape_of(*o) for o in outs),
        in_specs=[pl.BlockSpec(memory_space=spaces.get(kind, pltpu.HBM)) for kind, _ in ins],
        out_specs=tuple(pl.BlockSpec(memory_space=spaces.get(kind, pltpu.HBM)) for kind, _ in outs),
        scratch_shapes=[
            *buffers,
            *([pltpu.SemaphoreType.DMA((sum(counts),))] if n_far else []),
            *scratch,
        ],
        input_output_aliases=aliases or {},
        compiler_params=pltpu.CompilerParams(vmem_limit_bytes=limit),
        cost_estimate=pl.CostEstimate(flops=0, transcendentals=0, bytes_accessed=0),
        name=name,
    )(*[placed(*a) for a in ins])


def solution(mesh):
    n_head = mesh.shape["head"]
    n_seq = mesh.shape["seq"]

    def swap(value, axis, bit):
        size = n_head if axis == "head" else n_seq
        return lax.ppermute(value, axis, [(i, i ^ bit) for i in range(size)])

    rising = []
    bit = 1
    while bit < n_seq:
        rising.append(bit)
        bit *= 2
    seq_bits = rising[:1] + rising[:0:-1]

    offsets = [0]
    for bit in seq_bits:
        offsets = offsets + [o ^ bit for o in offsets]

    def body(
        layer_input,
        document_start,
        ln1_gain,
        w_qkv,
        sub_gain_attn,
        w_out,
        ln2_gain,
        w_in,
        sub_gain_ffn,
        w_ffo,
        dy,
    ):
        tokens, width = dy.shape
        quarter = layer_input.shape[1]
        cols = w_qkv.shape[2]
        heads = cols // HEAD_SIZE
        rows_dil = tokens // DILATION_RATE
        ff_part = w_in.shape[1]
        n_blocks = tokens // BLOCK
        n_far = n_seq
        h = lax.axis_index("head")
        s = lax.axis_index("seq")
        h_ref = jnp.reshape(h, (1,)).astype(jnp.int32)
        far_index = (s ^ jnp.array(offsets, jnp.int32)).astype(jnp.int32)
        place = jnp.concatenate([jnp.stack([h, s]).astype(jnp.int32), far_index])
        shaped = jax.ShapeDtypeStruct

        parts = [[] for _ in range(SPLIT)]
        for i in reversed(range(n_blocks)):
            min(parts, key=lambda part: sum(k + 1 for k in part)).append(i)
        parts = [sorted(part) for part in parts if part]
        home = {i: (p, n) for p, part in enumerate(parts) for n, i in enumerate(part)}

        def gather_seq(value, works):
            value = value[None]
            results = []
            for n in range(max(len(seq_bits), len(works))):
                if n < len(works):
                    result, value = works[n](value)
                    results.append(result)
                if n < len(seq_bits):
                    got = swap(value, "seq", seq_bits[n])
                    if n < len(works):
                        got, *results[n] = lax.optimization_barrier((got, *results[n]))
                    value = jnp.concatenate([value, got], 0)
            return value, results

        x_in = layer_input[0]

        def normed(value):
            mu = jnp.mean(value, axis=-1, keepdims=True)
            centred = value - mu
            rs = lax.rsqrt(jnp.mean(centred * centred, axis=-1, keepdims=True) + EPSILON)
            return centred * rs, rs

        def norm_kernel(need, done, x_r, g_r, o):
            o[...] = (normed(x_r[...].astype(F32))[0] * g_r[...]).astype(BF)

        g1_row = ln1_gain.reshape(1, -1)
        (xn,) = call(
            norm_kernel,
            [("h", x_in), ("v", g1_row)],
            [("h", shaped((quarter, width), BF))],
            margin=8,
            name="first_norm",
        )
        xn_core = swap(xn, "head", 1)
        xn_x = swap(xn, "head", 2)

        gain_part = jnp.concatenate([sub_gain_attn, sub_gain_ffn]).reshape(1, -1)
        gain_pair = jnp.concatenate([gain_part, swap(gain_part, "head", 1)], 0)
        gain_rel = jnp.concatenate([gain_pair, swap(gain_pair, "head", 2)], 0)
        gain_attn = gain_rel[:, :cols].reshape(width, 1)
        gain_ffn = gain_rel[:, cols:]
        w_own = jnp.concatenate([w_out, w_in, w_ffo], 0)
        w_core = swap(w_own, "head", 1)
        dy_own = lax.dynamic_slice_in_dim(dy, h * quarter, quarter, 0)

        seg_begin = s * tokens
        doc = jnp.clip((document_start - seg_begin) // DOC_MIN + 1, 0, tokens // DOC_MIN)
        lane = jnp.arange(LANES, dtype=jnp.int32)[None, :]
        same = lane - cols == doc[:, None]
        feature_lane = lane >= cols
        k_feat = jnp.where(same, 1.0, 0.0).astype(BF)
        q_feat = jnp.where(feature_lane & ~same, APART, 0.0).astype(BF)
        shift = (h * heads + jnp.arange(heads, dtype=jnp.int32)) % DILATION_RATE
        start_grid = document_start.reshape(rows_dil, DILATION_RATE)
        pick = jnp.arange(DILATION_RATE, dtype=jnp.int32)[:, None] == shift[None, :]
        start_dil = jnp.sum(jnp.where(pick[None], start_grid[:, :, None], 0), axis=1).T
        start_row = start_dil.reshape(1, heads * rows_dil)

        w_pad = jnp.pad(w_qkv, ((0, 0), (0, 0), (0, LANES - cols)))
        w_turn = w_qkv.transpose(0, 2, 1).reshape(3 * cols, width)
        xn_x = fence(xn_x, w_pad, w_turn, q_feat, k_feat, w_own, dy_own, start_row, gain_attn, gain_ffn)
        xn_diag = swap(xn_x, "head", 1)
        w_x = swap(fence(w_own, xn_x), "head", 2)

        def head_shift(h_value, l):
            return lax.rem(h_value * heads + l, DILATION_RATE)

        def spread(h_value, l):
            a = iota((rows_dil, tokens), 0)
            p = iota((rows_dil, tokens), 1)
            return jnp.where(p == a * DILATION_RATE + head_shift(h_value, l), 1.0, 0.0).astype(BF)

        def of_head(l):
            return slice(l * HEAD_SIZE, (l + 1) * HEAD_SIZE)

        def project_kernel(
            need, done, h_s, b0, b1, b2, b3, w_r, qf, kf,
            q_o, k_o, v_o, kt_o, vt_o, x_o, dil_kv, dil_q, qt_s,
        ):
            hv = h_s[0]
            for r, b in enumerate((b0, b1, b2, b3)):
                base = pl.multiple_of((hv ^ r) * quarter, quarter)
                span = pl.ds(base, quarter)
                xb = b[...]
                x_o[span, :] = xb
                qv = dot(xb, w_r[0]).astype(BF) * BF(HEAD_SIZE**-0.5)
                q_o[span, :] = qv + qf[span, :]
                kv = dot(xb, w_r[1]).astype(BF)
                k_o[span, :] = kv + kf[span, :]
                vv = dot(xb, w_r[2]).astype(BF)
                v_o[span, :] = vv
                qt_s[:, span] = turned(qv)[:cols].astype(BF)
                kt_o[:, span] = turned(kv)[:cols].astype(BF)
                vt_o[:, span] = turned(vv)[:cols].astype(BF)
            done(5)
            for l in range(heads):
                sel = spread(hv, l)
                dil_q[of_head(l), :] = dot_nt(qt_s[of_head(l), :], sel).astype(BF)
                dil_kv[of_head(l), :] = dot_nt(kt_o[of_head(l), :], sel).astype(BF)
                dil_kv[cols + l * HEAD_SIZE : cols + (l + 1) * HEAD_SIZE, :] = dot_nt(
                    vt_o[of_head(l), :], sel
                ).astype(BF)

        q_a, k_a, v_a, k_t, v_t, x_all, dil_kv, dil_q = call(
            project_kernel,
            [
                ("s", h_ref),
                ("v", xn),
                ("v", xn_core),
                ("v", xn_x),
                ("v", xn_diag),
                ("v", w_pad),
                ("v", q_feat),
                ("v", k_feat),
            ],
            [
                ("p", shaped((tokens, LANES), BF)),
                ("p", shaped((tokens, LANES), BF)),
                ("p", shaped((tokens, LANES), BF)),
                ("p", shaped((cols, tokens), BF)),
                ("v", shaped((cols, tokens), BF)),
                ("h", shaped((tokens, width), BF)),
                ("v", shaped((2 * cols, rows_dil), BF)),
                ("v", shaped((cols, rows_dil), BF)),
            ],
            scratch=[pltpu.VMEM((cols, tokens), BF)],
            name="project",
        )

        def stack_heads(value, size=heads):
            keep = iota(value.shape, 1) // HEAD_SIZE
            zero = jnp.zeros_like(value)
            return jnp.concatenate(
                [jnp.where((keep == l) | (keep >= size), value, zero) for l in range(size)], 0
            )

        wide = heads * BLOCK

        def causal_block():
            return iota((BLOCK, wide), 0) <= iota((BLOCK, wide), 1) % BLOCK

        def near_kernel(part, need, done, q_r, k_r, vt_r, o_o, lse_o):
            for n, i in enumerate(part):
                q_i = stack_heads(q_r[i * BLOCK : (i + 1) * BLOCK, :])
                top = total = None
                outs = None
                for j in [i] + list(range(i)):
                    sc = dot_nt(k_r[j * BLOCK : (j + 1) * BLOCK, :], q_i)
                    if j == i:
                        sc = jnp.where(causal_block(), sc, NEGATIVE)
                    part_top = jnp.max(sc, axis=0, keepdims=True)
                    new_top = part_top if top is None else jnp.maximum(top, part_top)
                    pr = jnp.exp(sc - new_top)
                    part_sum = jnp.sum(pr, axis=0, keepdims=True)
                    pb = pr.astype(BF)
                    fresh = [
                        dot(
                            vt_r[of_head(l), j * BLOCK : (j + 1) * BLOCK],
                            pb[:, l * BLOCK : (l + 1) * BLOCK],
                        )
                        for l in range(heads)
                    ]
                    if top is None:
                        total, outs = part_sum, fresh
                    else:
                        shrink = jnp.exp(top - new_top)
                        total = total * shrink + part_sum
                        outs = [
                            o * shrink[:, l * BLOCK : (l + 1) * BLOCK] + f
                            for l, (o, f) in enumerate(zip(outs, fresh))
                        ]
                    top = new_top
                lse = top + jnp.log(total)
                inv = 1.0 / total
                for l in range(heads):
                    cut = slice(l * BLOCK, (l + 1) * BLOCK)
                    o_o[of_head(l), n * BLOCK : (n + 1) * BLOCK] = outs[l] * inv[:, cut]
                    lse_o[l : l + 1, n * BLOCK : (n + 1) * BLOCK] = lse[:, cut]

        def near_work(part):
            def work(value):
                q_b, value = lax.optimization_barrier((q_a, value))
                size = len(part) * BLOCK
                result = call(
                    lambda *refs: near_kernel(part, *refs),
                    [("p", q_b), ("p", k_a), ("v", v_t)],
                    [("v", shaped((cols, size), F32)), ("v", shaped((heads, size), F32))],
                    name="near_forward",
                    margin=24,
                )
                return result, value

            return work

        far_kv, near_out = gather_seq(dil_kv, [near_work(part) for part in parts])
        near_o = [o for o, _ in near_out]
        near_lse = [lse for _, lse in near_out]
        n_parts = len(parts)

        def joined(refs, rows):
            pieces = []
            for i in range(n_blocks):
                p, n = home[i]
                pieces.append(refs[p][rows, n * BLOCK : (n + 1) * BLOCK])
            return jnp.concatenate(pieces, 1)

        def stack_dil(value):
            keep = iota(value.shape, 1) // HEAD_SIZE
            zero = jnp.zeros_like(value)
            return jnp.concatenate([jnp.where(keep == l, value, zero) for l in range(heads)], 0)

        far_wide = heads * rows_dil

        def far_place(p_s, key_owner, query_owner):
            col = iota((rows_dil, far_wide), 1)
            off = lax.rem(p_s[0] * heads + col // rows_dil, DILATION_RATE)
            key = key_owner * tokens + iota((rows_dil, far_wide), 0) * DILATION_RATE + off
            query = query_owner * tokens + (col % rows_dil) * DILATION_RATE + off
            return key, query

        def far_kernel(need, done, *refs):
            p_s, q_r, kv_r, start_r = refs[:4]
            o_r = refs[4 : 4 + n_parts]
            lse_r = refs[4 + n_parts : 4 + 2 * n_parts]
            ao_o, l_o, ldil_o, sum_o, *aob, top_s, total_s, out_s, low_s = refs[4 + 2 * n_parts :]
            hv = p_s[0]
            sv = p_s[1]
            q_v = stack_dil(turned(q_r[...]).astype(BF))
            start_v = start_r[...]
            top_s[...] = jnp.full((8, far_wide), NEGATIVE, F32)
            total_s[...] = jnp.zeros((8, far_wide), F32)
            out_s[...] = jnp.zeros((HEAD_SIZE, far_wide), F32)

            @pl.loop(0, n_far)
            def _(b):
                owner = p_s[2 + b]

                @pl.when(owner <= sv)
                def _():
                    top = top_s[:1]
                    sc = dot_nt(turned(kv_r[b, :cols]).astype(BF), q_v)
                    key, query = far_place(p_s, owner, sv)
                    sc = jnp.where((key <= query) & (key >= start_v), sc, NEGATIVE)
                    new_top = jnp.maximum(top, jnp.max(sc, axis=0, keepdims=True))
                    pr = jnp.exp(sc - new_top)
                    shrink = jnp.exp(top - new_top)
                    total_s[:1] = total_s[:1] * shrink + jnp.sum(pr, axis=0, keepdims=True)
                    pb = pr.astype(BF)
                    fresh = jnp.concatenate(
                        [
                            dot(
                                kv_r[b, cols + l * HEAD_SIZE : cols + (l + 1) * HEAD_SIZE],
                                pb[:, l * rows_dil : (l + 1) * rows_dil],
                            )
                            for l in range(heads)
                        ],
                        1,
                    )
                    out_s[...] = out_s[...] * shrink + fresh
                    top_s[:1] = new_top

            sum_o[...] = jnp.zeros((8, 128), F32)
            total = total_s[:1]
            lse_far = top_s[:1] + jnp.log(total)
            out = out_s[...] / total
            for l in range(heads):
                cut = slice(l * rows_dil, (l + 1) * rows_dil)
                rows = of_head(l)
                lf = lse_far[:, cut]
                sum_o[1:2, :] += lf
                put = spread(hv, l)
                l8 = jnp.broadcast_to(lf, (8, rows_dil))
                full_lf = sum(dot(t, put) for t in thirds(l8))[:1]
                high, low = halves(out[:, cut])
                full_o = dot(high, put) + dot(low, put)
                dilated = iota((1, tokens), 1) % DILATION_RATE == head_shift(hv, l)
                ln = joined(lse_r, slice(l, l + 1))
                for part in range(tokens // 128):
                    sum_o[:1, :] += ln[:, part * 128 : (part + 1) * 128]
                peak = jnp.maximum(ln, full_lf)
                both = peak + jnp.log(jnp.exp(ln - peak) + jnp.exp(full_lf - peak))
                tot = jnp.where(dilated, both, ln)
                w_near = jnp.exp(ln - tot)
                w_far = jnp.where(dilated, jnp.exp(full_lf - tot), 0.0)
                ao = joined(o_r, rows) * w_near + full_o * w_far
                ao_o[rows, :] = ao
                low_s[rows, :] = ao.astype(BF)
                l_o[l : l + 1, :] = tot
                t8 = jnp.broadcast_to(tot, (8, tokens))
                ldil_o[l : l + 1, :] = sum(dot_nt(t, put) for t in thirds(t8))[:1]
            for r, o in enumerate(aob):
                base = pl.multiple_of((hv ^ r) * quarter, quarter)
                o[...] = low_s[:, pl.ds(base, quarter)]

        ao_t, l_all, l_dil, lse_sums, *ao_low = call(
            far_kernel,
            [
                ("s", place),
                ("v", dil_q),
                ("v", far_kv),
                ("v", start_row),
                *[("v", o) for o in near_o],
                *[("v", lse) for lse in near_lse],
            ],
            [
                ("v", shaped((cols, tokens), F32)),
                ("v", shaped((heads, tokens), F32)),
                ("v", shaped((heads, rows_dil), F32)),
                ("v", shaped((8, 128), F32)),
                *[("v", shaped((cols, quarter), BF))] * n_head,
            ],
            scratch=[
                pltpu.VMEM((8, far_wide), F32),
                pltpu.VMEM((8, far_wide), F32),
                pltpu.VMEM((HEAD_SIZE, far_wide), F32),
                pltpu.VMEM((cols, tokens), BF),
            ],
            name="far_forward",
        )

        def exchange(pieces):
            return [pieces[0]] + [swap(pieces[r], "head", r) for r in range(1, n_head)]

        ao_rows = exchange(ao_low)
        w_x = fence(w_x, ao_low[0])
        w_rel = (w_own, w_core, w_x, swap(w_x, "head", 1))

        full_ff = ff_part * n_head
        chunk = min(BLOCK, quarter)
        order = (1, 3, 0, 2)
        slot = {r: n for n, r in enumerate(order)}

        def row_kernel(
            need, done, x_r, a0, a1, a2, a3, w0, w1, w2, w3, dy_r, ga_r, gf_r, g2_r,
            y_o, an_o, dhb_o, hn_o, gn_o, du_o, dao0, dao1, dao2, dao3, dh_o, va_o, vf_o, v2_o,
            gu_s, slope_s, dgn_s, w_out_s, hid_s,
        ):
            ws = (w0, w1, w2, w3)
            ao = jnp.concatenate([a[...].astype(F32) for a in (a0, a1, a2, a3)], 0)
            mu_a = jnp.mean(ao, axis=0, keepdims=True)
            power = jnp.mean(ao * ao, axis=0, keepdims=True)
            rs_a = lax.rsqrt(power - mu_a * mu_a + EPSILON)
            ahat = (ao - mu_a) * rs_a
            an_t = (ahat * ga_r[...]).astype(BF)
            an_o[...] = an_t
            for r, w in enumerate(ws):
                need(5 + r)
                w_out_s[r * cols : (r + 1) * cols, :] = w[:cols, :]
            hid_s[...] = x_r[...].astype(F32) + dot(turned(an_t).astype(BF), w_out_s[...])
            g2 = g2_r[...]
            vf_o[...] = jnp.zeros((n_head, ff_part), F32)
            v2_o[...] = jnp.zeros((1, width), F32)
            for c in range(quarter // chunk):
                span = slice(c * chunk, (c + 1) * chunk)
                hid = hid_s[span, :]
                mu2 = jnp.mean(hid, axis=-1, keepdims=True)
                centred = hid - mu2
                rs2 = lax.rsqrt(jnp.mean(centred * centred, axis=-1, keepdims=True) + EPSILON)
                xhat2 = centred * rs2
                hn = (xhat2 * g2).astype(BF)
                hn_o[span, :] = hn
                if c == 0:
                    need(9)
                dy_c = dy_r[span, :]
                sums = [jnp.zeros((chunk, 1), F32)] * 4
                for r, w in enumerate(ws):
                    u = dot(hn, w[cols : cols + width, :])
                    bell = jnp.exp(u * u * -0.5)
                    t = 1.0 / (1.0 + jnp.abs(u) * (ERF_P / math.sqrt(2.0)))
                    poly = ERF_C[4]
                    for coefficient in ERF_C[3::-1]:
                        poly = poly * t + coefficient
                    tail = poly * t * bell * 0.5
                    phi = jnp.where(u >= 0.0, 1.0 - tail, tail)
                    gu = u * phi
                    dgn = dot_nt(dy_c, w[cols + width :, :])
                    c_g = dgn * gf_r[r : r + 1, :]
                    gu_s[r] = gu
                    slope_s[r] = phi + u * bell * GAUSS_NORM
                    dgn_s[r] = dgn
                    terms = (gu, gu * gu, c_g, c_g * gu)
                    sums = [a + jnp.sum(b, axis=-1, keepdims=True) for a, b in zip(sums, terms)]
                mu_g = sums[0] / full_ff
                rs_g = lax.rsqrt(sums[1] / full_ff - mu_g * mu_g + EPSILON)
                m1 = sums[2] / full_ff
                m2 = (sums[3] - mu_g * sums[2]) * rs_g / full_ff
                y = hid
                dhn = jnp.zeros((chunk, width), F32)
                for r, w in enumerate(ws):
                    gf = gf_r[r : r + 1, :]
                    ghat = (gu_s[r] - mu_g) * rs_g
                    dgn = dgn_s[r]
                    gn = (ghat * gf).astype(BF)
                    du = (rs_g * (dgn * gf - m1 - ghat * m2) * slope_s[r]).astype(BF)
                    gn_o[slot[r], span, :] = gn
                    du_o[slot[r], span, :] = du
                    vf_o[r : r + 1, :] += jnp.sum(dgn * ghat, axis=0, keepdims=True)
                    y = y + dot(gn, w[cols + width :, :])
                    dhn = dhn + dot_nt(du, w[cols : cols + width, :])
                y_o[span, :] = y.astype(BF)
                v2_o[...] += jnp.sum(dhn * xhat2, axis=0, keepdims=True)
                c2 = dhn * g2
                dh = dy_c.astype(F32) + rs2 * (
                    c2
                    - jnp.mean(c2, axis=-1, keepdims=True)
                    - xhat2 * jnp.mean(c2 * xhat2, axis=-1, keepdims=True)
                )
                dh_o[span, :] = dh
                dhb_o[span, :] = dh.astype(BF)
            for k in (0, 1, 2, 3, 4, 5, 10):
                done(k)
            dan = dot_nt(w_out_s[...], dhb_o[...])
            column = jnp.sum(dan * ahat, axis=-1, keepdims=True)
            va_o[...] = jnp.broadcast_to(column, (width, 128)).T[:1]
            c_a = dan * ga_r[...]
            dao = rs_a * (
                c_a
                - jnp.mean(c_a, axis=0, keepdims=True)
                - ahat * jnp.mean(c_a * ahat, axis=0, keepdims=True)
            )
            for r, o in enumerate((dao0, dao1, dao2, dao3)):
                o[...] = dao[r * cols : (r + 1) * cols].astype(BF)

        y_rows, an_t, dhb, hn2, gn, du, *dao_low, dh, v_attn, v_ffn, v_ln2 = call(
            row_kernel,
            [
                ("h", x_in),
                *[("h", a) for a in ao_rows],
                *[("l", w) for w in w_rel],
                ("l", dy_own),
                ("v", gain_attn),
                ("v", gain_ffn),
                ("v", ln2_gain.reshape(1, -1)),
            ],
            [
                ("h", shaped((quarter, width), BF)),
                ("h", shaped((width, quarter), BF)),
                ("h", shaped((quarter, width), BF)),
                ("h", shaped((quarter, width), BF)),
                ("h", shaped((n_head, quarter, ff_part), BF)),
                ("h", shaped((n_head, quarter, ff_part), BF)),
                *[("v", shaped((cols, quarter), BF))] * n_head,
                ("h", shaped((quarter, width), F32)),
                ("v", shaped((1, width), F32)),
                ("v", shaped((n_head, ff_part), F32)),
                ("v", shaped((1, width), F32)),
            ],
            scratch=[
                pltpu.VMEM((n_head, chunk, ff_part), F32),
                pltpu.VMEM((n_head, chunk, ff_part), F32),
                pltpu.VMEM((n_head, chunk, ff_part), F32),
                pltpu.VMEM((width, width), BF),
                pltpu.VMEM((quarter, width), F32),
            ],
            margin=12,
            name="rows",
        )
        output = y_rows[None]
        dao_blocks = exchange(dao_low)


        def dot_tn(a, b):
            return lax.dot_general(a, b, (((0,), (0,)), ((), ())), preferred_element_type=F32)

        def ffo_kernel(need, done, gn_r, dy_r, send_o, own_o, side_o):
            for n, o in enumerate((send_o.at[0], send_o.at[1], own_o, side_o)):
                o[...] = dot_tn(gn_r[n], dy_r[...]).astype(BF)

        def in_kernel(need, done, hn_r, du_r, an_r, dhb_r, send_o, keep_o):
            for n, r in enumerate(order):
                o = send_o if n < 2 else keep_o
                o[n % 2, :width] = dot_tn(hn_r[...], du_r[n]).astype(BF)
                rows = an_r[r * cols : (r + 1) * cols, :]
                o[n % 2, width:] = dot(rows, dhb_r[...]).astype(BF)

        one = ("v", shaped((ff_part, width), BF))
        ffo_send, ffo_own, ffo_side = call(
            ffo_kernel,
            [("v", gn), ("v", dy_own)],
            [("v", shaped((2, ff_part, width), BF)), one, one],
            name="ffo_gradient",
        )
        grad = ("v", shaped((2, width + cols, width), BF))
        in_send, in_keep = call(
            in_kernel,
            [("v", hn2), ("v", du), ("v", an_t), ("v", dhb)],
            [grad, grad],
            name="in_gradient",
        )

        def plus(*terms):
            return sum(t.astype(F32) for t in terms).astype(BF)

        def half_seq(terms, axis, bit):
            size = terms[0].shape[axis] // 2
            upper = (s & bit) != 0
            away = jnp.where(upper, 0, size)

            def cut(t, at):
                return lax.dynamic_slice_in_dim(t, at, size, axis)

            return plus(*[cut(t, away) for t in terms]), [cut(t, size - away) for t in terms]

        def joined_seq(own, got, bit):
            upper = (s & bit) != 0
            return jnp.where(upper, jnp.concatenate([got, own], 0), jnp.concatenate([own, got], 0))

        n_note = 3 * heads
        note_rows = (3 * n_note + 15) // 16 * 16

        def prepare_kernel(
            need, done, h_s, d0, d1, d2, d3, ao_r, q_r, l_r, start_r, do_o, delta_o, sent_o, ddil_o, dt_s
        ):
            hv = h_s[0]
            for r, d in enumerate((d0, d1, d2, d3)):
                base = pl.multiple_of((hv ^ r) * quarter, quarter)
                dt_s[:, pl.ds(base, quarter)] = d[...]
            dao_v = dt_s[...].astype(F32)
            grown = jnp.concatenate([dao_v, jnp.zeros((LANES - cols, tokens), F32)], 0)
            do_o[...] = grown.T.astype(BF)
            prod = dao_v * ao_r[...]
            sent_o[:cols, :] = q_r[...]
            for l in range(heads):
                sel = spread(hv, l)
                at = cols + l * HEAD_SIZE
                sent_o[at : at + HEAD_SIZE, :] = dot_nt(dt_s[of_head(l), :], sel).astype(BF)
                delta = jnp.sum(prod[of_head(l)], axis=0, keepdims=True)
                delta_o[l : l + 1, :] = delta
                d8 = jnp.broadcast_to(delta, (8, tokens))
                ddil_o[l : l + 1, :] = sum(dot_nt(t, sel) for t in thirds(d8))[:1]
            found = [l_r[l : l + 1, :] for l in range(heads)]
            found += [ddil_o[l : l + 1, :] for l in range(heads)]
            found += [start_r[l : l + 1, :].astype(F32) for l in range(heads)]
            row = iota((note_rows, rows_dil), 0)
            notes = jnp.zeros((note_rows, rows_dil), F32)
            for n, value in enumerate(found):
                for t, piece in enumerate(thirds(value)):
                    notes = jnp.where(row == t * n_note + n, piece.astype(F32), notes)
            sent_o[2 * cols :, :] = notes.astype(BF)

        do_a, delta_all, far_note, delta_dil = call(
            prepare_kernel,
            [
                ("s", h_ref),
                ("h", fence(dao_blocks[0], ffo_send, in_send)),
                *[("h", d) for d in dao_blocks[1:]],
                ("v", ao_t),
                ("v", dil_q),
                ("v", l_dil),
                ("v", start_dil),
            ],
            [
                ("p", shaped((tokens, LANES), BF)),
                ("v", shaped((heads, tokens), F32)),
                ("v", shaped((2 * cols + note_rows, rows_dil), BF)),
                ("v", shaped((heads, rows_dil), F32)),
            ],
            scratch=[pltpu.VMEM((cols, tokens), BF)],
            name="prepare_backward",
        )

        def near_back_kernel(part, need, done, q_r, k_r, v_r, kt_r, do_r, l_r, d_r, *rest):
            dq_o, dk_o, dv_o = rest[-3:]
            fresh = len(rest) == 3
            for n, i in enumerate(reversed(part)):
                span = slice(i * BLOCK, (i + 1) * BLOCK)
                q_i = stack_heads(q_r[span, :])
                do_i = stack_heads(do_r[span, :])
                lse_i = jnp.concatenate([l_r[l : l + 1, span] for l in range(heads)], 1)
                del_i = jnp.concatenate([d_r[l : l + 1, span] for l in range(heads)], 1)
                dq_i = [None] * heads
                for j in range(i + 1):
                    keys = slice(j * BLOCK, (j + 1) * BLOCK)
                    pr = jnp.exp(dot_nt(k_r[keys, :], q_i) - lse_i)
                    if j == i:
                        pr = jnp.where(causal_block(), pr, 0.0)
                    dp = dot_nt(v_r[keys, :], do_i)
                    ds = (pr * (dp - del_i)).astype(BF)
                    dv = dot(pr.astype(BF), do_i)
                    dk = dot(ds, q_i)
                    if fresh and n == 0:
                        dv_o[keys, :] = dv
                        dk_o[keys, :] = dk
                    else:
                        dv_o[keys, :] += dv
                        dk_o[keys, :] += dk
                    for l in range(heads):
                        add = dot(kt_r[of_head(l), keys], ds[:, l * BLOCK : (l + 1) * BLOCK])
                        dq_i[l] = add if dq_i[l] is None else dq_i[l] + add
                for l in range(heads):
                    dq_o[of_head(l), span] = dq_i[l]

        grown_to = []

        def back_work(part):
            def work(value):
                q_b, value = lax.optimization_barrier((q_a, value))
                if part is parts[min(1, n_parts - 1)]:
                    q_b = start_sums(q_b)
                held = [("p", a) for a in grown_to]
                grown_to[:] = call(
                    lambda *refs: near_back_kernel(part, *refs),
                    [
                        ("p", q_b),
                        ("p", k_a),
                        ("p", v_a),
                        ("p", k_t),
                        ("p", do_a),
                        ("v", l_all),
                        ("v", delta_all),
                        *held,
                    ],
                    [
                        ("p", shaped((cols, tokens), F32)),
                        ("p", shaped((tokens, LANES), F32)),
                        ("p", shaped((tokens, LANES), F32)),
                    ],
                    name="near_backward",
                    margin=20,
                    aliases={7 + n: n for n in range(len(held))},
                )
                return grown_to, value

            return work

        ffo_send, in_send, far_note = lax.optimization_barrier((ffo_send, in_send, far_note))
        ffo_core = swap(ffo_send, "head", 1)
        in_core = swap(in_send, "head", 1)
        flying = {}

        def start_sums(q_b):
            flying["ffo_x"] = plus(ffo_side, ffo_core[1])
            flying["in_y"], flying["in_own"] = half_seq([in_keep, in_core], 1, rising[0])
            sent = lax.optimization_barrier((flying["ffo_x"], flying["in_y"], q_b))
            flying["ffo_got"] = swap(sent[0], "head", 2)
            flying["in_got"] = swap(sent[1], "seq", rising[0])
            return sent[2]

        far_q, back_out = gather_seq(far_note, [back_work(part) for part in parts])
        dq_near, dk_near, dv_near = grown_to
        ffo_got, in_got, far_q = lax.optimization_barrier((flying["ffo_got"], flying["in_got"], far_q))
        ffo_z, ffo_kept = half_seq([ffo_own, ffo_core[0], ffo_got], 0, rising[-1])
        in_x = plus(in_got[1], *[t[1] for t in flying["in_own"]])
        ffo_z, in_x, far_q = lax.optimization_barrier((ffo_z, in_x, far_q))
        ffo_z_got = swap(ffo_z, "seq", rising[-1])
        in_x_got = swap(in_x, "head", 2)

        def far_back_kernel(need, done, *refs):
            p_s, kv_r, fq_r, start_r, l_r, d_r = refs[:6]
            dqn_r, dkn_r, dvn_r, w_r, x_r, g_r, send_o, keep_o, part_o, v_o, d_o, dq_s, dk_s, dv_s = refs[6:]
            hv = p_s[0]
            sv = p_s[1]

            def rows_of(ref, b, first):
                return turned(ref[b, first : first + cols]).astype(BF)

            q_v = stack_dil(rows_of(fq_r, 0, 0))
            do_v = stack_dil(rows_of(fq_r, 0, cols))
            k_own = rows_of(kv_r, 0, 0)
            v_own = rows_of(kv_r, 0, cols)
            start_v = start_r[...]
            l_v = jnp.concatenate([l_r[l : l + 1, :] for l in range(heads)], 1)
            d_v = jnp.concatenate([d_r[l : l + 1, :] for l in range(heads)], 1)
            dq_s[...] = jnp.zeros_like(dq_s)
            dk_s[...] = jnp.zeros_like(dk_s)
            dv_s[...] = jnp.zeros_like(dv_s)

            @pl.loop(0, n_far)
            def _(b):
                owner = p_s[2 + b]

                @pl.when(owner <= sv)
                def _():
                    key, query = far_place(p_s, owner, sv)
                    keep = (key <= query) & (key >= start_v)
                    sc = dot_nt(rows_of(kv_r, b, 0), q_v)
                    pr = jnp.where(keep, jnp.exp(sc - l_v), 0.0)
                    dp = dot_nt(rows_of(kv_r, b, cols), do_v)
                    ds = (pr * (dp - d_v)).astype(BF)
                    for l in range(heads):
                        cut = slice(l * rows_dil, (l + 1) * rows_dil)
                        dq_s[of_head(l), :] += dot(kv_r[b, of_head(l)], ds[:, cut])

                @pl.when(owner >= sv)
                def _():
                    note = fq_r[b, 2 * cols :].astype(F32)

                    def row(kind):
                        found = []
                        for l in range(heads):
                            at = kind * heads + l
                            found.append(
                                sum(note[at + t * n_note : at + t * n_note + 1] for t in range(3))
                            )
                        return jnp.concatenate(found, 1)

                    key, query = far_place(p_s, sv, owner)
                    keep = (key <= query) & (key >= row(2).astype(jnp.int32))
                    q_b = stack_dil(rows_of(fq_r, b, 0))
                    do_b = stack_dil(rows_of(fq_r, b, cols))
                    sc = dot_nt(k_own, q_b)
                    pr = jnp.where(keep, jnp.exp(sc - row(0)), 0.0)
                    dp = dot_nt(v_own, do_b)
                    ds = (pr * (dp - row(1))).astype(BF)
                    dk_s[...] += dot(ds, q_b)
                    dv_s[...] += dot(pr.astype(BF), do_b)

            dk_t = turned(dk_s[...])
            dv_t = turned(dv_s[...])

            def placed(value, l):
                high, low = halves(value[of_head(l)])
                put = spread(hv, l)
                return dot(high, put) + dot(low, put)

            dk_near = dkn_r[...].T
            dv_near = dvn_r[...].T
            scale = HEAD_SIZE**-0.5
            dq_far = dq_s[...]
            for l in range(heads):
                rows = of_head(l)
                d_o[rows, :] = ((dqn_r[rows, :] + placed(dq_far, l)) * scale).astype(BF)
                at = cols + l * HEAD_SIZE
                d_o[at : at + HEAD_SIZE, :] = (dk_near[rows] + placed(dk_t, l)).astype(BF)
                at += cols
                d_o[at : at + HEAD_SIZE, :] = (dv_near[rows] + placed(dv_t, l)).astype(BF)
            for o, n, r in ((send_o, 0, 3), (send_o, 1, 1), (keep_o, 0, 2), (keep_o, 1, 0)):
                base = pl.multiple_of((hv ^ r) * quarter, quarter)
                o[n] = dot_tn(d_o[:, pl.ds(base, quarter)], w_r[...]).astype(o.dtype)
            need(10)
            part = dot(d_o[...], x_r[...])
            part_o[...] = part.astype(BF)
            v_o[...] = jnp.sum(part * w_r[...].astype(F32), axis=0, keepdims=True) / g_r[...]

        dxn_send, dxn_keep, g_part, v_ln1 = call(
            far_back_kernel,
            [
                ("s", place),
                ("v", far_kv),
                ("v", far_q),
                ("v", start_row),
                ("v", l_dil),
                ("v", delta_dil),
                ("p", dq_near),
                ("p", dk_near),
                ("p", dv_near),
                ("v", w_turn),
                ("l", x_all),
                ("v", g1_row),
            ],
            [
                ("v", shaped((2, quarter, width), BF)),
                ("v", shaped((2, quarter, width), F32)),
                ("v", shaped((3 * cols, width), BF)),
                ("v", shaped((1, width), F32)),
            ],
            scratch=[
                pltpu.VMEM((3 * cols, tokens), BF),
                pltpu.VMEM((cols, rows_dil), F32),
                pltpu.VMEM((rows_dil, cols), F32),
                pltpu.VMEM((rows_dil, cols), F32),
            ],
            margin=10,
            name="far_backward",
        )

        dxn_send, ffo_z_got, in_x_got = lax.optimization_barrier((dxn_send, ffo_z_got, in_x_got))

        def sum_rows():
            got = yield dxn_send, "head", 1, 1
            side = (dxn_keep[0] + got[0].astype(F32)).astype(BF)
            over_x = yield side, "head", 2, 3

            def last_kernel(need, done, x_r, g_r, keep_r, got_r, over_r, dh_r, o):
                xhat, rs = normed(x_r[...].astype(F32))
                dxn = keep_r[1] + got_r[1].astype(F32) + over_r[...].astype(F32)
                c = dxn * g_r[...]
                first = jnp.mean(c, axis=-1, keepdims=True)
                second = jnp.mean(c * xhat, axis=-1, keepdims=True)
                o[...] = dh_r[...] + rs * (c - first - xhat * second)

            (result,) = call(
                last_kernel,
                [("v", x_in), ("v", g1_row), ("v", dxn_keep), ("v", got), ("v", over_x), ("v", dh)],
                [("v", shaped((quarter, width), F32))],
                margin=12,
                name="first_norm_backward",
            )
            return result

        def sum_seq(terms, scatter, spread, last=1):
            for bit in scatter:
                send, kept = half_seq(terms, 0, bit)
                terms = [*kept, (yield send, "seq", bit, 1)]
            value = plus(*terms)
            for bit in spread:
                rounds = last if bit == spread[-1] else 1
                value = joined_seq(value, (yield value, "seq", bit, rounds), bit)
            return value

        def sum_ffo():
            bits = rising[-2:0:-1] + rising[:1]
            return (yield from sum_seq([*ffo_kept, ffo_z_got], bits, bits[::-1] + rising[-1:]))

        def sum_in():
            terms = [in_got[0], *[t[0] for t in flying["in_own"]], in_x_got]
            return (yield from sum_seq([plus(*terms)], rising[1:], rising[::-1], 2))

        def sum_qkv():
            return (yield from sum_seq([g_part], rising, rising[::-1]))

        def sum_small():
            v_rel = jnp.concatenate([v_attn.reshape(n_head, cols), v_ffn], 1)
            size = v_rel.shape[1]
            common = jnp.concatenate([v_ln1.reshape(-1), v_ln2.reshape(-1), lse_sums[:2].reshape(-1)])
            got = yield jnp.concatenate([v_rel[1], v_rel[3], common]), "head", 1, 1
            mine = v_rel[0] + got[:size]
            other = v_rel[2] + got[size : 2 * size]
            common = common + got[2 * size :]
            got = yield jnp.concatenate([other, common]), "head", 2, 1
            small = jnp.concatenate([mine, common]) + got
            for bit in rising:
                small = small + (yield small, "seq", bit, 1)
            return small

        def in_rounds(chains):
            results = [None] * len(chains)
            asks = {n: next(chain) for n, chain in enumerate(chains)}
            flying = {}
            number = 0
            while asks or flying:
                ready = list(asks)
                for n in ready:
                    value, axis, bit, rounds = asks[n]
                    flying[n] = (number + rounds - 1, swap(value, axis, bit))
                due = [n for n in flying if flying[n][0] <= number]
                held = lax.optimization_barrier(tuple(flying.pop(n)[1] for n in due))
                asks = {}
                for n, got in zip(due, held):
                    try:
                        asks[n] = chains[n].send(got)
                    except StopIteration as stop:
                        results[n] = stop.value
                number += 1
            return results

        dx, g_ffo, g_in_out, g_qkv, small = in_rounds(
            [
                sum_rows(),
                sum_ffo(),
                sum_in(),
                sum_qkv(),
                sum_small(),
            ]
        )
        g_in = g_in_out[:width].astype(F32)
        g_out = g_in_out[width:].astype(F32)
        g_qkv = g_qkv.astype(F32).reshape(3, cols, width).transpose(0, 2, 1)
        size = cols + ff_part
        g_sub_attn = small[:cols]
        g_sub_ffn = small[cols:size]
        g_ln1 = small[size : size + width]
        g_ln2 = small[size + width : size + 2 * width]
        total_heads = heads * n_head
        counts = jnp.array([tokens * n_seq * total_heads, rows_dil * n_seq * total_heads], F32)
        means = jnp.sum(small[size + 2 * width :].reshape(2, 128), axis=1) / counts
        return (
            output,
            dx[None],
            g_ln1,
            g_qkv,
            g_sub_attn,
            g_out,
            g_ln2,
            g_in,
            g_sub_ffn,
            g_ffo.astype(F32),
            means,
        )

    return jax.shard_map(
        body,
        mesh=mesh,
        in_specs=(
            P("head", "seq", None),
            P("seq"),
            P(),
            P(None, None, "head"),
            P("head"),
            P("head", None),
            P(),
            P(None, "head"),
            P("head"),
            P("head", None),
            P("seq", None),
        ),
        out_specs=(
            P("head", "seq", None),
            P("head", "seq", None),
            P(),
            P(None, None, "head"),
            P("head"),
            P("head", None),
            P(),
            P(None, "head"),
            P("head"),
            P("head", None),
            P(),
        ),
        check_vma=False,
    )
```

```python
import math

import jax
import jax.numpy as jnp
from jax import lax
from jax.experimental import pallas as pl
from jax.experimental.pallas import tpu as pltpu
from jax.sharding import PartitionSpec as P

HEAD_SIZE = 64
DILATION_RATE = 16
EPSILON = 1e-05
NEGATIVE = -1e30
APART = -(2.0**30)
DOC_MIN = 256
GAUSS_NORM = 1.0 / math.sqrt(2.0 * math.pi)
BLOCK = 256
LANES = 256
BF = jnp.bfloat16
F32 = jnp.float32
ERF_P = 0.3275911
ERF_C = (0.254829592, -0.284496736, 1.421413741, -1.453152027, 1.061405429)
SPLIT = 3
PIECES = 2
CHUNK = 256


def dot(a, b):
    return lax.dot_general(a, b, (((1,), (0,)), ((), ())), preferred_element_type=F32)


def dot_nt(a, b):
    return lax.dot_general(a, b, (((1,), (1,)), ((), ())), preferred_element_type=F32)


def dot_tn(a, b):
    return lax.dot_general(a, b, (((0,), (0,)), ((), ())), preferred_element_type=F32)


def iota(shape, axis):
    return lax.broadcasted_iota(jnp.int32, shape, axis)


def halves(value):
    high = value.astype(BF)
    return high, (value - high.astype(F32)).astype(BF)


def thirds(value):
    high = value.astype(BF)
    rest = value - high.astype(F32)
    middle = rest.astype(BF)
    return high, middle, (rest - middle.astype(F32)).astype(BF)


def fence(value, *before):
    return lax.optimization_barrier((value, *before))[0]


def turned(value):
    return value.astype(F32).T


def room(shape, dtype):
    shape = (1,) * (2 - len(shape)) + tuple(shape)
    size = jnp.dtype(dtype).itemsize
    lanes = (shape[-1] + 127) // 128 * 128
    rows = (shape[-2] + 15) // 16 * 16
    return math.prod(shape[:-2]) * rows * lanes * size


def call(kernel, ins, outs, scratch=(), margin=8, name=None, aliases=None, after=()):
    n_in, n_out, n_after = len(ins), len(outs), len(after)
    spaces = {"s": pltpu.SMEM, "v": pltpu.VMEM, "p": pltpu.VMEM, "a": pl.ANY}
    far_in = [i for i, (kind, _) in enumerate(ins) if kind not in spaces]
    far_out = [i for i, (kind, _) in enumerate(outs) if kind not in spaces]
    n_far = len(far_in) + len(far_out)
    far = [ins[i] for i in far_in] + [outs[i] for i in far_out]
    buffers = [pltpu.VMEM(a.shape, a.dtype) for _, a in far]
    counts = [a.shape[0] if kind == "b" else 1 for kind, a in far]

    def wrapped(*refs):
        refs = (*refs[:n_in], *refs[n_in + n_after :])
        given, results, rest = list(refs[:n_in]), list(refs[n_in : n_in + n_out]), refs[n_in + n_out :]
        arriving, leaving, started = {}, {}, []

        def copies(kind, n, source, target):
            semaphores = rest[n_far]
            first = sum(counts[:n])
            if kind != "b":
                return {0: pltpu.make_async_copy(source, target, semaphores.at[first])}
            return {
                m: pltpu.make_async_copy(source.at[m], target.at[m], semaphores.at[first + m])
                for m in range(counts[n])
            }

        for n, i in enumerate(far_in):
            arriving[i] = copies(ins[i][0], n, given[i], rest[n])
            for copy in arriving[i].values():
                copy.start()
            given[i] = rest[n]
        for n, i in enumerate(far_out, len(far_in)):
            leaving[i] = copies(outs[i][0], n, rest[n], results[i])
            results[i] = rest[n]

        def need(i, m=0):
            arriving[i].pop(m).wait()

        def done(i, m=0):
            copy = leaving[i].pop(m)
            copy.start()
            started.append(copy)

        for i in far_in:
            if ins[i][0] == "h":
                need(i)
        own = rest[n_far + 1 :] if n_far else rest
        kernel(need, done, *given, *results, *own)
        for i in far_in:
            for m in list(arriving[i]):
                need(i, m)
        for i in far_out:
            for m in list(leaving[i]):
                done(i, m)
        for copy in started:
            copy.wait()

    held = [(a.shape, a.dtype) for kind, a in ins if kind not in "spa"]
    held += [(a.shape, a.dtype) for kind, a in outs if kind != "p"]
    held += [(a.shape, a.dtype) for a in scratch if jnp.issubdtype(a.dtype, jnp.number)]
    limit = sum(room(*a) for a in held) + (margin << 20)

    def placed(kind, a):
        if kind in "svam":
            return a
        return pltpu.with_memory_space_constraint(a, spaces.get(kind, pltpu.HBM))

    def shape_of(kind, a):
        if kind == "v":
            return a
        return spaces.get(kind, pltpu.HBM)(a.shape, a.dtype)

    return pl.pallas_call(
        wrapped,
        out_shape=tuple(shape_of(*o) for o in outs),
        in_specs=[
            pl.BlockSpec(memory_space=pl.ANY if kind == "m" else spaces.get(kind, pltpu.HBM))
            for kind, _ in ins
        ]
        + [pl.BlockSpec(memory_space=pl.ANY)] * n_after,
        out_specs=tuple(pl.BlockSpec(memory_space=spaces.get(kind, pltpu.HBM)) for kind, _ in outs),
        scratch_shapes=[
            *buffers,
            *([pltpu.SemaphoreType.DMA((sum(counts),))] if n_far else []),
            *scratch,
        ],
        input_output_aliases=aliases or {},
        compiler_params=pltpu.CompilerParams(vmem_limit_bytes=limit),
        cost_estimate=pl.CostEstimate(flops=0, transcendentals=0, bytes_accessed=0),
        name=name,
    )(*[placed(*a) for a in ins], *after)


def solution(mesh):
    n_head = mesh.shape["head"]
    n_seq = mesh.shape["seq"]

    def swap(value, axis, bit):
        size = n_head if axis == "head" else n_seq
        return lax.ppermute(value, axis, [(i, i ^ bit) for i in range(size)])

    rising = []
    bit = 1
    while bit < n_seq:
        rising.append(bit)
        bit *= 2
    seq_bits = rising[:1] + rising[:0:-1]

    offsets = [0]
    for bit in seq_bits:
        offsets = offsets + [o ^ bit for o in offsets]

    def body(
        layer_input,
        document_start,
        ln1_gain,
        w_qkv,
        sub_gain_attn,
        w_out,
        ln2_gain,
        w_in,
        sub_gain_ffn,
        w_ffo,
        dy,
    ):
        tokens, width = dy.shape
        quarter = layer_input.shape[1]
        cols = w_qkv.shape[2]
        heads = cols // HEAD_SIZE
        rows_dil = tokens // DILATION_RATE
        ff_part = w_in.shape[1]
        n_blocks = tokens // BLOCK
        n_far = n_seq
        h = lax.axis_index("head")
        s = lax.axis_index("seq")
        h_ref = jnp.reshape(h, (1,)).astype(jnp.int32)
        s_ref = jnp.reshape(s, (1,)).astype(jnp.int32)
        far_index = (s ^ jnp.array(offsets, jnp.int32)).astype(jnp.int32)
        place = jnp.concatenate([jnp.stack([h, s]).astype(jnp.int32), far_index])
        shaped = jax.ShapeDtypeStruct

        parts = [[] for _ in range(SPLIT)]
        for i in reversed(range(n_blocks)):
            min(parts, key=lambda part: sum(k + 1 for k in part)).append(i)
        parts = [sorted(part) for part in parts if part]
        home = {i: (p, n) for p, part in enumerate(parts) for n, i in enumerate(part)}

        def stacked(value, got, kind):
            size = value.shape[0]

            def stack_kernel(need, done, v_r, g_r, o_r, semaphores):
                copies = [
                    pltpu.make_async_copy(v_r, o_r.at[:size], semaphores.at[0]),
                    pltpu.make_async_copy(g_r, o_r.at[size:], semaphores.at[1]),
                ]
                for copy in copies:
                    copy.start()
                for copy in copies:
                    copy.wait()

            return call(
                stack_kernel,
                [("a", value), ("a", got)],
                [(kind, shaped((2 * size, *value.shape[1:]), value.dtype))],
                scratch=[pltpu.SemaphoreType.DMA((2,))],
                name="stack",
            )[0]

        def gather_seq(value, works, kind):
            value = value[None]
            results = []
            tokens = ()
            for n in range(max(len(seq_bits), len(works))):
                got = swap(value, "seq", seq_bits[n]) if n < len(seq_bits) else None
                if n < len(works):
                    result, token = works[n](value, *tokens)
                    results.append(result)
                    tokens = (token,)
                    if got is not None:
                        got, *tokens = lax.optimization_barrier((got, token))
                if got is not None:
                    value = stacked(value, got, kind if n == len(seq_bits) - 1 else "v")
            return value, results, tokens

        x_in = layer_input[0]

        def normed(value):
            mu = jnp.mean(value, axis=-1, keepdims=True)
            centred = value - mu
            rs = lax.rsqrt(jnp.mean(centred * centred, axis=-1, keepdims=True) + EPSILON)
            return centred * rs, rs

        def norm_kernel(need, done, x_r, g_r, o):
            o[...] = (normed(x_r[...].astype(F32))[0] * g_r[...]).astype(BF)

        g1_row = ln1_gain.reshape(1, -1)
        (xn,) = call(
            norm_kernel,
            [("h", x_in), ("v", g1_row)],
            [("h", shaped((quarter, width), BF))],
            margin=8,
            name="first_norm",
        )
        xn_core = swap(xn, "head", 1)
        xn_x = swap(xn, "head", 2)

        gain_part = fence(jnp.concatenate([sub_gain_attn, sub_gain_ffn]).reshape(1, -1), xn)
        gain_pair = jnp.concatenate([gain_part, swap(gain_part, "head", 1)], 0)
        gain_rel = jnp.concatenate([gain_pair, swap(gain_pair, "head", 2)], 0)
        gain_attn = gain_rel[:, :cols].reshape(1, width)
        g2_row = ln2_gain.reshape(1, -1)
        gain_ffn = gain_rel[:, cols:]
        w_own = jnp.concatenate([w_out, w_in, w_ffo], 0)
        w_core = swap(w_own, "head", 1)
        dy_own = lax.dynamic_slice_in_dim(dy, h * quarter, quarter, 0)

        seg_begin = s * tokens
        doc = jnp.clip((document_start - seg_begin) // DOC_MIN + 1, 0, tokens // DOC_MIN)
        lane = jnp.arange(LANES, dtype=jnp.int32)[None, :]
        same = lane - cols == doc[:, None]
        feature_lane = lane >= cols
        k_feat = jnp.where(same, 1.0, 0.0).astype(BF)
        q_feat = jnp.where(feature_lane & ~same, APART, 0.0).astype(BF)
        shift = (h * heads + jnp.arange(heads, dtype=jnp.int32)) % DILATION_RATE
        start_grid = document_start.reshape(rows_dil, DILATION_RATE)
        pick = jnp.arange(DILATION_RATE, dtype=jnp.int32)[:, None] == shift[None, :]
        start_dil = jnp.sum(jnp.where(pick[None], start_grid[:, :, None], 0), axis=1).T
        start_row = start_dil.reshape(1, heads * rows_dil)

        w_pad = jnp.pad(w_qkv, ((0, 0), (0, 0), (0, LANES - cols)))
        w_turn = w_qkv.transpose(0, 2, 1).reshape(3 * cols, width)
        w_rows = w_own.shape[0]
        piece = w_rows // (2 * PIECES)
        my_half = (s % 2) * (w_rows // 2)
        w_cut = [
            lax.dynamic_slice_in_dim(w_own, my_half + n * piece, piece, 0) for n in range(PIECES)
        ]
        xn_x = fence(
            xn_x, w_pad, w_turn, q_feat, k_feat, *w_cut, dy_own, start_row, gain_attn, gain_ffn, g2_row
        )
        xn_diag = swap(xn_x, "head", 1)
        w_half = [swap(w, "head", 2) for w in lax.optimization_barrier((*w_cut, xn_x))[:PIECES]]

        def head_shift(h_value, l):
            return lax.rem(h_value * heads + l, DILATION_RATE)

        def spread(h_value, l):
            a = iota((rows_dil, tokens), 0)
            p = iota((rows_dil, tokens), 1)
            return jnp.where(p == a * DILATION_RATE + head_shift(h_value, l), 1.0, 0.0).astype(BF)

        def of_head(l):
            return slice(l * HEAD_SIZE, (l + 1) * HEAD_SIZE)

        def project_kernel(
            need, done, h_s, b0, b1, b2, b3, w_r, qf, kf,
            q_o, k_o, v_o, kt_o, vt_o, x_o, dil_kv, dil_q, qt_s,
        ):
            hv = h_s[0]
            for i in (5, 6, 7):
                need(i)
            for r, b in enumerate((b0, b1, b2, b3)):
                base = pl.multiple_of((hv ^ r) * quarter, quarter)
                span = pl.ds(base, quarter)
                need(1 + r)
                xb = b[...]
                x_o[span, :] = xb
                qv = dot(xb, w_r[0]).astype(BF) * BF(HEAD_SIZE**-0.5)
                q_o[span, :] = qv + qf[span, :]
                kv = dot(xb, w_r[1]).astype(BF)
                k_o[span, :] = kv + kf[span, :]
                vv = dot(xb, w_r[2]).astype(BF)
                v_o[span, :] = vv
                qt_s[:, span] = turned(qv)[:cols].astype(BF)
                kt_o[:, span] = turned(kv)[:cols].astype(BF)
                vt_o[:, span] = turned(vv)[:cols].astype(BF)
            done(5)
            for l in range(heads):
                sel = spread(hv, l)
                dil_q[of_head(l), :] = dot_nt(qt_s[of_head(l), :], sel).astype(BF)
                dil_kv[of_head(l), :] = dot_nt(kt_o[of_head(l), :], sel).astype(BF)
                dil_kv[cols + l * HEAD_SIZE : cols + (l + 1) * HEAD_SIZE, :] = dot_nt(
                    vt_o[of_head(l), :], sel
                ).astype(BF)

        q_a, k_a, v_a, k_t, v_t, x_all, dil_kv, dil_q = call(
            project_kernel,
            [
                ("s", h_ref),
                ("m", xn),
                ("m", xn_core),
                ("m", xn_x),
                ("m", xn_diag),
                ("m", w_pad),
                ("m", q_feat),
                ("m", k_feat),
            ],
            [
                ("p", shaped((tokens, LANES), BF)),
                ("p", shaped((tokens, LANES), BF)),
                ("p", shaped((tokens, LANES), BF)),
                ("p", shaped((cols, tokens), BF)),
                ("v", shaped((cols, tokens), BF)),
                ("h", shaped((tokens, width), BF)),
                ("v", shaped((2 * cols, rows_dil), BF)),
                ("v", shaped((cols, rows_dil), BF)),
            ],
            scratch=[pltpu.VMEM((cols, tokens), BF)],
            name="project",
        )

        def stack_heads(value, size=heads):
            keep = iota(value.shape, 1) // HEAD_SIZE
            zero = jnp.zeros_like(value)
            return jnp.concatenate(
                [jnp.where((keep == l) | (keep >= size), value, zero) for l in range(size)], 0
            )

        wide = heads * BLOCK

        def causal_block():
            return iota((BLOCK, wide), 0) <= iota((BLOCK, wide), 1) % BLOCK

        def near_kernel(part, need, done, q_r, k_r, vt_r, o_o, lse_o):
            for n, i in enumerate(part):
                q_i = stack_heads(q_r[i * BLOCK : (i + 1) * BLOCK, :])
                top = total = None
                outs = None
                for j in [i] + list(range(i)):
                    sc = dot_nt(k_r[j * BLOCK : (j + 1) * BLOCK, :], q_i)
                    if j == i:
                        sc = jnp.where(causal_block(), sc, NEGATIVE)
                    part_top = jnp.max(sc, axis=0, keepdims=True)
                    new_top = part_top if top is None else jnp.maximum(top, part_top)
                    pr = jnp.exp(sc - new_top)
                    part_sum = jnp.sum(pr, axis=0, keepdims=True)
                    pb = pr.astype(BF)
                    fresh = [
                        dot(
                            vt_r[of_head(l), j * BLOCK : (j + 1) * BLOCK],
                            pb[:, l * BLOCK : (l + 1) * BLOCK],
                        )
                        for l in range(heads)
                    ]
                    if top is None:
                        total, outs = part_sum, fresh
                    else:
                        shrink = jnp.exp(top - new_top)
                        total = total * shrink + part_sum
                        outs = [
                            o * shrink[:, l * BLOCK : (l + 1) * BLOCK] + f
                            for l, (o, f) in enumerate(zip(outs, fresh))
                        ]
                    top = new_top
                lse = top + jnp.log(total)
                inv = 1.0 / total
                for l in range(heads):
                    cut = slice(l * BLOCK, (l + 1) * BLOCK)
                    o_o[of_head(l), n * BLOCK : (n + 1) * BLOCK] = outs[l] * inv[:, cut]
                    lse_o[l : l + 1, n * BLOCK : (n + 1) * BLOCK] = lse[:, cut]

        near_lse = []

        def near_work(part):
            def work(*after):
                size = len(part) * BLOCK
                after = [*after, *w_half[len(near_lse) - 1 : len(near_lse)]]
                result = call(
                    lambda *refs: near_kernel(part, *refs),
                    [("p", q_a), ("p", k_a), ("v", v_t)],
                    [("v", shaped((cols, size), F32)), ("v", shaped((heads, size), F32))],
                    name="near_forward",
                    margin=24,
                    after=after,
                )
                near_lse.append(result[1])
                return result, result[1]

            return work

        far_kv, near_out, _ = gather_seq(dil_kv, [near_work(part) for part in parts], "h")
        w_other = [swap(w, "seq", 1) for w in w_half]
        near_o = [o for o, _ in near_out]
        n_parts = len(parts)

        def joined(refs, rows):
            pieces = []
            for i in range(n_blocks):
                p, n = home[i]
                pieces.append(refs[p][rows, n * BLOCK : (n + 1) * BLOCK])
            return jnp.concatenate(pieces, 1)

        def stack_dil(value):
            keep = iota(value.shape, 1) // HEAD_SIZE
            zero = jnp.zeros_like(value)
            return jnp.concatenate([jnp.where(keep == l, value, zero) for l in range(heads)], 0)

        far_wide = heads * rows_dil

        def far_place(p_s, key_owner, query_owner):
            col = iota((rows_dil, far_wide), 1)
            off = lax.rem(p_s[0] * heads + col // rows_dil, DILATION_RATE)
            key = key_owner * tokens + iota((rows_dil, far_wide), 0) * DILATION_RATE + off
            query = query_owner * tokens + (col % rows_dil) * DILATION_RATE + off
            return key, query

        def far_kernel(need, done, *refs):
            p_s, q_r, kv_r, start_r = refs[:4]
            o_r = refs[4 : 4 + n_parts]
            lse_r = refs[4 + n_parts : 4 + 2 * n_parts]
            ao_o, l_o, ldil_o, sum_o, *aob, top_s, total_s, out_s, low_s = refs[4 + 2 * n_parts :]
            hv = p_s[0]
            sv = p_s[1]
            q_v = stack_dil(turned(q_r[...]).astype(BF))
            start_v = start_r[...]
            top_s[...] = jnp.full((8, far_wide), NEGATIVE, F32)
            total_s[...] = jnp.zeros((8, far_wide), F32)
            out_s[...] = jnp.zeros((HEAD_SIZE, far_wide), F32)

            @pl.loop(0, n_far)
            def _(b):
                owner = p_s[2 + b]

                @pl.when(owner <= sv)
                def _():
                    top = top_s[:1]
                    sc = dot_nt(turned(kv_r[b, :cols]).astype(BF), q_v)
                    key, query = far_place(p_s, owner, sv)
                    sc = jnp.where((key <= query) & (key >= start_v), sc, NEGATIVE)
                    new_top = jnp.maximum(top, jnp.max(sc, axis=0, keepdims=True))
                    pr = jnp.exp(sc - new_top)
                    shrink = jnp.exp(top - new_top)
                    total_s[:1] = total_s[:1] * shrink + jnp.sum(pr, axis=0, keepdims=True)
                    pb = pr.astype(BF)
                    fresh = jnp.concatenate(
                        [
                            dot(
                                kv_r[b, cols + l * HEAD_SIZE : cols + (l + 1) * HEAD_SIZE],
                                pb[:, l * rows_dil : (l + 1) * rows_dil],
                            )
                            for l in range(heads)
                        ],
                        1,
                    )
                    out_s[...] = out_s[...] * shrink + fresh
                    top_s[:1] = new_top

            sum_o[...] = jnp.zeros((8, 128), F32)
            total = total_s[:1]
            lse_far = top_s[:1] + jnp.log(total)
            out = out_s[...] / total
            for l in range(heads):
                cut = slice(l * rows_dil, (l + 1) * rows_dil)
                rows = of_head(l)
                lf = lse_far[:, cut]
                sum_o[1:2, :] += lf
                put = spread(hv, l)
                l8 = jnp.broadcast_to(lf, (8, rows_dil))
                full_lf = sum(dot(t, put) for t in thirds(l8))[:1]
                high, low = halves(out[:, cut])
                full_o = dot(high, put) + dot(low, put)
                dilated = iota((1, tokens), 1) % DILATION_RATE == head_shift(hv, l)
                ln = joined(lse_r, slice(l, l + 1))
                for part in range(tokens // 128):
                    sum_o[:1, :] += ln[:, part * 128 : (part + 1) * 128]
                peak = jnp.maximum(ln, full_lf)
                both = peak + jnp.log(jnp.exp(ln - peak) + jnp.exp(full_lf - peak))
                tot = jnp.where(dilated, both, ln)
                w_near = jnp.exp(ln - tot)
                w_far = jnp.where(dilated, jnp.exp(full_lf - tot), 0.0)
                ao = joined(o_r, rows) * w_near + full_o * w_far
                ao_o[rows, :] = ao
                low_s[rows, :] = ao.astype(BF)
                l_o[l : l + 1, :] = tot
                t8 = jnp.broadcast_to(tot, (8, tokens))
                ldil_o[l : l + 1, :] = sum(dot_nt(t, put) for t in thirds(t8))[:1]
            for r, o in enumerate(aob):
                base = pl.multiple_of((hv ^ r) * quarter, quarter)
                o[...] = low_s[:, pl.ds(base, quarter)]

        ao_t, l_all, l_dil, lse_sums, *ao_low = call(
            far_kernel,
            [
                ("s", place),
                ("v", dil_q),
                ("h", far_kv),
                ("v", start_row),
                *[("v", o) for o in near_o],
                *[("v", lse) for lse in near_lse],
            ],
            [
                ("h", shaped((cols, tokens), F32)),
                ("h", shaped((heads, tokens), F32)),
                ("h", shaped((heads, rows_dil), F32)),
                ("h", shaped((8, 128), F32)),
                ("h", shaped((cols, quarter), BF)),
                *[("v", shaped((cols, quarter), BF))] * (n_head - 1),
            ],
            scratch=[
                pltpu.VMEM((8, far_wide), F32),
                pltpu.VMEM((8, far_wide), F32),
                pltpu.VMEM((HEAD_SIZE, far_wide), F32),
                pltpu.VMEM((cols, tokens), BF),
            ],
            name="far_forward",
            after=w_other[:1],
        )

        def exchange(pieces):
            return [pieces[0]] + [swap(pieces[r], "head", r) for r in range(1, n_head)]

        ao_rows = exchange(ao_low)
        *w_side, _ = lax.optimization_barrier((*w_half, *w_other, ao_low[0]))
        w_diag = [swap(w, "head", 1) for w in w_side]

        full_ff = ff_part * n_head
        chunk = min(CHUNK, quarter)
        order = (1, 3, 0, 2)
        slot = {r: n for n, r in enumerate(order)}

        def row_kernel(
            need, done, s_r, x_r, a0, a1, a2, a3, w0, w1, dy_r, ga_r, gf_r, g2_r, *refs
        ):
            side, refs = refs[: 4 * PIECES], refs[4 * PIECES :]
            (
            y_o, an_o, dhb_o, hn_o, gn_o, du_o, dao0, dao1, dao2, dao3, dh_o, va_o, vf_o, v2_o,
            gu_s, slope_s, dgn_s, w_out_s, hid_s, w2, w3, semaphores,
            ) = refs
            ws = (w0, w1, w2, w3)
            copies = []
            for n, ref in enumerate(side):
                half = (s_r[0] + n // PIECES) % 2
                at = pl.multiple_of(half * (w_rows // 2) + n % PIECES * piece, 8)
                copy = pltpu.make_async_copy(
                    ref, ws[2 + n // (2 * PIECES)].at[pl.ds(at, piece)], semaphores.at[n]
                )
                copy.start()
                copies.append(copy)
            for i in range(2, 6):
                need(i)
            ao = jnp.concatenate([a[...].astype(F32) for a in (a0, a1, a2, a3)], 0)
            mu_a = jnp.mean(ao, axis=0, keepdims=True)
            power = jnp.mean(ao * ao, axis=0, keepdims=True)
            rs_a = lax.rsqrt(power - mu_a * mu_a + EPSILON)
            ahat = (ao - mu_a) * rs_a
            ga = jnp.broadcast_to(ga_r[...], (128, width)).T[:, :1]
            an_t = (ahat * ga).astype(BF)
            an_o[...] = an_t
            for r, w in enumerate(ws):
                if r < 2:
                    need(6 + r)
                elif r == 2:
                    for copy in copies:
                        copy.wait()
                w_out_s[r * cols : (r + 1) * cols, :] = w[:cols, :]
            hid_s[...] = x_r[...].astype(F32) + dot(turned(an_t).astype(BF), w_out_s[...])
            g2 = g2_r[...]
            vf_o[...] = jnp.zeros((n_head, ff_part), F32)
            v2_o[...] = jnp.zeros((1, width), F32)
            for c in range(quarter // chunk):
                span = slice(c * chunk, (c + 1) * chunk)
                hid = hid_s[span, :]
                mu2 = jnp.mean(hid, axis=-1, keepdims=True)
                centred = hid - mu2
                rs2 = lax.rsqrt(jnp.mean(centred * centred, axis=-1, keepdims=True) + EPSILON)
                xhat2 = centred * rs2
                hn = (xhat2 * g2).astype(BF)
                hn_o[span, :] = hn
                if c == 0:
                    need(8)
                dy_c = dy_r[span, :]
                sums = [jnp.zeros((chunk, 1), F32)] * 4
                for r, w in enumerate(ws):
                    u = dot(hn, w[cols : cols + width, :])
                    bell = jnp.exp(u * u * -0.5)
                    t = 1.0 / (1.0 + jnp.abs(u) * (ERF_P / math.sqrt(2.0)))
                    poly = ERF_C[4]
                    for coefficient in ERF_C[3::-1]:
                        poly = poly * t + coefficient
                    tail = poly * t * bell * 0.5
                    phi = jnp.where(u >= 0.0, 1.0 - tail, tail)
                    gu = u * phi
                    dgn = dot_nt(dy_c, w[cols + width :, :])
                    c_g = dgn * gf_r[r : r + 1, :]
                    gu_s[r] = gu
                    slope_s[r] = phi + u * bell * GAUSS_NORM
                    dgn_s[r] = dgn
                    terms = (gu, gu * gu, c_g, c_g * gu)
                    sums = [a + jnp.sum(b, axis=-1, keepdims=True) for a, b in zip(sums, terms)]
                mu_g = sums[0] / full_ff
                rs_g = lax.rsqrt(sums[1] / full_ff - mu_g * mu_g + EPSILON)
                m1 = sums[2] / full_ff
                m2 = (sums[3] - mu_g * sums[2]) * rs_g / full_ff
                y = hid
                dhn = jnp.zeros((chunk, width), F32)
                for r, w in enumerate(ws):
                    gf = gf_r[r : r + 1, :]
                    ghat = (gu_s[r] - mu_g) * rs_g
                    dgn = dgn_s[r]
                    gn = (ghat * gf).astype(BF)
                    du = (rs_g * (dgn * gf - m1 - ghat * m2) * slope_s[r]).astype(BF)
                    gn_o[slot[r], span, :] = gn
                    du_o[slot[r], span, :] = du
                    vf_o[r : r + 1, :] += jnp.sum(dgn * ghat, axis=0, keepdims=True)
                    y = y + dot(gn, w[cols + width :, :])
                    dhn = dhn + dot_nt(du, w[cols : cols + width, :])
                y_o[span, :] = y.astype(BF)
                v2_o[...] += jnp.sum(dhn * xhat2, axis=0, keepdims=True)
                c2 = dhn * g2
                dh = dy_c.astype(F32) + rs2 * (
                    c2
                    - jnp.mean(c2, axis=-1, keepdims=True)
                    - xhat2 * jnp.mean(c2 * xhat2, axis=-1, keepdims=True)
                )
                dh_o[span, :] = dh
                dhb_o[span, :] = dh.astype(BF)
            for k in (0, 1, 2, 3, 4, 5, 10):
                done(k)
            dan = dot_nt(w_out_s[...], dhb_o[...])
            column = jnp.sum(dan * ahat, axis=-1, keepdims=True)
            va_o[...] = jnp.broadcast_to(column, (width, 128)).T[:1]
            c_a = dan * ga
            dao = rs_a * (
                c_a
                - jnp.mean(c_a, axis=0, keepdims=True)
                - ahat * jnp.mean(c_a * ahat, axis=0, keepdims=True)
            )
            for r, o in enumerate((dao0, dao1, dao2, dao3)):
                o[...] = dao[r * cols : (r + 1) * cols].astype(BF)

        y_rows, an_t, dhb, hn2, gn, du, *dao_low, dh, v_attn, v_ffn, v_ln2 = call(
            row_kernel,
            [
                ("s", s_ref),
                ("h", x_in),
                *[("m", a) for a in ao_rows],
                ("l", w_own),
                ("l", w_core),
                ("l", dy_own),
                ("v", gain_attn),
                ("v", gain_ffn),
                ("v", g2_row),
                *[("a", w) for w in (*w_side, *w_diag)],
            ],
            [
                ("h", shaped((quarter, width), BF)),
                ("h", shaped((width, quarter), BF)),
                ("h", shaped((quarter, width), BF)),
                ("h", shaped((quarter, width), BF)),
                ("h", shaped((n_head, quarter, ff_part), BF)),
                ("h", shaped((n_head, quarter, ff_part), BF)),
                *[("v", shaped((cols, quarter), BF))] * n_head,
                ("h", shaped((quarter, width), F32)),
                ("v", shaped((1, width), F32)),
                ("v", shaped((n_head, ff_part), F32)),
                ("v", shaped((1, width), F32)),
            ],
            scratch=[
                pltpu.VMEM((n_head, chunk, ff_part), F32),
                pltpu.VMEM((n_head, chunk, ff_part), F32),
                pltpu.VMEM((n_head, chunk, ff_part), F32),
                pltpu.VMEM((width, width), BF),
                pltpu.VMEM((quarter, width), F32),
                pltpu.VMEM((w_rows, width), BF),
                pltpu.VMEM((w_rows, width), BF),
                pltpu.SemaphoreType.DMA((4 * PIECES,)),
            ],
            margin=14,
            name="rows",
        )
        output = y_rows[None]
        dao_blocks = exchange(dao_low)


        def weights_kernel(
            need, done, gn_r, dy_r, hn_r, du_r, an_r, dhb_r, send_o, own_o, side_o, send_i, keep_i
        ):
            need(1)
            for n, o in enumerate((send_o.at[0], send_o.at[1], own_o, side_o)):
                need(0, n)
                o[...] = dot_tn(gn_r[n], dy_r[...]).astype(BF)
                done(*((0, n) if n < 2 else (n - 1, 0)))
            for i in (2, 4, 5):
                need(i)
            for n, r in enumerate(order):
                need(3, n)
                o = send_i if n < 2 else keep_i
                o[n % 2, :width] = dot_tn(hn_r[...], du_r[n]).astype(BF)
                rows = an_r[r * cols : (r + 1) * cols, :]
                o[n % 2, width:] = dot(rows, dhb_r[...]).astype(BF)
                done(3 + n // 2, n % 2)

        one = ("h", shaped((ff_part, width), BF))
        two = ("b", shaped((2, width + cols, width), BF))
        ffo_send, ffo_own, ffo_side, in_send, in_keep = call(
            weights_kernel,
            [("b", gn), ("l", dy_own), ("l", hn2), ("b", du), ("l", an_t), ("l", dhb)],
            [("b", shaped((2, ff_part, width), BF)), one, one, two, two],
            name="weight_gradients",
        )

        def plus(*terms):
            return sum(t.astype(F32) for t in terms).astype(BF)

        class Half:
            def __init__(self, terms, bit):
                self.terms = [t if isinstance(t, tuple) else (t, None) for t in terms]
                self.bit = bit
                self.size = self.terms[0][0].shape[-2] // 2

            def shapes(self):
                return [("v", shaped((self.size, width), BF))] * 2

            def buffers(self):
                return 2 * len(self.terms)

            def start(self, index, ins, outs, bufs, begin):
                upper = (index // self.bit) % 2
                for n, (_, lead) in enumerate(self.terms):
                    ref = ins[n] if lead is None else ins[n].at[lead]
                    for m, at in enumerate(((1 - upper) * self.size, upper * self.size)):
                        begin(ref.at[pl.ds(pl.multiple_of(at, 8), self.size)], bufs[2 * n + m])

            def plain(self):
                found = []
                upper = (s // self.bit) % 2
                for at in ((1 - upper) * self.size, upper * self.size):
                    parts = [t if lead is None else t[lead] for t, lead in self.terms]
                    parts = [lax.dynamic_slice_in_dim(t, at, self.size, 0) for t in parts]
                    found.append(plus(*parts))
                return found

            def finish(self, outs, bufs):
                for m in range(2):
                    parts = [bufs[2 * n + m][...].astype(F32) for n in range(len(self.terms))]
                    outs[m][...] = sum(parts[1:], parts[0]).astype(BF)

        class Joined:
            def __init__(self, own, got, bit):
                self.terms = [(own, None), (got, None)]
                self.bit = bit
                self.size = own.shape[0]

            def shapes(self):
                return [("v", shaped((2 * self.size, width), BF))]

            def buffers(self):
                return 0

            def start(self, index, ins, outs, bufs, begin):
                upper = (index // self.bit) % 2
                for ref, at in zip(ins, (upper * self.size, (1 - upper) * self.size)):
                    begin(ref, outs[0].at[pl.ds(pl.multiple_of(at, 8), self.size)])

            def plain(self):
                own, got = [t for t, _ in self.terms]
                upper = (s // self.bit) % 2 == 1
                return [
                    jnp.where(upper, jnp.concatenate([got, own], 0), jnp.concatenate([own, got], 0))
                ]

            def finish(self, outs, bufs):
                pass

        def combine(jobs):
            made = combine_tiles([job for job in jobs if job.size % 8 == 0])
            return [made.pop(0) if job.size % 8 == 0 else job.plain() for job in jobs]

        def combine_tiles(jobs):
            if not jobs:
                return []
            n_in = [len(job.terms) for job in jobs]
            n_out = [len(job.shapes()) for job in jobs]
            n_buf = [job.buffers() for job in jobs]
            total = sum(max(job.buffers(), len(job.terms)) for job in jobs)

            def kernel(need, done, s_r, *refs):
                index = s_r[0]
                ins = refs[: sum(n_in)]
                outs = refs[sum(n_in) : sum(n_in) + sum(n_out)]
                bufs = refs[sum(n_in) + sum(n_out) : -1]
                semaphores = refs[-1]
                found = []

                def begin(source, target):
                    copy = pltpu.make_async_copy(source, target, semaphores.at[len(found)])
                    copy.start()
                    found.append(copy)

                work = []
                a = b = c = 0
                for n, job in enumerate(jobs):
                    mine = (outs[b : b + n_out[n]], bufs[c : c + n_buf[n]])
                    before = len(found)
                    job.start(index, ins[a : a + n_in[n]], *mine, begin)
                    work.append((job, mine, found[before:]))
                    a, b, c = a + n_in[n], b + n_out[n], c + n_buf[n]
                for job, mine, copies in work:
                    for copy in copies:
                        copy.wait()
                    job.finish(*mine)

            results = call(
                kernel,
                [("s", s_ref), *[("a", t) for job in jobs for t, _ in job.terms]],
                [o for job in jobs for o in job.shapes()],
                scratch=[
                    *[
                        pltpu.VMEM((job.size, width), BF)
                        for job in jobs
                        for _ in range(job.buffers())
                    ],
                    pltpu.SemaphoreType.DMA((total,)),
                ],
                name="combine",
            )
            found = []
            at = 0
            for n in n_out:
                found.append(results[at : at + n])
                at += n
            return found

        n_note = 3 * heads
        note_rows = (3 * n_note + 15) // 16 * 16

        def prepare_kernel(
            need, done, h_s, d0, d1, d2, d3, ao_r, q_r, l_r, start_r, do_o, delta_o, sent_o, ddil_o, dt_s
        ):
            hv = h_s[0]
            for r, d in enumerate((d0, d1, d2, d3)):
                need(1 + r)
                base = pl.multiple_of((hv ^ r) * quarter, quarter)
                dt_s[:, pl.ds(base, quarter)] = d[...]
            dao_v = dt_s[...].astype(F32)
            grown = jnp.concatenate([dao_v, jnp.zeros((LANES - cols, tokens), F32)], 0)
            do_o[...] = grown.T.astype(BF)
            prod = dao_v * ao_r[...]
            sent_o[:cols, :] = q_r[...]
            for l in range(heads):
                sel = spread(hv, l)
                at = cols + l * HEAD_SIZE
                sent_o[at : at + HEAD_SIZE, :] = dot_nt(dt_s[of_head(l), :], sel).astype(BF)
                delta = jnp.sum(prod[of_head(l)], axis=0, keepdims=True)
                delta_o[l : l + 1, :] = delta
                d8 = jnp.broadcast_to(delta, (8, tokens))
                ddil_o[l : l + 1, :] = sum(dot_nt(t, sel) for t in thirds(d8))[:1]
            found = [l_r[l : l + 1, :] for l in range(heads)]
            found += [ddil_o[l : l + 1, :] for l in range(heads)]
            found += [start_r[l : l + 1, :].astype(F32) for l in range(heads)]
            row = iota((note_rows, rows_dil), 0)
            notes = jnp.zeros((note_rows, rows_dil), F32)
            for n, value in enumerate(found):
                for t, piece in enumerate(thirds(value)):
                    notes = jnp.where(row == t * n_note + n, piece.astype(F32), notes)
            sent_o[2 * cols :, :] = notes.astype(BF)

        do_a, delta_all, far_note, delta_dil = call(
            prepare_kernel,
            [
                ("s", h_ref),
                ("m", fence(dao_blocks[0], ffo_send, in_send)),
                *[("m", d) for d in dao_blocks[1:]],
                ("h", ao_t),
                ("v", dil_q),
                ("v", l_dil),
                ("v", start_dil),
            ],
            [
                ("p", shaped((tokens, LANES), BF)),
                ("v", shaped((heads, tokens), F32)),
                ("v", shaped((2 * cols + note_rows, rows_dil), BF)),
                ("v", shaped((heads, rows_dil), F32)),
            ],
            scratch=[pltpu.VMEM((cols, tokens), BF)],
            name="prepare_backward",
        )

        def near_back_kernel(part, need, done, q_r, k_r, v_r, kt_r, do_r, l_r, d_r, *rest):
            dq_o, dk_o, dv_o, token_o = rest[-4:]
            fresh = len(rest) == 4
            token_o[...] = jnp.zeros((8, 128), F32)
            for n, i in enumerate(reversed(part)):
                span = slice(i * BLOCK, (i + 1) * BLOCK)
                q_i = stack_heads(q_r[span, :])
                do_i = stack_heads(do_r[span, :])
                lse_i = jnp.concatenate([l_r[l : l + 1, span] for l in range(heads)], 1)
                del_i = jnp.concatenate([d_r[l : l + 1, span] for l in range(heads)], 1)
                dq_i = [None] * heads
                for j in range(i + 1):
                    keys = slice(j * BLOCK, (j + 1) * BLOCK)
                    pr = jnp.exp(dot_nt(k_r[keys, :], q_i) - lse_i)
                    if j == i:
                        pr = jnp.where(causal_block(), pr, 0.0)
                    dp = dot_nt(v_r[keys, :], do_i)
                    ds = (pr * (dp - del_i)).astype(BF)
                    dv = dot(pr.astype(BF), do_i)
                    dk = dot(ds, q_i)
                    if fresh and n == 0:
                        dv_o[keys, :] = dv
                        dk_o[keys, :] = dk
                    else:
                        dv_o[keys, :] += dv
                        dk_o[keys, :] += dk
                    for l in range(heads):
                        add = dot(kt_r[of_head(l), keys], ds[:, l * BLOCK : (l + 1) * BLOCK])
                        dq_i[l] = add if dq_i[l] is None else dq_i[l] + add
                for l in range(heads):
                    dq_o[of_head(l), span] = dq_i[l]

        grown_to = []

        def back_work(part):
            def work(value, *after):
                after = [value, *after]
                if part is parts[min(1, n_parts - 1)]:
                    after += start_sums(value)
                held = [("p", a) for a in grown_to]
                *grown_to[:], token = call(
                    lambda *refs: near_back_kernel(part, *refs),
                    [
                        ("p", q_a),
                        ("p", k_a),
                        ("p", v_a),
                        ("p", k_t),
                        ("p", do_a),
                        ("v", l_all),
                        ("v", delta_all),
                        *held,
                    ],
                    [
                        ("p", shaped((cols, tokens), F32)),
                        ("p", shaped((tokens, LANES), F32)),
                        ("p", shaped((tokens, LANES), F32)),
                        ("v", shaped((8, 128), F32)),
                    ],
                    name="near_backward",
                    margin=20,
                    aliases={7 + n: n for n in range(len(held))},
                    after=after,
                )
                return None, token

            return work

        ffo_send, in_send, _ = lax.optimization_barrier((ffo_send, in_send, far_note))
        ffo_core = swap(ffo_send, "head", 1)
        in_core = swap(in_send, "head", 1)
        flying = {}

        def start_sums(value):
            nonlocal ffo_core, in_core
            ffo_core, in_core = lax.optimization_barrier((ffo_core, in_core, value))[:2]
            flying["ffo_x"] = plus(ffo_side, ffo_core[1])
            upper = (s & rising[0]) != 0
            size = (width + cols) // 2
            away = jnp.where(upper, 0, size)
            flying["in_y"], flying["in_own"] = [
                plus(*[lax.dynamic_slice_in_dim(t, at, size, 1) for t in (in_keep, in_core)])
                for at in (away, size - away)
            ]
            flying["ffo_got"] = swap(flying["ffo_x"], "head", 2)
            flying["in_got"] = swap(flying["in_y"], "seq", rising[0])
            return flying["ffo_x"], flying["in_y"]

        far_q, _, tokens_back = gather_seq(far_note, [back_work(part) for part in parts], "v")
        dq_near, dk_near, dv_near = grown_to
        ffo_got, in_got, *tokens_back = lax.optimization_barrier(
            (flying["ffo_got"], flying["in_got"], *tokens_back)
        )
        (ffo_z, ffo_kept), _ = combine([Half([ffo_own, (ffo_core, 0), ffo_got], rising[1])]) + [None]
        in_x = plus(in_got[1], flying["in_own"][1])
        ffo_z_got = swap(ffo_z, "seq", rising[1])
        in_x_got = swap(in_x, "head", 2)

        def far_back_kernel(need, done, *refs):
            p_s, kv_r, fq_r, start_r, l_r, d_r = refs[:6]
            dqn_r, dkn_r, dvn_r, w_r, x_r, g_r, send_o, keep_o, part_o, v_o, d_o, dq_s, dk_s, dv_s = refs[6:]
            hv = p_s[0]
            sv = p_s[1]

            def rows_of(ref, b, first):
                return turned(ref[b, first : first + cols]).astype(BF)

            q_v = stack_dil(rows_of(fq_r, 0, 0))
            do_v = stack_dil(rows_of(fq_r, 0, cols))
            k_own = rows_of(kv_r, 0, 0)
            v_own = rows_of(kv_r, 0, cols)
            start_v = start_r[...]
            l_v = jnp.concatenate([l_r[l : l + 1, :] for l in range(heads)], 1)
            d_v = jnp.concatenate([d_r[l : l + 1, :] for l in range(heads)], 1)
            dq_s[...] = jnp.zeros_like(dq_s)
            dk_s[...] = jnp.zeros_like(dk_s)
            dv_s[...] = jnp.zeros_like(dv_s)

            @pl.loop(0, n_far)
            def _(b):
                owner = p_s[2 + b]

                @pl.when(owner <= sv)
                def _():
                    key, query = far_place(p_s, owner, sv)
                    keep = (key <= query) & (key >= start_v)
                    sc = dot_nt(rows_of(kv_r, b, 0), q_v)
                    pr = jnp.where(keep, jnp.exp(sc - l_v), 0.0)
                    dp = dot_nt(rows_of(kv_r, b, cols), do_v)
                    ds = (pr * (dp - d_v)).astype(BF)
                    for l in range(heads):
                        cut = slice(l * rows_dil, (l + 1) * rows_dil)
                        dq_s[of_head(l), :] += dot(kv_r[b, of_head(l)], ds[:, cut])

                @pl.when(owner >= sv)
                def _():
                    note = fq_r[b, 2 * cols :].astype(F32)

                    def row(kind):
                        found = []
                        for l in range(heads):
                            at = kind * heads + l
                            found.append(
                                sum(note[at + t * n_note : at + t * n_note + 1] for t in range(3))
                            )
                        return jnp.concatenate(found, 1)

                    key, query = far_place(p_s, sv, owner)
                    keep = (key <= query) & (key >= row(2).astype(jnp.int32))
                    q_b = stack_dil(rows_of(fq_r, b, 0))
                    do_b = stack_dil(rows_of(fq_r, b, cols))
                    sc = dot_nt(k_own, q_b)
                    pr = jnp.where(keep, jnp.exp(sc - row(0)), 0.0)
                    dp = dot_nt(v_own, do_b)
                    ds = (pr * (dp - row(1))).astype(BF)
                    dk_s[...] += dot(ds, q_b)
                    dv_s[...] += dot(pr.astype(BF), do_b)

            dk_t = turned(dk_s[...])
            dv_t = turned(dv_s[...])

            def placed(value, l):
                high, low = halves(value[of_head(l)])
                put = spread(hv, l)
                return dot(high, put) + dot(low, put)

            dk_near = dkn_r[...].T
            dv_near = dvn_r[...].T
            scale = HEAD_SIZE**-0.5
            dq_far = dq_s[...]
            for l in range(heads):
                rows = of_head(l)
                d_o[rows, :] = ((dqn_r[rows, :] + placed(dq_far, l)) * scale).astype(BF)
                at = cols + l * HEAD_SIZE
                d_o[at : at + HEAD_SIZE, :] = (dk_near[rows] + placed(dk_t, l)).astype(BF)
                at += cols
                d_o[at : at + HEAD_SIZE, :] = (dv_near[rows] + placed(dv_t, l)).astype(BF)
            for o, n, r in ((send_o, 0, 3), (send_o, 1, 1), (keep_o, 0, 2), (keep_o, 1, 0)):
                base = pl.multiple_of((hv ^ r) * quarter, quarter)
                o[n] = dot_tn(d_o[:, pl.ds(base, quarter)], w_r[...]).astype(o.dtype)
            need(10)
            part = dot(d_o[...], x_r[...])
            part_o[...] = part.astype(BF)
            v_o[...] = jnp.sum(part * w_r[...].astype(F32), axis=0, keepdims=True) / g_r[...]

        dxn_send, dxn_keep, g_part, v_ln1 = call(
            far_back_kernel,
            [
                ("s", place),
                ("h", far_kv),
                ("v", far_q),
                ("v", start_row),
                ("v", l_dil),
                ("v", delta_dil),
                ("p", dq_near),
                ("p", dk_near),
                ("p", dv_near),
                ("v", w_turn),
                ("l", x_all),
                ("v", g1_row),
            ],
            [
                ("v", shaped((2, quarter, width), BF)),
                ("v", shaped((2, quarter, width), F32)),
                ("v", shaped((3 * cols, width), BF)),
                ("v", shaped((1, width), F32)),
            ],
            scratch=[
                pltpu.VMEM((3 * cols, tokens), BF),
                pltpu.VMEM((cols, rows_dil), F32),
                pltpu.VMEM((rows_dil, cols), F32),
                pltpu.VMEM((rows_dil, cols), F32),
            ],
            margin=12,
            name="far_backward",
            after=(ffo_z, in_x, *tokens_back),
        )

        dxn_send, ffo_z_got, in_x_got = lax.optimization_barrier((dxn_send, ffo_z_got, in_x_got))

        def sum_rows():
            got = yield dxn_send, "head", 1, 1
            side = (dxn_keep[0] + got[0].astype(F32)).astype(BF)
            over_x = yield side, "head", 2, 3

            def last_kernel(need, done, x_r, g_r, keep_r, got_r, over_r, dh_r, o):
                xhat, rs = normed(x_r[...].astype(F32))
                dxn = keep_r[1] + got_r[1].astype(F32) + over_r[...].astype(F32)
                c = dxn * g_r[...]
                first = jnp.mean(c, axis=-1, keepdims=True)
                second = jnp.mean(c * xhat, axis=-1, keepdims=True)
                o[...] = dh_r[...] + rs * (c - first - xhat * second)

            (result,) = call(
                last_kernel,
                [("v", x_in), ("v", g1_row), ("v", dxn_keep), ("v", got), ("v", over_x), ("v", dh)],
                [("v", shaped((quarter, width), F32))],
                margin=12,
                name="first_norm_backward",
            )
            return result

        def sum_seq(terms, scatter, spread, last=1):
            for bit in scatter:
                send, kept = yield Half(terms, bit)
                terms = [kept, (yield send, "seq", bit, 1)]
            value = None
            for bit in spread:
                if value is None:
                    value = plus(*terms)
                rounds = last if bit == spread[-1] else 1
                got = yield value, "seq", bit, rounds
                (value,) = yield Joined(value, got, bit)
            return value

        def sum_ffo():
            bits = rising[2:] + rising[:1]
            terms = [ffo_kept, ffo_z_got]
            value = yield from sum_seq(terms, bits, bits[::-1] + rising[1:2])
            return value.astype(F32)

        def sum_in():
            terms = [(in_got, 0), (flying["in_own"], 0), in_x_got]
            value = yield from sum_seq(terms, rising[1:], rising[::-1])
            return value[:width].astype(F32), value[width:].astype(F32)

        def sum_qkv():
            return (yield from sum_seq([g_part], rising, rising[::-1]))

        def sum_small():
            v_rel = jnp.concatenate([v_attn.reshape(n_head, cols), v_ffn], 1)
            size = v_rel.shape[1]
            common = jnp.concatenate([v_ln1.reshape(-1), v_ln2.reshape(-1), lse_sums[:2].reshape(-1)])
            got = yield jnp.concatenate([v_rel[1], v_rel[3], common]), "head", 1, 1
            mine = v_rel[0] + got[:size]
            other = v_rel[2] + got[size : 2 * size]
            common = common + got[2 * size :]
            got = yield jnp.concatenate([other, common]), "head", 2, 1
            small = jnp.concatenate([mine, common]) + got
            for bit in rising:
                small = small + (yield small, "seq", bit, 1)
            total_heads = heads * n_head
            counts = jnp.array([tokens * n_seq * total_heads, rows_dil * n_seq * total_heads], F32)
            means = jnp.sum(small[size + 2 * width :].reshape(2, 128), axis=1) / counts
            return (
                small[:cols],
                small[cols:size],
                small[size : size + width],
                small[size + width : size + 2 * width],
                means,
            )

        def in_rounds(chains):
            results = [None] * len(chains)
            large = (1, 2, 3)
            asks = {}
            flying = {}
            ended = []

            def resume(n, value):
                try:
                    asks[n] = chains[n].send(value)
                except StopIteration as stop:
                    results[n] = stop.value
                    ended.append(n)

            def settle():
                jobs = [n for n in asks if not isinstance(asks[n], tuple)]
                if jobs:
                    for n, made in zip(jobs, combine([asks.pop(n) for n in jobs])):
                        resume(n, made)

            for n in range(len(chains)):
                resume(n, None)
            number = 0
            while asks or flying:
                settle()
                for n in list(asks):
                    value, axis, bit, rounds = asks.pop(n)
                    flying[n] = (number + rounds - 1, swap(value, axis, bit))
                due = [n for n in flying if flying[n][0] <= number]
                held = tuple(flying.pop(n)[1] for n in due)
                flat, tree = jax.tree.flatten((held, [results[n] for n in ended]))
                held, again = jax.tree.unflatten(tree, lax.optimization_barrier(tuple(flat)))
                for n, value in zip(ended, again):
                    results[n] = value
                for n, got in zip(due, held):
                    if n in large:
                        resume(n, got)
                settle()
                sent = [asks[n][0] for n in large if n in asks]
                for n, got in zip(due, held):
                    if n not in large:
                        resume(n, fence(got, sent[0]) if sent else got)
                number += 1
            return results

        dx, g_ffo, (g_in, g_out), g_qkv, (g_sub_attn, g_sub_ffn, g_ln1, g_ln2, means) = in_rounds(
            [sum_rows(), sum_ffo(), sum_in(), sum_qkv(), sum_small()]
        )
        g_qkv = g_qkv.astype(F32).reshape(3, cols, width).transpose(0, 2, 1)
        return (
            output,
            dx[None],
            g_ln1,
            g_qkv,
            g_sub_attn,
            g_out,
            g_ln2,
            g_in,
            g_sub_ffn,
            g_ffo,
            means,
        )

    return jax.shard_map(
        body,
        mesh=mesh,
        in_specs=(
            P("head", "seq", None),
            P("seq"),
            P(),
            P(None, None, "head"),
            P("head"),
            P("head", None),
            P(),
            P(None, "head"),
            P("head"),
            P("head", None),
            P("seq", None),
        ),
        out_specs=(
            P("head", "seq", None),
            P("head", "seq", None),
            P(),
            P(None, None, "head"),
            P("head"),
            P("head", None),
            P(),
            P(None, "head"),
            P("head"),
            P("head", None),
            P(),
        ),
        check_vma=False,
    )
```

```python
import math

import jax
import jax.numpy as jnp
from jax import lax
from jax.experimental import pallas as pl
from jax.experimental.pallas import tpu as pltpu
from jax.sharding import PartitionSpec as P

HEAD_SIZE = 64
DILATION_RATE = 16
EPSILON = 1e-05
NEGATIVE = -1e30
APART = -(2.0**30)
DOC_MIN = 256
GAUSS_NORM = 1.0 / math.sqrt(2.0 * math.pi)
BLOCK = 256
LANES = 256
BF = jnp.bfloat16
F32 = jnp.float32
ERF_P = 0.3275911
ERF_C = (0.254829592, -0.284496736, 1.421413741, -1.453152027, 1.061405429)
SPLIT = 3
PIECES = 2
CHUNK = 256


def dot(a, b):
    return lax.dot_general(a, b, (((1,), (0,)), ((), ())), preferred_element_type=F32)


def dot_nt(a, b):
    return lax.dot_general(a, b, (((1,), (1,)), ((), ())), preferred_element_type=F32)


def dot_tn(a, b):
    return lax.dot_general(a, b, (((0,), (0,)), ((), ())), preferred_element_type=F32)


def iota(shape, axis):
    return lax.broadcasted_iota(jnp.int32, shape, axis)


def halves(value):
    high = value.astype(BF)
    return high, (value - high.astype(F32)).astype(BF)


def thirds(value):
    high = value.astype(BF)
    rest = value - high.astype(F32)
    middle = rest.astype(BF)
    return high, middle, (rest - middle.astype(F32)).astype(BF)


def fence(value, *before):
    return lax.optimization_barrier((value, *before))[0]


def turned(value):
    return value.astype(F32).T


def room(shape, dtype):
    shape = (1,) * (2 - len(shape)) + tuple(shape)
    size = jnp.dtype(dtype).itemsize
    lanes = (shape[-1] + 127) // 128 * 128
    rows = (shape[-2] + 15) // 16 * 16
    return math.prod(shape[:-2]) * rows * lanes * size


def call(kernel, ins, outs, scratch=(), margin=8, name=None, aliases=None, after=()):
    n_in, n_out, n_after = len(ins), len(outs), len(after)
    spaces = {"s": pltpu.SMEM, "v": pltpu.VMEM, "p": pltpu.VMEM, "a": pl.ANY}
    far_in = [i for i, (kind, _) in enumerate(ins) if kind not in spaces]
    far_out = [i for i, (kind, _) in enumerate(outs) if kind not in spaces]
    n_far = len(far_in) + len(far_out)
    far = [ins[i] for i in far_in] + [outs[i] for i in far_out]
    buffers = [pltpu.VMEM(a.shape, a.dtype) for _, a in far]
    counts = [a.shape[0] if kind == "b" else 1 for kind, a in far]

    def wrapped(*refs):
        refs = (*refs[:n_in], *refs[n_in + n_after :])
        given, results, rest = list(refs[:n_in]), list(refs[n_in : n_in + n_out]), refs[n_in + n_out :]
        arriving, leaving, started = {}, {}, []

        def copies(kind, n, source, target):
            semaphores = rest[n_far]
            first = sum(counts[:n])
            if kind != "b":
                return {0: pltpu.make_async_copy(source, target, semaphores.at[first])}
            return {
                m: pltpu.make_async_copy(source.at[m], target.at[m], semaphores.at[first + m])
                for m in range(counts[n])
            }

        for n, i in enumerate(far_in):
            arriving[i] = copies(ins[i][0], n, given[i], rest[n])
            for copy in arriving[i].values():
                copy.start()
            given[i] = rest[n]
        for n, i in enumerate(far_out, len(far_in)):
            leaving[i] = copies(outs[i][0], n, rest[n], results[i])
            results[i] = rest[n]

        def need(i, m=0):
            arriving[i].pop(m).wait()

        def done(i, m=0):
            copy = leaving[i].pop(m)
            copy.start()
            started.append(copy)

        for i in far_in:
            if ins[i][0] == "h":
                need(i)
        own = rest[n_far + 1 :] if n_far else rest
        kernel(need, done, *given, *results, *own)
        for i in far_in:
            for m in list(arriving[i]):
                need(i, m)
        for i in far_out:
            for m in list(leaving[i]):
                done(i, m)
        for copy in started:
            copy.wait()

    held = [(a.shape, a.dtype) for kind, a in ins if kind not in "spa"]
    held += [(a.shape, a.dtype) for kind, a in outs if kind != "p"]
    held += [(a.shape, a.dtype) for a in scratch if jnp.issubdtype(a.dtype, jnp.number)]
    limit = sum(room(*a) for a in held) + (margin << 20)

    def placed(kind, a):
        if kind in "svam":
            return a
        return pltpu.with_memory_space_constraint(a, spaces.get(kind, pltpu.HBM))

    def shape_of(kind, a):
        if kind == "v":
            return a
        return spaces.get(kind, pltpu.HBM)(a.shape, a.dtype)

    return pl.pallas_call(
        wrapped,
        out_shape=tuple(shape_of(*o) for o in outs),
        in_specs=[
            pl.BlockSpec(memory_space=pl.ANY if kind == "m" else spaces.get(kind, pltpu.HBM))
            for kind, _ in ins
        ]
        + [pl.BlockSpec(memory_space=pl.ANY)] * n_after,
        out_specs=tuple(pl.BlockSpec(memory_space=spaces.get(kind, pltpu.HBM)) for kind, _ in outs),
        scratch_shapes=[
            *buffers,
            *([pltpu.SemaphoreType.DMA((sum(counts),))] if n_far else []),
            *scratch,
        ],
        input_output_aliases=aliases or {},
        compiler_params=pltpu.CompilerParams(vmem_limit_bytes=limit),
        cost_estimate=pl.CostEstimate(flops=0, transcendentals=0, bytes_accessed=0),
        name=name,
    )(*[placed(*a) for a in ins], *after)


def solution(mesh):
    n_head = mesh.shape["head"]
    n_seq = mesh.shape["seq"]

    def swap(value, axis, bit):
        size = n_head if axis == "head" else n_seq
        return lax.ppermute(value, axis, [(i, i ^ bit) for i in range(size)])

    rising = []
    bit = 1
    while bit < n_seq:
        rising.append(bit)
        bit *= 2
    seq_bits = rising[:1] + rising[:0:-1]

    offsets = [0]
    for bit in seq_bits:
        offsets = offsets + [o ^ bit for o in offsets]

    def body(
        layer_input,
        document_start,
        ln1_gain,
        w_qkv,
        sub_gain_attn,
        w_out,
        ln2_gain,
        w_in,
        sub_gain_ffn,
        w_ffo,
        dy,
    ):
        tokens, width = dy.shape
        quarter = layer_input.shape[1]
        cols = w_qkv.shape[2]
        heads = cols // HEAD_SIZE
        rows_dil = tokens // DILATION_RATE
        ff_part = w_in.shape[1]
        n_blocks = tokens // BLOCK
        n_far = n_seq
        h = lax.axis_index("head")
        s = lax.axis_index("seq")
        h_ref = jnp.reshape(h, (1,)).astype(jnp.int32)
        s_ref = jnp.reshape(s, (1,)).astype(jnp.int32)
        far_index = (s ^ jnp.array(offsets, jnp.int32)).astype(jnp.int32)
        place = jnp.concatenate([jnp.stack([h, s]).astype(jnp.int32), far_index])
        shaped = jax.ShapeDtypeStruct

        parts = [[] for _ in range(SPLIT)]
        for i in reversed(range(n_blocks)):
            min(parts, key=lambda part: sum(k + 1 for k in part)).append(i)
        parts = [sorted(part) for part in parts if part]
        home = {i: (p, n) for p, part in enumerate(parts) for n, i in enumerate(part)}

        def stacked(value, got, kind):
            size = value.shape[0]

            def stack_kernel(need, done, v_r, g_r, o_r, semaphores):
                copies = [
                    pltpu.make_async_copy(v_r, o_r.at[:size], semaphores.at[0]),
                    pltpu.make_async_copy(g_r, o_r.at[size:], semaphores.at[1]),
                ]
                for copy in copies:
                    copy.start()
                for copy in copies:
                    copy.wait()

            return call(
                stack_kernel,
                [("a", value), ("a", got)],
                [(kind, shaped((2 * size, *value.shape[1:]), value.dtype))],
                scratch=[pltpu.SemaphoreType.DMA((2,))],
                name="stack",
            )[0]

        def gather_seq(value, works, kind):
            value = value[None]
            results = []
            tokens = ()
            for n in range(max(len(seq_bits), len(works))):
                got = swap(value, "seq", seq_bits[n]) if n < len(seq_bits) else None
                if n < len(works):
                    result, token = works[n](value, *tokens)
                    results.append(result)
                    tokens = (token,)
                    if got is not None:
                        got, *tokens = lax.optimization_barrier((got, token))
                if got is not None:
                    value = stacked(value, got, kind if n == len(seq_bits) - 1 else "v")
            return value, results, tokens

        x_in = layer_input[0]

        def normed(value):
            mu = jnp.mean(value, axis=-1, keepdims=True)
            centred = value - mu
            rs = lax.rsqrt(jnp.mean(centred * centred, axis=-1, keepdims=True) + EPSILON)
            return centred * rs, rs

        def norm_kernel(need, done, x_r, g_r, o):
            o[...] = (normed(x_r[...].astype(F32))[0] * g_r[...]).astype(BF)

        g1_row = ln1_gain.reshape(1, -1)
        (xn,) = call(
            norm_kernel,
            [("h", x_in), ("v", g1_row)],
            [("h", shaped((quarter, width), BF))],
            margin=8,
            name="first_norm",
        )
        xn_core = swap(xn, "head", 1)
        xn_x = swap(xn, "head", 2)

        gain_part = fence(jnp.concatenate([sub_gain_attn, sub_gain_ffn]).reshape(1, -1), xn)
        gain_pair = jnp.concatenate([gain_part, swap(gain_part, "head", 1)], 0)
        gain_rel = jnp.concatenate([gain_pair, swap(gain_pair, "head", 2)], 0)
        gain_attn = gain_rel[:, :cols].reshape(1, width)
        g2_row = ln2_gain.reshape(1, -1)
        gain_ffn = gain_rel[:, cols:]
        w_own = jnp.concatenate([w_out, w_in, w_ffo], 0)
        w_core = swap(w_own, "head", 1)
        dy_own = lax.dynamic_slice_in_dim(dy, h * quarter, quarter, 0)

        seg_begin = s * tokens
        doc = jnp.clip((document_start - seg_begin) // DOC_MIN + 1, 0, tokens // DOC_MIN)
        lane = jnp.arange(LANES, dtype=jnp.int32)[None, :]
        same = lane - cols == doc[:, None]
        feature_lane = lane >= cols
        k_feat = jnp.where(same, 1.0, 0.0).astype(BF)
        q_feat = jnp.where(feature_lane & ~same, APART, 0.0).astype(BF)
        shift = (h * heads + jnp.arange(heads, dtype=jnp.int32)) % DILATION_RATE
        start_grid = document_start.reshape(rows_dil, DILATION_RATE)
        pick = jnp.arange(DILATION_RATE, dtype=jnp.int32)[:, None] == shift[None, :]
        start_dil = jnp.sum(jnp.where(pick[None], start_grid[:, :, None], 0), axis=1).T
        start_row = start_dil.reshape(1, heads * rows_dil)

        w_pad = jnp.pad(w_qkv, ((0, 0), (0, 0), (0, LANES - cols)))
        w_turn = w_qkv.transpose(0, 2, 1).reshape(3 * cols, width)
        w_rows = w_own.shape[0]
        piece = w_rows // (2 * PIECES)
        my_half = (s % 2) * (w_rows // 2)
        w_cut = [
            lax.dynamic_slice_in_dim(w_own, my_half + n * piece, piece, 0) for n in range(PIECES)
        ]
        xn_x = fence(
            xn_x, w_pad, w_turn, q_feat, k_feat, *w_cut, dy_own, start_row, gain_attn, gain_ffn, g2_row
        )
        xn_diag = swap(xn_x, "head", 1)
        w_half = [swap(w, "head", 2) for w in lax.optimization_barrier((*w_cut, xn_x))[:PIECES]]

        def head_shift(h_value, l):
            return lax.rem(h_value * heads + l, DILATION_RATE)

        def spread(h_value, l):
            a = iota((rows_dil, tokens), 0)
            p = iota((rows_dil, tokens), 1)
            return jnp.where(p == a * DILATION_RATE + head_shift(h_value, l), 1.0, 0.0).astype(BF)

        def of_head(l):
            return slice(l * HEAD_SIZE, (l + 1) * HEAD_SIZE)

        def project_kernel(
            need, done, h_s, b0, b1, b2, b3, w_r, qf, kf,
            q_o, k_o, v_o, kt_o, vt_o, x_o, dil_kv, dil_q, qt_s,
        ):
            hv = h_s[0]
            for i in (5, 6, 7):
                need(i)
            for r, b in enumerate((b0, b1, b2, b3)):
                base = pl.multiple_of((hv ^ r) * quarter, quarter)
                span = pl.ds(base, quarter)
                need(1 + r)
                xb = b[...]
                x_o[span, :] = xb
                qv = dot(xb, w_r[0]).astype(BF) * BF(HEAD_SIZE**-0.5)
                q_o[span, :] = qv + qf[span, :]
                kv = dot(xb, w_r[1]).astype(BF)
                k_o[span, :] = kv + kf[span, :]
                vv = dot(xb, w_r[2]).astype(BF)
                v_o[span, :] = vv
                qt_s[:, span] = turned(qv)[:cols].astype(BF)
                kt_o[:, span] = turned(kv)[:cols].astype(BF)
                vt_o[:, span] = turned(vv)[:cols].astype(BF)
            done(5)
            for l in range(heads):
                sel = spread(hv, l)
                dil_q[of_head(l), :] = dot_nt(qt_s[of_head(l), :], sel).astype(BF)
                dil_kv[of_head(l), :] = dot_nt(kt_o[of_head(l), :], sel).astype(BF)
                dil_kv[cols + l * HEAD_SIZE : cols + (l + 1) * HEAD_SIZE, :] = dot_nt(
                    vt_o[of_head(l), :], sel
                ).astype(BF)

        q_a, k_a, v_a, k_t, v_t, x_all, dil_kv, dil_q = call(
            project_kernel,
            [
                ("s", h_ref),
                ("m", xn),
                ("m", xn_core),
                ("m", xn_x),
                ("m", xn_diag),
                ("l", w_pad),
                ("l", q_feat),
                ("l", k_feat),
            ],
            [
                ("p", shaped((tokens, LANES), BF)),
                ("p", shaped((tokens, LANES), BF)),
                ("p", shaped((tokens, LANES), BF)),
                ("p", shaped((cols, tokens), BF)),
                ("v", shaped((cols, tokens), BF)),
                ("h", shaped((tokens, width), BF)),
                ("v", shaped((2 * cols, rows_dil), BF)),
                ("v", shaped((cols, rows_dil), BF)),
            ],
            scratch=[pltpu.VMEM((cols, tokens), BF)],
            name="project",
        )

        def stack_heads(value, size=heads):
            keep = iota(value.shape, 1) // HEAD_SIZE
            zero = jnp.zeros_like(value)
            return jnp.concatenate(
                [jnp.where((keep == l) | (keep >= size), value, zero) for l in range(size)], 0
            )

        wide = heads * BLOCK

        def causal_block():
            return iota((BLOCK, wide), 0) <= iota((BLOCK, wide), 1) % BLOCK

        def near_kernel(part, need, done, q_r, k_r, vt_r, o_o, lse_o):
            for n, i in enumerate(part):
                q_i = stack_heads(q_r[i * BLOCK : (i + 1) * BLOCK, :])
                top = total = None
                outs = None
                for j in [i] + list(range(i)):
                    sc = dot_nt(k_r[j * BLOCK : (j + 1) * BLOCK, :], q_i)
                    if j == i:
                        sc = jnp.where(causal_block(), sc, NEGATIVE)
                    part_top = jnp.max(sc, axis=0, keepdims=True)
                    new_top = part_top if top is None else jnp.maximum(top, part_top)
                    pr = jnp.exp(sc - new_top)
                    part_sum = jnp.sum(pr, axis=0, keepdims=True)
                    pb = pr.astype(BF)
                    fresh = [
                        dot(
                            vt_r[of_head(l), j * BLOCK : (j + 1) * BLOCK],
                            pb[:, l * BLOCK : (l + 1) * BLOCK],
                        )
                        for l in range(heads)
                    ]
                    if top is None:
                        total, outs = part_sum, fresh
                    else:
                        shrink = jnp.exp(top - new_top)
                        total = total * shrink + part_sum
                        outs = [
                            o * shrink[:, l * BLOCK : (l + 1) * BLOCK] + f
                            for l, (o, f) in enumerate(zip(outs, fresh))
                        ]
                    top = new_top
                lse = top + jnp.log(total)
                inv = 1.0 / total
                for l in range(heads):
                    cut = slice(l * BLOCK, (l + 1) * BLOCK)
                    o_o[of_head(l), n * BLOCK : (n + 1) * BLOCK] = outs[l] * inv[:, cut]
                    lse_o[l : l + 1, n * BLOCK : (n + 1) * BLOCK] = lse[:, cut]

        near_lse = []

        def near_work(part):
            def work(*after):
                size = len(part) * BLOCK
                after = [*after, *w_half[len(near_lse) - 1 : len(near_lse)]]
                result = call(
                    lambda *refs: near_kernel(part, *refs),
                    [("p", q_a), ("p", k_a), ("v", v_t)],
                    [("v", shaped((cols, size), F32)), ("v", shaped((heads, size), F32))],
                    name="near_forward",
                    margin=24,
                    after=after,
                )
                near_lse.append(result[1])
                return result, result[1]

            return work

        far_kv, near_out, _ = gather_seq(dil_kv, [near_work(part) for part in parts], "h")
        w_other = [swap(w, "seq", 1) for w in w_half]
        near_o = [o for o, _ in near_out]
        n_parts = len(parts)

        def joined(refs, rows):
            pieces = []
            for i in range(n_blocks):
                p, n = home[i]
                pieces.append(refs[p][rows, n * BLOCK : (n + 1) * BLOCK])
            return jnp.concatenate(pieces, 1)

        def stack_dil(value):
            keep = iota(value.shape, 1) // HEAD_SIZE
            zero = jnp.zeros_like(value)
            return jnp.concatenate([jnp.where(keep == l, value, zero) for l in range(heads)], 0)

        far_wide = heads * rows_dil

        def far_place(p_s, key_owner, query_owner):
            col = iota((rows_dil, far_wide), 1)
            off = lax.rem(p_s[0] * heads + col // rows_dil, DILATION_RATE)
            key = key_owner * tokens + iota((rows_dil, far_wide), 0) * DILATION_RATE + off
            query = query_owner * tokens + (col % rows_dil) * DILATION_RATE + off
            return key, query

        def far_kernel(need, done, *refs):
            p_s, q_r, kv_r, start_r = refs[:4]
            o_r = refs[4 : 4 + n_parts]
            lse_r = refs[4 + n_parts : 4 + 2 * n_parts]
            ao_o, l_o, ldil_o, sum_o, *aob, top_s, total_s, out_s, low_s = refs[4 + 2 * n_parts :]
            hv = p_s[0]
            sv = p_s[1]
            q_v = stack_dil(turned(q_r[...]).astype(BF))
            start_v = start_r[...]
            top_s[...] = jnp.full((8, far_wide), NEGATIVE, F32)
            total_s[...] = jnp.zeros((8, far_wide), F32)
            out_s[...] = jnp.zeros((HEAD_SIZE, far_wide), F32)

            @pl.loop(0, n_far)
            def _(b):
                owner = p_s[2 + b]

                @pl.when(owner <= sv)
                def _():
                    top = top_s[:1]
                    sc = dot_nt(turned(kv_r[b, :cols]).astype(BF), q_v)
                    key, query = far_place(p_s, owner, sv)
                    sc = jnp.where((key <= query) & (key >= start_v), sc, NEGATIVE)
                    new_top = jnp.maximum(top, jnp.max(sc, axis=0, keepdims=True))
                    pr = jnp.exp(sc - new_top)
                    shrink = jnp.exp(top - new_top)
                    total_s[:1] = total_s[:1] * shrink + jnp.sum(pr, axis=0, keepdims=True)
                    pb = pr.astype(BF)
                    fresh = jnp.concatenate(
                        [
                            dot(
                                kv_r[b, cols + l * HEAD_SIZE : cols + (l + 1) * HEAD_SIZE],
                                pb[:, l * rows_dil : (l + 1) * rows_dil],
                            )
                            for l in range(heads)
                        ],
                        1,
                    )
                    out_s[...] = out_s[...] * shrink + fresh
                    top_s[:1] = new_top

            sum_o[...] = jnp.zeros((8, 128), F32)
            total = total_s[:1]
            lse_far = top_s[:1] + jnp.log(total)
            out = out_s[...] / total
            for l in range(heads):
                cut = slice(l * rows_dil, (l + 1) * rows_dil)
                rows = of_head(l)
                lf = lse_far[:, cut]
                sum_o[1:2, :] += lf
                put = spread(hv, l)
                l8 = jnp.broadcast_to(lf, (8, rows_dil))
                full_lf = sum(dot(t, put) for t in thirds(l8))[:1]
                high, low = halves(out[:, cut])
                full_o = dot(high, put) + dot(low, put)
                dilated = iota((1, tokens), 1) % DILATION_RATE == head_shift(hv, l)
                ln = joined(lse_r, slice(l, l + 1))
                for part in range(tokens // 128):
                    sum_o[:1, :] += ln[:, part * 128 : (part + 1) * 128]
                peak = jnp.maximum(ln, full_lf)
                both = peak + jnp.log(jnp.exp(ln - peak) + jnp.exp(full_lf - peak))
                tot = jnp.where(dilated, both, ln)
                w_near = jnp.exp(ln - tot)
                w_far = jnp.where(dilated, jnp.exp(full_lf - tot), 0.0)
                ao = joined(o_r, rows) * w_near + full_o * w_far
                ao_o[rows, :] = ao
                low_s[rows, :] = ao.astype(BF)
                l_o[l : l + 1, :] = tot
                t8 = jnp.broadcast_to(tot, (8, tokens))
                ldil_o[l : l + 1, :] = sum(dot_nt(t, put) for t in thirds(t8))[:1]
            for r, o in enumerate(aob):
                base = pl.multiple_of((hv ^ r) * quarter, quarter)
                o[...] = low_s[:, pl.ds(base, quarter)]

        ao_t, l_all, l_dil, lse_sums, *ao_low = call(
            far_kernel,
            [
                ("s", place),
                ("v", dil_q),
                ("h", far_kv),
                ("v", start_row),
                *[("v", o) for o in near_o],
                *[("v", lse) for lse in near_lse],
            ],
            [
                ("h", shaped((cols, tokens), F32)),
                ("h", shaped((heads, tokens), F32)),
                ("h", shaped((heads, rows_dil), F32)),
                ("h", shaped((8, 128), F32)),
                ("h", shaped((cols, quarter), BF)),
                *[("v", shaped((cols, quarter), BF))] * (n_head - 1),
            ],
            scratch=[
                pltpu.VMEM((8, far_wide), F32),
                pltpu.VMEM((8, far_wide), F32),
                pltpu.VMEM((HEAD_SIZE, far_wide), F32),
                pltpu.VMEM((cols, tokens), BF),
            ],
            name="far_forward",
            after=w_other[:1],
        )

        def exchange(pieces):
            return [pieces[0]] + [swap(pieces[r], "head", r) for r in range(1, n_head)]

        ao_rows = exchange(ao_low)
        *w_side, _ = lax.optimization_barrier((*w_half, *w_other, ao_low[0]))
        w_diag = [swap(w, "head", 1) for w in w_side]

        full_ff = ff_part * n_head
        chunk = min(CHUNK, quarter)
        order = (1, 3, 0, 2)
        slot = {r: n for n, r in enumerate(order)}

        def row_kernel(
            need, done, s_r, x_r, a0, a1, a2, a3, w0, w1, dy_r, ga_r, gf_r, g2_r, *refs
        ):
            side, refs = refs[: 4 * PIECES], refs[4 * PIECES :]
            (
            y_o, an_o, dhb_o, hn_o, gn_o, du_o, dao0, dao1, dao2, dao3, dh_o, va_o, vf_o, v2_o,
            gu_s, slope_s, dgn_s, w_out_s, hid_s, w2, w3, semaphores,
            ) = refs
            ws = (w0, w1, w2, w3)
            copies = []
            for n, ref in enumerate(side):
                half = (s_r[0] + n // PIECES) % 2
                at = pl.multiple_of(half * (w_rows // 2) + n % PIECES * piece, 8)
                copy = pltpu.make_async_copy(
                    ref, ws[2 + n // (2 * PIECES)].at[pl.ds(at, piece)], semaphores.at[n]
                )
                copy.start()
                copies.append(copy)
            for i in range(2, 6):
                need(i)
            ao = jnp.concatenate([a[...].astype(F32) for a in (a0, a1, a2, a3)], 0)
            mu_a = jnp.mean(ao, axis=0, keepdims=True)
            power = jnp.mean(ao * ao, axis=0, keepdims=True)
            rs_a = lax.rsqrt(power - mu_a * mu_a + EPSILON)
            ahat = (ao - mu_a) * rs_a
            ga = jnp.broadcast_to(ga_r[...], (128, width)).T[:, :1]
            an_t = (ahat * ga).astype(BF)
            an_o[...] = an_t
            for r, w in enumerate(ws):
                if r < 2:
                    need(6 + r)
                elif r == 2:
                    for copy in copies:
                        copy.wait()
                w_out_s[r * cols : (r + 1) * cols, :] = w[:cols, :]
            hid_s[...] = x_r[...].astype(F32) + dot(turned(an_t).astype(BF), w_out_s[...])
            g2 = g2_r[...]
            vf_o[...] = jnp.zeros((n_head, ff_part), F32)
            v2_o[...] = jnp.zeros((1, width), F32)
            for c in range(quarter // chunk):
                span = slice(c * chunk, (c + 1) * chunk)
                hid = hid_s[span, :]
                mu2 = jnp.mean(hid, axis=-1, keepdims=True)
                centred = hid - mu2
                rs2 = lax.rsqrt(jnp.mean(centred * centred, axis=-1, keepdims=True) + EPSILON)
                xhat2 = centred * rs2
                hn = (xhat2 * g2).astype(BF)
                hn_o[span, :] = hn
                if c == 0:
                    need(8)
                dy_c = dy_r[span, :]
                sums = [jnp.zeros((chunk, 1), F32)] * 4
                for r, w in enumerate(ws):
                    u = dot(hn, w[cols : cols + width, :])
                    bell = jnp.exp(u * u * -0.5)
                    t = 1.0 / (1.0 + jnp.abs(u) * (ERF_P / math.sqrt(2.0)))
                    poly = ERF_C[4]
                    for coefficient in ERF_C[3::-1]:
                        poly = poly * t + coefficient
                    tail = poly * t * bell * 0.5
                    phi = jnp.where(u >= 0.0, 1.0 - tail, tail)
                    gu = u * phi
                    dgn = dot_nt(dy_c, w[cols + width :, :])
                    c_g = dgn * gf_r[r : r + 1, :]
                    gu_s[r] = gu
                    slope_s[r] = phi + u * bell * GAUSS_NORM
                    dgn_s[r] = dgn
                    terms = (gu, gu * gu, c_g, c_g * gu)
                    sums = [a + jnp.sum(b, axis=-1, keepdims=True) for a, b in zip(sums, terms)]
                mu_g = sums[0] / full_ff
                rs_g = lax.rsqrt(sums[1] / full_ff - mu_g * mu_g + EPSILON)
                m1 = sums[2] / full_ff
                m2 = (sums[3] - mu_g * sums[2]) * rs_g / full_ff
                y = hid
                dhn = jnp.zeros((chunk, width), F32)
                for r, w in enumerate(ws):
                    gf = gf_r[r : r + 1, :]
                    ghat = (gu_s[r] - mu_g) * rs_g
                    dgn = dgn_s[r]
                    gn = (ghat * gf).astype(BF)
                    du = (rs_g * (dgn * gf - m1 - ghat * m2) * slope_s[r]).astype(BF)
                    gn_o[slot[r], span, :] = gn
                    du_o[slot[r], span, :] = du
                    vf_o[r : r + 1, :] += jnp.sum(dgn * ghat, axis=0, keepdims=True)
                    y = y + dot(gn, w[cols + width :, :])
                    dhn = dhn + dot_nt(du, w[cols : cols + width, :])
                y_o[span, :] = y.astype(BF)
                v2_o[...] += jnp.sum(dhn * xhat2, axis=0, keepdims=True)
                c2 = dhn * g2
                dh = dy_c.astype(F32) + rs2 * (
                    c2
                    - jnp.mean(c2, axis=-1, keepdims=True)
                    - xhat2 * jnp.mean(c2 * xhat2, axis=-1, keepdims=True)
                )
                dh_o[span, :] = dh
                dhb_o[span, :] = dh.astype(BF)
            for k in (0, 1, 2, 3, 4, 5, 10):
                done(k)
            dan = dot_nt(w_out_s[...], dhb_o[...])
            column = jnp.sum(dan * ahat, axis=-1, keepdims=True)
            va_o[...] = jnp.broadcast_to(column, (width, 128)).T[:1]
            c_a = dan * ga
            dao = rs_a * (
                c_a
                - jnp.mean(c_a, axis=0, keepdims=True)
                - ahat * jnp.mean(c_a * ahat, axis=0, keepdims=True)
            )
            for r, o in enumerate((dao0, dao1, dao2, dao3)):
                o[...] = dao[r * cols : (r + 1) * cols].astype(BF)

        y_rows, an_t, dhb, hn2, gn, du, *dao_low, dh, v_attn, v_ffn, v_ln2 = call(
            row_kernel,
            [
                ("s", s_ref),
                ("h", x_in),
                *[("m", a) for a in ao_rows],
                ("l", w_own),
                ("l", w_core),
                ("l", dy_own),
                ("v", gain_attn),
                ("v", gain_ffn),
                ("v", g2_row),
                *[("a", w) for w in (*w_side, *w_diag)],
            ],
            [
                ("h", shaped((quarter, width), BF)),
                ("h", shaped((width, quarter), BF)),
                ("h", shaped((quarter, width), BF)),
                ("h", shaped((quarter, width), BF)),
                ("h", shaped((n_head, quarter, ff_part), BF)),
                ("h", shaped((n_head, quarter, ff_part), BF)),
                *[("v", shaped((cols, quarter), BF))] * n_head,
                ("h", shaped((quarter, width), F32)),
                ("v", shaped((1, width), F32)),
                ("v", shaped((n_head, ff_part), F32)),
                ("v", shaped((1, width), F32)),
            ],
            scratch=[
                pltpu.VMEM((n_head, chunk, ff_part), F32),
                pltpu.VMEM((n_head, chunk, ff_part), F32),
                pltpu.VMEM((n_head, chunk, ff_part), F32),
                pltpu.VMEM((width, width), BF),
                pltpu.VMEM((quarter, width), F32),
                pltpu.VMEM((w_rows, width), BF),
                pltpu.VMEM((w_rows, width), BF),
                pltpu.SemaphoreType.DMA((4 * PIECES,)),
            ],
            margin=14,
            name="rows",
        )
        output = y_rows[None]
        dao_blocks = exchange(dao_low)


        def weights_kernel(
            need, done, gn_r, dy_r, hn_r, du_r, an_r, dhb_r, send_o, own_o, side_o, send_i, keep_i
        ):
            need(1)
            for n, o in enumerate((send_o.at[0], send_o.at[1], own_o, side_o)):
                need(0, n)
                o[...] = dot_tn(gn_r[n], dy_r[...]).astype(BF)
                done(*((0, n) if n < 2 else (n - 1, 0)))
            for i in (2, 4, 5):
                need(i)
            for n, r in enumerate(order):
                need(3, n)
                o = send_i if n < 2 else keep_i
                o[n % 2, :width] = dot_tn(hn_r[...], du_r[n]).astype(BF)
                rows = an_r[r * cols : (r + 1) * cols, :]
                o[n % 2, width:] = dot(rows, dhb_r[...]).astype(BF)
                done(3 + n // 2, n % 2)

        one = ("h", shaped((ff_part, width), BF))
        two = ("b", shaped((2, width + cols, width), BF))
        ffo_send, ffo_own, ffo_side, in_send, in_keep = call(
            weights_kernel,
            [("b", gn), ("l", dy_own), ("l", hn2), ("b", du), ("l", an_t), ("l", dhb)],
            [("b", shaped((2, ff_part, width), BF)), one, one, two, two],
            name="weight_gradients",
        )

        def plus(*terms):
            return sum(t.astype(F32) for t in terms).astype(BF)

        class Half:
            def __init__(self, terms, bit):
                self.terms = [t if isinstance(t, tuple) else (t, None) for t in terms]
                self.bit = bit
                self.size = self.terms[0][0].shape[-2] // 2

            def shapes(self):
                return [("v", shaped((self.size, width), BF))] * 2

            def buffers(self):
                return 2 * len(self.terms)

            def start(self, index, ins, outs, bufs, begin):
                upper = (index // self.bit) % 2
                for n, (_, lead) in enumerate(self.terms):
                    ref = ins[n] if lead is None else ins[n].at[lead]
                    for m, at in enumerate(((1 - upper) * self.size, upper * self.size)):
                        begin(ref.at[pl.ds(pl.multiple_of(at, 8), self.size)], bufs[2 * n + m])

            def plain(self):
                found = []
                upper = (s // self.bit) % 2
                for at in ((1 - upper) * self.size, upper * self.size):
                    parts = [t if lead is None else t[lead] for t, lead in self.terms]
                    parts = [lax.dynamic_slice_in_dim(t, at, self.size, 0) for t in parts]
                    found.append(plus(*parts))
                return found

            def finish(self, outs, bufs):
                for m in range(2):
                    parts = [bufs[2 * n + m][...].astype(F32) for n in range(len(self.terms))]
                    outs[m][...] = sum(parts[1:], parts[0]).astype(BF)

        class Joined:
            def __init__(self, own, got, bit):
                self.terms = [(own, None), (got, None)]
                self.bit = bit
                self.size = own.shape[0]

            def shapes(self):
                return [("v", shaped((2 * self.size, width), BF))]

            def buffers(self):
                return 0

            def start(self, index, ins, outs, bufs, begin):
                upper = (index // self.bit) % 2
                for ref, at in zip(ins, (upper * self.size, (1 - upper) * self.size)):
                    begin(ref, outs[0].at[pl.ds(pl.multiple_of(at, 8), self.size)])

            def plain(self):
                own, got = [t for t, _ in self.terms]
                upper = (s // self.bit) % 2 == 1
                return [
                    jnp.where(upper, jnp.concatenate([got, own], 0), jnp.concatenate([own, got], 0))
                ]

            def finish(self, outs, bufs):
                pass

        def combine(jobs):
            made = combine_tiles([job for job in jobs if job.size % 8 == 0])
            return [made.pop(0) if job.size % 8 == 0 else job.plain() for job in jobs]

        def combine_tiles(jobs):
            if not jobs:
                return []
            n_in = [len(job.terms) for job in jobs]
            n_out = [len(job.shapes()) for job in jobs]
            n_buf = [job.buffers() for job in jobs]
            total = sum(max(job.buffers(), len(job.terms)) for job in jobs)

            def kernel(need, done, s_r, *refs):
                index = s_r[0]
                ins = refs[: sum(n_in)]
                outs = refs[sum(n_in) : sum(n_in) + sum(n_out)]
                bufs = refs[sum(n_in) + sum(n_out) : -1]
                semaphores = refs[-1]
                found = []

                def begin(source, target):
                    copy = pltpu.make_async_copy(source, target, semaphores.at[len(found)])
                    copy.start()
                    found.append(copy)

                work = []
                a = b = c = 0
                for n, job in enumerate(jobs):
                    mine = (outs[b : b + n_out[n]], bufs[c : c + n_buf[n]])
                    before = len(found)
                    job.start(index, ins[a : a + n_in[n]], *mine, begin)
                    work.append((job, mine, found[before:]))
                    a, b, c = a + n_in[n], b + n_out[n], c + n_buf[n]
                for job, mine, copies in work:
                    for copy in copies:
                        copy.wait()
                    job.finish(*mine)

            results = call(
                kernel,
                [("s", s_ref), *[("a", t) for job in jobs for t, _ in job.terms]],
                [o for job in jobs for o in job.shapes()],
                scratch=[
                    *[
                        pltpu.VMEM((job.size, width), BF)
                        for job in jobs
                        for _ in range(job.buffers())
                    ],
                    pltpu.SemaphoreType.DMA((total,)),
                ],
                name="combine",
            )
            found = []
            at = 0
            for n in n_out:
                found.append(results[at : at + n])
                at += n
            return found

        n_note = 3 * heads
        note_rows = (3 * n_note + 15) // 16 * 16

        def prepare_kernel(
            need, done, h_s, d0, d1, d2, d3, ao_r, q_r, l_r, start_r, do_o, delta_o, sent_o, ddil_o, dt_s
        ):
            hv = h_s[0]
            for r, d in enumerate((d0, d1, d2, d3)):
                need(1 + r)
                base = pl.multiple_of((hv ^ r) * quarter, quarter)
                dt_s[:, pl.ds(base, quarter)] = d[...]
            dao_v = dt_s[...].astype(F32)
            grown = jnp.concatenate([dao_v, jnp.zeros((LANES - cols, tokens), F32)], 0)
            do_o[...] = grown.T.astype(BF)
            need(5)
            prod = dao_v * ao_r[...]
            sent_o[:cols, :] = q_r[...]
            for l in range(heads):
                sel = spread(hv, l)
                at = cols + l * HEAD_SIZE
                sent_o[at : at + HEAD_SIZE, :] = dot_nt(dt_s[of_head(l), :], sel).astype(BF)
                delta = jnp.sum(prod[of_head(l)], axis=0, keepdims=True)
                delta_o[l : l + 1, :] = delta
                d8 = jnp.broadcast_to(delta, (8, tokens))
                ddil_o[l : l + 1, :] = sum(dot_nt(t, sel) for t in thirds(d8))[:1]
            found = [l_r[l : l + 1, :] for l in range(heads)]
            found += [ddil_o[l : l + 1, :] for l in range(heads)]
            found += [start_r[l : l + 1, :].astype(F32) for l in range(heads)]
            row = iota((note_rows, rows_dil), 0)
            notes = jnp.zeros((note_rows, rows_dil), F32)
            for n, value in enumerate(found):
                for t, piece in enumerate(thirds(value)):
                    notes = jnp.where(row == t * n_note + n, piece.astype(F32), notes)
            sent_o[2 * cols :, :] = notes.astype(BF)

        do_a, delta_all, far_note, delta_dil = call(
            prepare_kernel,
            [
                ("s", h_ref),
                ("m", fence(dao_blocks[0], ffo_send, in_send)),
                *[("m", d) for d in dao_blocks[1:]],
                ("l", ao_t),
                ("v", dil_q),
                ("v", l_dil),
                ("v", start_dil),
            ],
            [
                ("p", shaped((tokens, LANES), BF)),
                ("v", shaped((heads, tokens), F32)),
                ("v", shaped((2 * cols + note_rows, rows_dil), BF)),
                ("v", shaped((heads, rows_dil), F32)),
            ],
            scratch=[pltpu.VMEM((cols, tokens), BF)],
            name="prepare_backward",
        )

        def near_back_kernel(part, need, done, q_r, k_r, v_r, kt_r, do_r, l_r, d_r, *rest):
            dq_o, dk_o, dv_o, token_o = rest[-4:]
            fresh = len(rest) == 4
            token_o[...] = jnp.zeros((8, 128), F32)
            for n, i in enumerate(reversed(part)):
                span = slice(i * BLOCK, (i + 1) * BLOCK)
                q_i = stack_heads(q_r[span, :])
                do_i = stack_heads(do_r[span, :])
                lse_i = jnp.concatenate([l_r[l : l + 1, span] for l in range(heads)], 1)
                del_i = jnp.concatenate([d_r[l : l + 1, span] for l in range(heads)], 1)
                dq_i = [None] * heads
                for j in range(i + 1):
                    keys = slice(j * BLOCK, (j + 1) * BLOCK)
                    pr = jnp.exp(dot_nt(k_r[keys, :], q_i) - lse_i)
                    if j == i:
                        pr = jnp.where(causal_block(), pr, 0.0)
                    dp = dot_nt(v_r[keys, :], do_i)
                    ds = (pr * (dp - del_i)).astype(BF)
                    dv = dot(pr.astype(BF), do_i)
                    dk = dot(ds, q_i)
                    if fresh and n == 0:
                        dv_o[keys, :] = dv
                        dk_o[keys, :] = dk
                    else:
                        dv_o[keys, :] += dv
                        dk_o[keys, :] += dk
                    for l in range(heads):
                        add = dot(kt_r[of_head(l), keys], ds[:, l * BLOCK : (l + 1) * BLOCK])
                        dq_i[l] = add if dq_i[l] is None else dq_i[l] + add
                for l in range(heads):
                    dq_o[of_head(l), span] = dq_i[l]

        grown_to = []

        def back_work(part):
            def work(value, *after):
                after = [value, *after]
                if part is parts[0]:
                    in_y = fence(flying["in_y"], value)
                    flying["in_got"] = swap(in_y, "seq", rising[0])
                    after += [flying["ffo_x"], in_y]
                held = [("p", a) for a in grown_to]
                *grown_to[:], token = call(
                    lambda *refs: near_back_kernel(part, *refs),
                    [
                        ("p", q_a),
                        ("p", k_a),
                        ("p", v_a),
                        ("p", k_t),
                        ("p", do_a),
                        ("v", l_all),
                        ("v", delta_all),
                        *held,
                    ],
                    [
                        ("p", shaped((cols, tokens), F32)),
                        ("p", shaped((tokens, LANES), F32)),
                        ("p", shaped((tokens, LANES), F32)),
                        ("v", shaped((8, 128), F32)),
                    ],
                    name="near_backward",
                    margin=20,
                    aliases={7 + n: n for n in range(len(held))},
                    after=after,
                )
                return None, token

            return work

        ffo_send, in_send, _ = lax.optimization_barrier((ffo_send, in_send, far_note))
        ffo_core = swap(ffo_send, "head", 1)
        in_core = swap(in_send, "head", 1)
        flying = {}

        def start_sums(value):
            flying["ffo_x"] = plus(ffo_side, ffo_core[1])
            upper = (s & rising[0]) != 0
            size = (width + cols) // 2
            away = jnp.where(upper, 0, size)
            flying["in_y"], flying["in_own"] = [
                plus(*[lax.dynamic_slice_in_dim(t, at, size, 1) for t in (in_keep, in_core)])
                for at in (away, size - away)
            ]
            flying["ffo_got"] = swap(flying["ffo_x"], "head", 2)
            return None, delta_dil

        far_q, _, tokens_back = gather_seq(
            far_note, [start_sums, *[back_work(part) for part in parts]], "v"
        )
        dq_near, dk_near, dv_near = grown_to
        ffo_got, in_got, *tokens_back = lax.optimization_barrier(
            (flying["ffo_got"], flying["in_got"], *tokens_back)
        )
        (ffo_z, ffo_kept), _ = combine([Half([ffo_own, (ffo_core, 0), ffo_got], rising[1])]) + [None]
        in_x = plus(in_got[1], flying["in_own"][1])
        ffo_z_got = swap(ffo_z, "seq", rising[1])
        in_x_got = swap(in_x, "head", 2)

        def far_back_kernel(need, done, *refs):
            p_s, kv_r, fq_r, start_r, l_r, d_r = refs[:6]
            dqn_r, dkn_r, dvn_r, w_r, x_r, g_r, send_o, keep_o, away_o, stay_o, v_o, d_o, dq_s, dk_s, dv_s = refs[6:]
            hv = p_s[0]
            sv = p_s[1]

            def rows_of(ref, b, first):
                return turned(ref[b, first : first + cols]).astype(BF)

            q_v = stack_dil(rows_of(fq_r, 0, 0))
            do_v = stack_dil(rows_of(fq_r, 0, cols))
            k_own = rows_of(kv_r, 0, 0)
            v_own = rows_of(kv_r, 0, cols)
            start_v = start_r[...]
            l_v = jnp.concatenate([l_r[l : l + 1, :] for l in range(heads)], 1)
            d_v = jnp.concatenate([d_r[l : l + 1, :] for l in range(heads)], 1)
            dq_s[...] = jnp.zeros_like(dq_s)
            dk_s[...] = jnp.zeros_like(dk_s)
            dv_s[...] = jnp.zeros_like(dv_s)

            @pl.loop(0, n_far)
            def _(b):
                owner = p_s[2 + b]

                @pl.when(owner <= sv)
                def _():
                    key, query = far_place(p_s, owner, sv)
                    keep = (key <= query) & (key >= start_v)
                    sc = dot_nt(rows_of(kv_r, b, 0), q_v)
                    pr = jnp.where(keep, jnp.exp(sc - l_v), 0.0)
                    dp = dot_nt(rows_of(kv_r, b, cols), do_v)
                    ds = (pr * (dp - d_v)).astype(BF)
                    for l in range(heads):
                        cut = slice(l * rows_dil, (l + 1) * rows_dil)
                        dq_s[of_head(l), :] += dot(kv_r[b, of_head(l)], ds[:, cut])

                @pl.when(owner >= sv)
                def _():
                    note = fq_r[b, 2 * cols :].astype(F32)

                    def row(kind):
                        found = []
                        for l in range(heads):
                            at = kind * heads + l
                            found.append(
                                sum(note[at + t * n_note : at + t * n_note + 1] for t in range(3))
                            )
                        return jnp.concatenate(found, 1)

                    key, query = far_place(p_s, sv, owner)
                    keep = (key <= query) & (key >= row(2).astype(jnp.int32))
                    q_b = stack_dil(rows_of(fq_r, b, 0))
                    do_b = stack_dil(rows_of(fq_r, b, cols))
                    sc = dot_nt(k_own, q_b)
                    pr = jnp.where(keep, jnp.exp(sc - row(0)), 0.0)
                    dp = dot_nt(v_own, do_b)
                    ds = (pr * (dp - row(1))).astype(BF)
                    dk_s[...] += dot(ds, q_b)
                    dv_s[...] += dot(pr.astype(BF), do_b)

            dk_t = turned(dk_s[...])
            dv_t = turned(dv_s[...])

            def placed(value, l):
                high, low = halves(value[of_head(l)])
                put = spread(hv, l)
                return dot(high, put) + dot(low, put)

            dk_near = dkn_r[...].T
            dv_near = dvn_r[...].T
            scale = HEAD_SIZE**-0.5
            dq_far = dq_s[...]
            for l in range(heads):
                rows = of_head(l)
                d_o[rows, :] = ((dqn_r[rows, :] + placed(dq_far, l)) * scale).astype(BF)
                at = cols + l * HEAD_SIZE
                d_o[at : at + HEAD_SIZE, :] = (dk_near[rows] + placed(dk_t, l)).astype(BF)
                at += cols
                d_o[at : at + HEAD_SIZE, :] = (dv_near[rows] + placed(dv_t, l)).astype(BF)
            for o, n, r in ((send_o, 0, 3), (send_o, 1, 1), (keep_o, 0, 2), (keep_o, 1, 0)):
                base = pl.multiple_of((hv ^ r) * quarter, quarter)
                o[n] = dot_tn(d_o[:, pl.ds(base, quarter)], w_r[...]).astype(o.dtype)
            need(10)
            part = dot(d_o[...], x_r[...])
            half = 3 * cols // 2
            for upper in (0, 1):

                @pl.when(lax.rem(sv, 2) == upper)
                def _():
                    away_o[...] = part[(1 - upper) * half : (2 - upper) * half].astype(BF)
                    stay_o[...] = part[upper * half : (1 + upper) * half].astype(BF)

            v_o[...] = jnp.sum(part * w_r[...].astype(F32), axis=0, keepdims=True) / g_r[...]

        dxn_send, dxn_keep, qkv_away, qkv_stay, v_ln1 = call(
            far_back_kernel,
            [
                ("s", place),
                ("h", far_kv),
                ("v", far_q),
                ("v", start_row),
                ("v", l_dil),
                ("v", delta_dil),
                ("p", dq_near),
                ("p", dk_near),
                ("p", dv_near),
                ("v", w_turn),
                ("l", x_all),
                ("v", g1_row),
            ],
            [
                ("v", shaped((2, quarter, width), BF)),
                ("v", shaped((2, quarter, width), F32)),
                ("v", shaped((3 * cols // 2, width), BF)),
                ("v", shaped((3 * cols // 2, width), BF)),
                ("v", shaped((1, width), F32)),
            ],
            scratch=[
                pltpu.VMEM((3 * cols, tokens), BF),
                pltpu.VMEM((cols, rows_dil), F32),
                pltpu.VMEM((rows_dil, cols), F32),
                pltpu.VMEM((rows_dil, cols), F32),
            ],
            margin=12,
            name="far_backward",
            after=(ffo_z, in_x, *tokens_back),
        )

        dxn_send, ffo_z_got, in_x_got = lax.optimization_barrier((dxn_send, ffo_z_got, in_x_got))

        def sum_rows():
            got = yield dxn_send, "head", 1, 1
            side = (dxn_keep[0] + got[0].astype(F32)).astype(BF)
            over_x = yield side, "head", 2, 3

            def last_kernel(need, done, x_r, g_r, keep_r, got_r, over_r, dh_r, o):
                xhat, rs = normed(x_r[...].astype(F32))
                dxn = keep_r[1] + got_r[1].astype(F32) + over_r[...].astype(F32)
                c = dxn * g_r[...]
                first = jnp.mean(c, axis=-1, keepdims=True)
                second = jnp.mean(c * xhat, axis=-1, keepdims=True)
                o[...] = dh_r[...] + rs * (c - first - xhat * second)

            (result,) = call(
                last_kernel,
                [("v", x_in), ("v", g1_row), ("v", dxn_keep), ("v", got), ("v", over_x), ("v", dh)],
                [("v", shaped((quarter, width), F32))],
                margin=12,
                name="first_norm_backward",
            )
            return result

        def sum_seq(terms, scatter, spread, last=1):
            for bit in scatter:
                send, kept = yield Half(terms, bit)
                terms = [kept, (yield send, "seq", bit, 1)]
            value = None
            for bit in spread:
                if value is None:
                    value = plus(*terms)
                rounds = last if bit == spread[-1] else 1
                got = yield value, "seq", bit, rounds
                (value,) = yield Joined(value, got, bit)
            return value

        def sum_ffo():
            bits = rising[2:] + rising[:1]
            terms = [ffo_kept, ffo_z_got]
            value = yield from sum_seq(terms, bits, bits[::-1] + rising[1:2])
            return value.astype(F32)

        def sum_in():
            terms = [(in_got, 0), (flying["in_own"], 0), in_x_got]
            value = yield from sum_seq(terms, rising[1:], rising[::-1])
            return value[:width].astype(F32), value[width:].astype(F32)

        def sum_qkv():
            got = yield qkv_away, "seq", rising[0], 1
            return (yield from sum_seq([qkv_stay, got], rising[1:], rising[::-1]))

        def sum_small():
            v_rel = jnp.concatenate([v_attn.reshape(n_head, cols), v_ffn], 1)
            size = v_rel.shape[1]
            common = jnp.concatenate([v_ln1.reshape(-1), v_ln2.reshape(-1), lse_sums[:2].reshape(-1)])
            got = yield jnp.concatenate([v_rel[1], v_rel[3], common]), "head", 1, 1
            mine = v_rel[0] + got[:size]
            other = v_rel[2] + got[size : 2 * size]
            common = common + got[2 * size :]
            got = yield jnp.concatenate([other, common]), "head", 2, 1
            small = jnp.concatenate([mine, common]) + got
            for bit in rising:
                small = small + (yield small, "seq", bit, 1)
            total_heads = heads * n_head
            counts = jnp.array([tokens * n_seq * total_heads, rows_dil * n_seq * total_heads], F32)
            means = jnp.sum(small[size + 2 * width :].reshape(2, 128), axis=1) / counts
            return (
                small[:cols],
                small[cols:size],
                small[size : size + width],
                small[size + width : size + 2 * width],
                means,
            )

        def in_rounds(chains):
            results = [None] * len(chains)
            large = (1, 2, 3)
            asks = {}
            flying = {}
            ended = []

            def resume(n, value):
                try:
                    asks[n] = chains[n].send(value)
                except StopIteration as stop:
                    results[n] = stop.value
                    ended.append(n)

            def settle():
                jobs = [n for n in asks if not isinstance(asks[n], tuple)]
                if jobs:
                    for n, made in zip(jobs, combine([asks.pop(n) for n in jobs])):
                        resume(n, made)

            for n in range(len(chains)):
                resume(n, None)
            number = 0
            while asks or flying:
                settle()
                for n in list(asks)[::-1] if number == 0 else list(asks):
                    value, axis, bit, rounds = asks.pop(n)
                    flying[n] = (number + rounds - 1, swap(value, axis, bit))
                due = [n for n in flying if flying[n][0] <= number]
                held = tuple(flying.pop(n)[1] for n in due)
                flat, tree = jax.tree.flatten((held, [results[n] for n in ended]))
                held, again = jax.tree.unflatten(tree, lax.optimization_barrier(tuple(flat)))
                for n, value in zip(ended, again):
                    results[n] = value
                for n, got in zip(due, held):
                    if n in large:
                        resume(n, got)
                settle()
                sent = [asks[n][0] for n in large if n in asks]
                for n, got in zip(due, held):
                    if n not in large:
                        resume(n, fence(got, sent[0]) if sent else got)
                number += 1
            return results

        dx, g_ffo, (g_in, g_out), g_qkv, (g_sub_attn, g_sub_ffn, g_ln1, g_ln2, means) = in_rounds(
            [sum_rows(), sum_ffo(), sum_in(), sum_qkv(), sum_small()]
        )
        g_qkv = g_qkv.astype(F32).reshape(3, cols, width).transpose(0, 2, 1)
        return (
            output,
            dx[None],
            g_ln1,
            g_qkv,
            g_sub_attn,
            g_out,
            g_ln2,
            g_in,
            g_sub_ffn,
            g_ffo,
            means,
        )

    return jax.shard_map(
        body,
        mesh=mesh,
        in_specs=(
            P("head", "seq", None),
            P("seq"),
            P(),
            P(None, None, "head"),
            P("head"),
            P("head", None),
            P(),
            P(None, "head"),
            P("head"),
            P("head", None),
            P("seq", None),
        ),
        out_specs=(
            P("head", "seq", None),
            P("head", "seq", None),
            P(),
            P(None, None, "head"),
            P("head"),
            P("head", None),
            P(),
            P(None, "head"),
            P("head"),
            P("head", None),
            P(),
        ),
        check_vma=False,
    )
```

```python
import math

import jax
import jax.numpy as jnp
from jax import lax
from jax.experimental import pallas as pl
from jax.experimental.pallas import tpu as pltpu
from jax.sharding import PartitionSpec as P

HEAD_SIZE = 64
DILATION_RATE = 16
EPSILON = 1e-05
NEGATIVE = -1e30
APART = -(2.0**30)
DOC_MIN = 256
GAUSS_NORM = 1.0 / math.sqrt(2.0 * math.pi)
BLOCK = 256
LANES = 256
BF = jnp.bfloat16
F32 = jnp.float32
ERF_P = 0.3275911
ERF_C = (0.254829592, -0.284496736, 1.421413741, -1.453152027, 1.061405429)
SPLIT = 3
PIECES = 2
CHUNK = 256


def dot(a, b):
    return lax.dot_general(a, b, (((1,), (0,)), ((), ())), preferred_element_type=F32)


def dot_nt(a, b):
    return lax.dot_general(a, b, (((1,), (1,)), ((), ())), preferred_element_type=F32)


def dot_tn(a, b):
    return lax.dot_general(a, b, (((0,), (0,)), ((), ())), preferred_element_type=F32)


def iota(shape, axis):
    return lax.broadcasted_iota(jnp.int32, shape, axis)


def halves(value):
    high = value.astype(BF)
    return high, (value - high.astype(F32)).astype(BF)


def thirds(value):
    high = value.astype(BF)
    rest = value - high.astype(F32)
    middle = rest.astype(BF)
    return high, middle, (rest - middle.astype(F32)).astype(BF)


def fence(value, *before):
    return lax.optimization_barrier((value, *before))[0]


def turned(value):
    return value.astype(F32).T


def room(shape, dtype):
    shape = (1,) * (2 - len(shape)) + tuple(shape)
    size = jnp.dtype(dtype).itemsize
    lanes = (shape[-1] + 127) // 128 * 128
    rows = (shape[-2] + 15) // 16 * 16
    return math.prod(shape[:-2]) * rows * lanes * size


def call(kernel, ins, outs, scratch=(), margin=8, name=None, aliases=None, after=()):
    n_in, n_out, n_after = len(ins), len(outs), len(after)
    spaces = {"s": pltpu.SMEM, "v": pltpu.VMEM, "p": pltpu.VMEM, "a": pl.ANY, "r": pltpu.HBM}
    far_in = [i for i, (kind, _) in enumerate(ins) if kind not in spaces]
    far_out = [i for i, (kind, _) in enumerate(outs) if kind not in spaces]
    n_far = len(far_in) + len(far_out)
    far = [ins[i] for i in far_in] + [outs[i] for i in far_out]
    buffers = [pltpu.VMEM(a.shape, a.dtype) for _, a in far]
    counts = [a.shape[0] if kind == "b" else 1 for kind, a in far]

    def wrapped(*refs):
        refs = (*refs[:n_in], *refs[n_in + n_after :])
        given, results, rest = list(refs[:n_in]), list(refs[n_in : n_in + n_out]), refs[n_in + n_out :]
        arriving, leaving, started = {}, {}, []

        def copies(kind, n, source, target):
            semaphores = rest[n_far]
            first = sum(counts[:n])
            if kind != "b":
                return {0: pltpu.make_async_copy(source, target, semaphores.at[first])}
            return {
                m: pltpu.make_async_copy(source.at[m], target.at[m], semaphores.at[first + m])
                for m in range(counts[n])
            }

        for n, i in enumerate(far_in):
            arriving[i] = copies(ins[i][0], n, given[i], rest[n])
            for copy in arriving[i].values():
                copy.start()
            given[i] = rest[n]
        for n, i in enumerate(far_out, len(far_in)):
            leaving[i] = copies(outs[i][0], n, rest[n], results[i])
            results[i] = rest[n]

        def need(i, m=0):
            arriving[i].pop(m).wait()

        def done(i, m=0):
            copy = leaving[i].pop(m)
            copy.start()
            started.append(copy)

        for i in far_in:
            if ins[i][0] == "h":
                need(i)
        own = rest[n_far + 1 :] if n_far else rest
        kernel(need, done, *given, *results, *own)
        for i in far_in:
            for m in list(arriving[i]):
                need(i, m)
        for i in far_out:
            for m in list(leaving[i]):
                done(i, m)
        for copy in started:
            copy.wait()

    held = [(a.shape, a.dtype) for kind, a in ins if kind not in "spar"]
    held += [(a.shape, a.dtype) for kind, a in outs if kind != "p"]
    held += [(a.shape, a.dtype) for a in scratch if jnp.issubdtype(a.dtype, jnp.number)]
    limit = sum(room(*a) for a in held) + (margin << 20)

    def placed(kind, a):
        if kind in "svam":
            return a
        return pltpu.with_memory_space_constraint(a, spaces.get(kind, pltpu.HBM))

    def shape_of(kind, a):
        if kind == "v":
            return a
        return spaces.get(kind, pltpu.HBM)(a.shape, a.dtype)

    return pl.pallas_call(
        wrapped,
        out_shape=tuple(shape_of(*o) for o in outs),
        in_specs=[
            pl.BlockSpec(memory_space=pl.ANY if kind == "m" else spaces.get(kind, pltpu.HBM))
            for kind, _ in ins
        ]
        + [pl.BlockSpec(memory_space=pl.ANY)] * n_after,
        out_specs=tuple(pl.BlockSpec(memory_space=spaces.get(kind, pltpu.HBM)) for kind, _ in outs),
        scratch_shapes=[
            *buffers,
            *([pltpu.SemaphoreType.DMA((sum(counts),))] if n_far else []),
            *scratch,
        ],
        input_output_aliases=aliases or {},
        compiler_params=pltpu.CompilerParams(vmem_limit_bytes=limit),
        cost_estimate=pl.CostEstimate(flops=0, transcendentals=0, bytes_accessed=0),
        name=name,
    )(*[placed(*a) for a in ins], *after)


def solution(mesh):
    n_head = mesh.shape["head"]
    n_seq = mesh.shape["seq"]

    def swap(value, axis, bit):
        size = n_head if axis == "head" else n_seq
        return lax.ppermute(value, axis, [(i, i ^ bit) for i in range(size)])

    rising = []
    bit = 1
    while bit < n_seq:
        rising.append(bit)
        bit *= 2
    seq_bits = rising[:1] + rising[:0:-1]

    offsets = [0]
    for bit in seq_bits:
        offsets = offsets + [o ^ bit for o in offsets]

    def body(
        layer_input,
        document_start,
        ln1_gain,
        w_qkv,
        sub_gain_attn,
        w_out,
        ln2_gain,
        w_in,
        sub_gain_ffn,
        w_ffo,
        dy,
    ):
        tokens, width = dy.shape
        quarter = layer_input.shape[1]
        cols = w_qkv.shape[2]
        heads = cols // HEAD_SIZE
        rows_dil = tokens // DILATION_RATE
        ff_part = w_in.shape[1]
        n_blocks = tokens // BLOCK
        n_far = n_seq
        h = lax.axis_index("head")
        s = lax.axis_index("seq")
        h_ref = jnp.reshape(h, (1,)).astype(jnp.int32)
        s_ref = jnp.reshape(s, (1,)).astype(jnp.int32)
        far_index = (s ^ jnp.array(offsets, jnp.int32)).astype(jnp.int32)
        place = jnp.concatenate([jnp.stack([h, s]).astype(jnp.int32), far_index])
        shaped = jax.ShapeDtypeStruct

        parts = [[] for _ in range(SPLIT)]
        for i in reversed(range(n_blocks)):
            min(parts, key=lambda part: sum(k + 1 for k in part)).append(i)
        parts = [sorted(part) for part in parts if part]
        n_parts = len(parts)
        home = {i: (p, n) for p, part in enumerate(parts) for n, i in enumerate(part)}

        def stacked(value, got, kind):
            size = value.shape[0]

            def stack_kernel(need, done, v_r, g_r, o_r, semaphores):
                copies = [
                    pltpu.make_async_copy(v_r, o_r.at[:size], semaphores.at[0]),
                    pltpu.make_async_copy(g_r, o_r.at[size:], semaphores.at[1]),
                ]
                for copy in copies:
                    copy.start()
                for copy in copies:
                    copy.wait()

            return call(
                stack_kernel,
                [("a", value), ("a", got)],
                [(kind, shaped((2 * size, *value.shape[1:]), value.dtype))],
                scratch=[pltpu.SemaphoreType.DMA((2,))],
                name="stack",
            )[0]

        def gather_seq(value, works, kind):
            value = value[None]
            results = []
            tokens = ()
            for n in range(max(len(seq_bits), len(works))):
                got = swap(value, "seq", seq_bits[n]) if n < len(seq_bits) else None
                if n < len(works):
                    result, token = works[n](value, *tokens)
                    results.append(result)
                    tokens = (token,)
                    if got is not None:
                        got, *tokens = lax.optimization_barrier((got, token))
                if got is not None:
                    value = stacked(value, got, kind if n == len(seq_bits) - 1 else "v")
            return value, results, tokens

        x_in = layer_input[0]

        def normed(value):
            mu = jnp.mean(value, axis=-1, keepdims=True)
            centred = value - mu
            rs = lax.rsqrt(jnp.mean(centred * centred, axis=-1, keepdims=True) + EPSILON)
            return centred * rs, rs

        def norm_kernel(need, done, x_r, g_r, o):
            o[...] = (normed(x_r[...].astype(F32))[0] * g_r[...]).astype(BF)

        g1_row = ln1_gain.reshape(1, -1)
        (xn,) = call(
            norm_kernel,
            [("h", x_in), ("v", g1_row)],
            [("h", shaped((quarter, width), BF))],
            margin=8,
            name="first_norm",
        )
        xn_core = swap(xn, "head", 1)
        xn_x = swap(xn, "head", 2)

        gain_part = fence(jnp.concatenate([sub_gain_attn, sub_gain_ffn]).reshape(1, -1), xn)
        gain_pair = jnp.concatenate([gain_part, swap(gain_part, "head", 1)], 0)
        gain_rel = jnp.concatenate([gain_pair, swap(gain_pair, "head", 2)], 0)
        gain_attn = gain_rel[:, :cols].reshape(1, width)
        g2_row = ln2_gain.reshape(1, -1)
        gain_ffn = gain_rel[:, cols:]
        w_own = jnp.concatenate([w_out, w_in, w_ffo], 0)
        w_core = swap(w_own, "head", 1)
        dy_own = lax.dynamic_slice_in_dim(dy, h * quarter, quarter, 0)

        seg_begin = s * tokens
        doc = jnp.clip((document_start - seg_begin) // DOC_MIN + 1, 0, tokens // DOC_MIN)
        lane = jnp.arange(LANES, dtype=jnp.int32)[None, :]
        same = lane - cols == doc[:, None]
        feature_lane = lane >= cols
        k_feat = jnp.where(same, 1.0, 0.0).astype(BF)
        q_feat = jnp.where(feature_lane & ~same, APART, 0.0).astype(BF)
        shift = (h * heads + jnp.arange(heads, dtype=jnp.int32)) % DILATION_RATE
        start_grid = document_start.reshape(rows_dil, DILATION_RATE)
        pick = jnp.arange(DILATION_RATE, dtype=jnp.int32)[:, None] == shift[None, :]
        start_dil = jnp.sum(jnp.where(pick[None], start_grid[:, :, None], 0), axis=1).T
        start_row = start_dil.reshape(1, heads * rows_dil)

        w_pad = jnp.pad(w_qkv, ((0, 0), (0, 0), (0, LANES - cols)))
        w_turn = w_qkv.transpose(0, 2, 1).reshape(3 * cols, width)
        w_rows = w_own.shape[0]
        piece = w_rows // (2 * PIECES)
        my_half = (s % 2) * (w_rows // 2)
        w_cut = [
            lax.dynamic_slice_in_dim(w_own, my_half + n * piece, piece, 0) for n in range(PIECES)
        ]
        xn_x = fence(
            xn_x, w_pad, w_turn, q_feat, k_feat, *w_cut, dy_own, start_row, gain_attn, gain_ffn, g2_row
        )
        xn_diag = swap(xn_x, "head", 1)
        w_half = [swap(w, "head", 2) for w in lax.optimization_barrier((*w_cut, xn_x))[:PIECES]]

        def head_shift(h_value, l):
            return lax.rem(h_value * heads + l, DILATION_RATE)

        def spread(h_value, l):
            a = iota((rows_dil, tokens), 0)
            p = iota((rows_dil, tokens), 1)
            return jnp.where(p == a * DILATION_RATE + head_shift(h_value, l), 1.0, 0.0).astype(BF)

        def of_head(l):
            return slice(l * HEAD_SIZE, (l + 1) * HEAD_SIZE)

        def project_kernel(
            need, done, h_s, b0, b1, b2, b3, w_r, qf, kf,
            q_o, k_o, v_o, kt_o, vt_o, x_o, dil_kv, dil_q, qt_s,
        ):
            hv = h_s[0]
            for i in (5, 6, 7):
                need(i)
            for r, b in enumerate((b0, b1, b2, b3)):
                base = pl.multiple_of((hv ^ r) * quarter, quarter)
                span = pl.ds(base, quarter)
                need(1 + r)
                xb = b[...]
                x_o[span, :] = xb
                qv = dot(xb, w_r[0]).astype(BF) * BF(HEAD_SIZE**-0.5)
                q_o[span, :] = qv + qf[span, :]
                kv = dot(xb, w_r[1]).astype(BF)
                k_o[span, :] = kv + kf[span, :]
                vv = dot(xb, w_r[2]).astype(BF)
                v_o[span, :] = vv
                qt_s[:, span] = turned(qv)[:cols].astype(BF)
                kt_o[:, span] = turned(kv)[:cols].astype(BF)
                vt_o[:, span] = turned(vv)[:cols].astype(BF)
            done(5)
            for l in range(heads):
                sel = spread(hv, l)
                dil_q[of_head(l), :] = dot_nt(qt_s[of_head(l), :], sel).astype(BF)
                dil_kv[of_head(l), :] = dot_nt(kt_o[of_head(l), :], sel).astype(BF)
                dil_kv[cols + l * HEAD_SIZE : cols + (l + 1) * HEAD_SIZE, :] = dot_nt(
                    vt_o[of_head(l), :], sel
                ).astype(BF)

        q_a, k_a, v_a, k_t, v_t, x_all, dil_kv, dil_q = call(
            project_kernel,
            [
                ("s", h_ref),
                ("m", xn),
                ("m", xn_core),
                ("m", xn_x),
                ("m", xn_diag),
                ("l", w_pad),
                ("l", q_feat),
                ("l", k_feat),
            ],
            [
                ("p", shaped((tokens, LANES), BF)),
                ("p", shaped((tokens, LANES), BF)),
                ("p", shaped((tokens, LANES), BF)),
                ("p", shaped((cols, tokens), BF)),
                ("v", shaped((cols, tokens), BF)),
                ("h", shaped((tokens, width), BF)),
                ("v", shaped((2 * cols, rows_dil), BF)),
                ("v", shaped((cols, rows_dil), BF)),
            ],
            scratch=[pltpu.VMEM((cols, tokens), BF)],
            name="project",
        )

        def stack_heads(value, size=heads):
            keep = iota(value.shape, 1) // HEAD_SIZE
            zero = jnp.zeros_like(value)
            return jnp.concatenate(
                [jnp.where((keep == l) | (keep >= size), value, zero) for l in range(size)], 0
            )

        wide = heads * BLOCK

        def causal_block():
            return iota((BLOCK, wide), 0) <= iota((BLOCK, wide), 1) % BLOCK

        def near_kernel(part, need, done, q_r, k_r, vt_r, o_o, lse_o):
            for n, i in enumerate(part):
                q_i = stack_heads(q_r[i * BLOCK : (i + 1) * BLOCK, :])
                top = total = None
                outs = None
                for j in [i] + list(range(i)):
                    sc = dot_nt(k_r[j * BLOCK : (j + 1) * BLOCK, :], q_i)
                    if j == i:
                        sc = jnp.where(causal_block(), sc, NEGATIVE)
                    part_top = jnp.max(sc, axis=0, keepdims=True)
                    new_top = part_top if top is None else jnp.maximum(top, part_top)
                    pr = jnp.exp(sc - new_top)
                    part_sum = jnp.sum(pr, axis=0, keepdims=True)
                    pb = pr.astype(BF)
                    fresh = [
                        dot(
                            vt_r[of_head(l), j * BLOCK : (j + 1) * BLOCK],
                            pb[:, l * BLOCK : (l + 1) * BLOCK],
                        )
                        for l in range(heads)
                    ]
                    if top is None:
                        total, outs = part_sum, fresh
                    else:
                        shrink = jnp.exp(top - new_top)
                        total = total * shrink + part_sum
                        outs = [
                            o * shrink[:, l * BLOCK : (l + 1) * BLOCK] + f
                            for l, (o, f) in enumerate(zip(outs, fresh))
                        ]
                    top = new_top
                lse = top + jnp.log(total)
                inv = 1.0 / total
                for l in range(heads):
                    cut = slice(l * BLOCK, (l + 1) * BLOCK)
                    o_o[of_head(l), n * BLOCK : (n + 1) * BLOCK] = outs[l] * inv[:, cut]
                    lse_o[l : l + 1, n * BLOCK : (n + 1) * BLOCK] = lse[:, cut]

        near_lse = []

        def near_work(part):
            def work(*after):
                size = len(part) * BLOCK
                after = [*after, *w_half[len(near_lse) - 1 : len(near_lse)]]
                result = call(
                    lambda *refs: near_kernel(part, *refs),
                    [("p", q_a), ("p", k_a), ("v", v_t)],
                    [("v", shaped((cols, size), F32)), ("v", shaped((heads, size), F32))],
                    name="near_forward",
                    margin=24,
                    after=after,
                )
                near_lse.append(result[1])
                return result, result[1]

            return work

        far_kv, near_out, _ = gather_seq(dil_kv, [near_work(part) for part in parts], "h")
        w_other = [
            swap(fence(w, near_lse[min(n, n_parts - 1)]), "seq", 1) for n, w in enumerate(w_half)
        ]
        near_o = [o for o, _ in near_out]

        def joined(refs, rows):
            pieces = []
            for i in range(n_blocks):
                p, n = home[i]
                pieces.append(refs[p][rows, n * BLOCK : (n + 1) * BLOCK])
            return jnp.concatenate(pieces, 1)

        def stack_dil(value):
            keep = iota(value.shape, 1) // HEAD_SIZE
            zero = jnp.zeros_like(value)
            return jnp.concatenate([jnp.where(keep == l, value, zero) for l in range(heads)], 0)

        far_wide = heads * rows_dil

        def far_place(p_s, key_owner, query_owner):
            col = iota((rows_dil, far_wide), 1)
            off = lax.rem(p_s[0] * heads + col // rows_dil, DILATION_RATE)
            key = key_owner * tokens + iota((rows_dil, far_wide), 0) * DILATION_RATE + off
            query = query_owner * tokens + (col % rows_dil) * DILATION_RATE + off
            return key, query

        def far_kernel(need, done, *refs):
            p_s, q_r, kv_r, start_r = refs[:4]
            o_r = refs[4 : 4 + n_parts]
            lse_r = refs[4 + n_parts : 4 + 2 * n_parts]
            ao_o, l_o, ldil_o, sum_o, *aob, top_s, total_s, out_s, low_s = refs[4 + 2 * n_parts :]
            hv = p_s[0]
            sv = p_s[1]
            q_v = stack_dil(turned(q_r[...]).astype(BF))
            start_v = start_r[...]
            top_s[...] = jnp.full((8, far_wide), NEGATIVE, F32)
            total_s[...] = jnp.zeros((8, far_wide), F32)
            out_s[...] = jnp.zeros((HEAD_SIZE, far_wide), F32)

            @pl.loop(0, n_far)
            def _(b):
                owner = p_s[2 + b]

                @pl.when(owner <= sv)
                def _():
                    top = top_s[:1]
                    sc = dot_nt(turned(kv_r[b, :cols]).astype(BF), q_v)
                    key, query = far_place(p_s, owner, sv)
                    sc = jnp.where((key <= query) & (key >= start_v), sc, NEGATIVE)
                    new_top = jnp.maximum(top, jnp.max(sc, axis=0, keepdims=True))
                    pr = jnp.exp(sc - new_top)
                    shrink = jnp.exp(top - new_top)
                    total_s[:1] = total_s[:1] * shrink + jnp.sum(pr, axis=0, keepdims=True)
                    pb = pr.astype(BF)
                    fresh = jnp.concatenate(
                        [
                            dot(
                                kv_r[b, cols + l * HEAD_SIZE : cols + (l + 1) * HEAD_SIZE],
                                pb[:, l * rows_dil : (l + 1) * rows_dil],
                            )
                            for l in range(heads)
                        ],
                        1,
                    )
                    out_s[...] = out_s[...] * shrink + fresh
                    top_s[:1] = new_top

            sum_o[...] = jnp.zeros((8, 128), F32)
            total = total_s[:1]
            lse_far = top_s[:1] + jnp.log(total)
            out = out_s[...] / total
            for l in range(heads):
                cut = slice(l * rows_dil, (l + 1) * rows_dil)
                rows = of_head(l)
                lf = lse_far[:, cut]
                sum_o[1:2, :] += lf
                put = spread(hv, l)
                l8 = jnp.broadcast_to(lf, (8, rows_dil))
                full_lf = sum(dot(t, put) for t in thirds(l8))[:1]
                high, low = halves(out[:, cut])
                full_o = dot(high, put) + dot(low, put)
                dilated = iota((1, tokens), 1) % DILATION_RATE == head_shift(hv, l)
                ln = joined(lse_r, slice(l, l + 1))
                for part in range(tokens // 128):
                    sum_o[:1, :] += ln[:, part * 128 : (part + 1) * 128]
                peak = jnp.maximum(ln, full_lf)
                both = peak + jnp.log(jnp.exp(ln - peak) + jnp.exp(full_lf - peak))
                tot = jnp.where(dilated, both, ln)
                w_near = jnp.exp(ln - tot)
                w_far = jnp.where(dilated, jnp.exp(full_lf - tot), 0.0)
                ao = joined(o_r, rows) * w_near + full_o * w_far
                ao_o[rows, :] = ao
                low_s[rows, :] = ao.astype(BF)
                l_o[l : l + 1, :] = tot
                t8 = jnp.broadcast_to(tot, (8, tokens))
                ldil_o[l : l + 1, :] = sum(dot_nt(t, put) for t in thirds(t8))[:1]
            for r, o in enumerate(aob):
                base = pl.multiple_of((hv ^ r) * quarter, quarter)
                o[...] = low_s[:, pl.ds(base, quarter)]

        ao_t, l_all, l_dil, lse_sums, *ao_low = call(
            far_kernel,
            [
                ("s", place),
                ("v", dil_q),
                ("h", far_kv),
                ("v", start_row),
                *[("v", o) for o in near_o],
                *[("v", lse) for lse in near_lse],
            ],
            [
                ("h", shaped((cols, tokens), F32)),
                ("h", shaped((heads, tokens), F32)),
                ("h", shaped((heads, rows_dil), F32)),
                ("h", shaped((8, 128), F32)),
                ("h", shaped((cols, quarter), BF)),
                *[("v", shaped((cols, quarter), BF))] * (n_head - 1),
            ],
            scratch=[
                pltpu.VMEM((8, far_wide), F32),
                pltpu.VMEM((8, far_wide), F32),
                pltpu.VMEM((HEAD_SIZE, far_wide), F32),
                pltpu.VMEM((cols, tokens), BF),
            ],
            name="far_forward",
            after=w_other[:1],
        )

        def exchange(pieces):
            return [pieces[0]] + [swap(pieces[r], "head", r) for r in range(1, n_head)]

        ao_rows = exchange(ao_low)
        *w_side, _ = lax.optimization_barrier((*w_half, *w_other, ao_low[0]))
        w_diag = [swap(w, "head", 1) for w in w_side]

        full_ff = ff_part * n_head
        chunk = min(CHUNK, quarter)
        order = (1, 3, 0, 2)
        slot = {r: n for n, r in enumerate(order)}

        def row_kernel(
            need, done, s_r, x_r, a0, a1, a2, a3, w0, w1, dy_r, ga_r, gf_r, g2_r, *refs
        ):
            side, refs = refs[: 4 * PIECES], refs[4 * PIECES :]
            (
            y_o, an_o, dhb_o, hn_o, gn_o, du_o, dao0, dao1, dao2, dao3, dh_o, va_o, vf_o, v2_o,
            gu_s, slope_s, dgn_s, w_out_s, hid_s, w2, w3, semaphores,
            ) = refs
            ws = (w0, w1, w2, w3)
            copies = []
            for n, ref in enumerate(side):
                half = (s_r[0] + n // PIECES) % 2
                at = pl.multiple_of(half * (w_rows // 2) + n % PIECES * piece, 8)
                copy = pltpu.make_async_copy(
                    ref, ws[2 + n // (2 * PIECES)].at[pl.ds(at, piece)], semaphores.at[n]
                )
                copy.start()
                copies.append(copy)
            for i in range(2, 6):
                need(i)
            ao = jnp.concatenate([a[...].astype(F32) for a in (a0, a1, a2, a3)], 0)
            mu_a = jnp.mean(ao, axis=0, keepdims=True)
            power = jnp.mean(ao * ao, axis=0, keepdims=True)
            rs_a = lax.rsqrt(power - mu_a * mu_a + EPSILON)
            ahat = (ao - mu_a) * rs_a
            ga = jnp.broadcast_to(ga_r[...], (128, width)).T[:, :1]
            an_t = (ahat * ga).astype(BF)
            an_o[...] = an_t
            for r, w in enumerate(ws):
                if r < 2:
                    need(6 + r)
                elif r == 2:
                    for copy in copies:
                        copy.wait()
                w_out_s[r * cols : (r + 1) * cols, :] = w[:cols, :]
            hid_s[...] = x_r[...].astype(F32) + dot(turned(an_t).astype(BF), w_out_s[...])
            g2 = g2_r[...]
            vf_o[...] = jnp.zeros((n_head, ff_part), F32)
            v2_o[...] = jnp.zeros((1, width), F32)
            for c in range(quarter // chunk):
                span = slice(c * chunk, (c + 1) * chunk)
                hid = hid_s[span, :]
                mu2 = jnp.mean(hid, axis=-1, keepdims=True)
                centred = hid - mu2
                rs2 = lax.rsqrt(jnp.mean(centred * centred, axis=-1, keepdims=True) + EPSILON)
                xhat2 = centred * rs2
                hn = (xhat2 * g2).astype(BF)
                hn_o[span, :] = hn
                if c == 0:
                    need(8)
                dy_c = dy_r[span, :]
                sums = [jnp.zeros((chunk, 1), F32)] * 4
                for r, w in enumerate(ws):
                    u = dot(hn, w[cols : cols + width, :])
                    bell = jnp.exp(u * u * -0.5)
                    t = 1.0 / (1.0 + jnp.abs(u) * (ERF_P / math.sqrt(2.0)))
                    poly = ERF_C[4]
                    for coefficient in ERF_C[3::-1]:
                        poly = poly * t + coefficient
                    tail = poly * t * bell * 0.5
                    phi = jnp.where(u >= 0.0, 1.0 - tail, tail)
                    gu = u * phi
                    dgn = dot_nt(dy_c, w[cols + width :, :])
                    c_g = dgn * gf_r[r : r + 1, :]
                    gu_s[r] = gu
                    slope_s[r] = phi + u * bell * GAUSS_NORM
                    dgn_s[r] = dgn
                    terms = (gu, gu * gu, c_g, c_g * gu)
                    sums = [a + jnp.sum(b, axis=-1, keepdims=True) for a, b in zip(sums, terms)]
                mu_g = sums[0] / full_ff
                rs_g = lax.rsqrt(sums[1] / full_ff - mu_g * mu_g + EPSILON)
                m1 = sums[2] / full_ff
                m2 = (sums[3] - mu_g * sums[2]) * rs_g / full_ff
                y = hid
                dhn = jnp.zeros((chunk, width), F32)
                for r, w in enumerate(ws):
                    gf = gf_r[r : r + 1, :]
                    ghat = (gu_s[r] - mu_g) * rs_g
                    dgn = dgn_s[r]
                    gn = (ghat * gf).astype(BF)
                    du = (rs_g * (dgn * gf - m1 - ghat * m2) * slope_s[r]).astype(BF)
                    gn_o[slot[r], span, :] = gn
                    du_o[slot[r], span, :] = du
                    vf_o[r : r + 1, :] += jnp.sum(dgn * ghat, axis=0, keepdims=True)
                    y = y + dot(gn, w[cols + width :, :])
                    dhn = dhn + dot_nt(du, w[cols : cols + width, :])
                y_o[span, :] = y.astype(BF)
                v2_o[...] += jnp.sum(dhn * xhat2, axis=0, keepdims=True)
                c2 = dhn * g2
                dh = dy_c.astype(F32) + rs2 * (
                    c2
                    - jnp.mean(c2, axis=-1, keepdims=True)
                    - xhat2 * jnp.mean(c2 * xhat2, axis=-1, keepdims=True)
                )
                dh_o[span, :] = dh
                dhb_o[span, :] = dh.astype(BF)
            for k in (0, 1, 2, 3, 4, 5, 10):
                done(k)
            dan = dot_nt(w_out_s[...], dhb_o[...])
            column = jnp.sum(dan * ahat, axis=-1, keepdims=True)
            va_o[...] = jnp.broadcast_to(column, (width, 128)).T[:1]
            c_a = dan * ga
            dao = rs_a * (
                c_a
                - jnp.mean(c_a, axis=0, keepdims=True)
                - ahat * jnp.mean(c_a * ahat, axis=0, keepdims=True)
            )
            for r, o in enumerate((dao0, dao1, dao2, dao3)):
                o[...] = dao[r * cols : (r + 1) * cols].astype(BF)

        y_rows, an_t, dhb, hn2, gn, du, *dao_low, dh, v_attn, v_ffn, v_ln2 = call(
            row_kernel,
            [
                ("s", s_ref),
                ("h", x_in),
                *[("l", a) for a in ao_rows],
                ("l", w_own),
                ("l", w_core),
                ("l", dy_own),
                ("v", gain_attn),
                ("v", gain_ffn),
                ("v", g2_row),
                *[("r", w) for w in (*w_side, *w_diag)],
            ],
            [
                ("h", shaped((quarter, width), BF)),
                ("h", shaped((width, quarter), BF)),
                ("h", shaped((quarter, width), BF)),
                ("h", shaped((quarter, width), BF)),
                ("h", shaped((n_head, quarter, ff_part), BF)),
                ("h", shaped((n_head, quarter, ff_part), BF)),
                *[("v", shaped((cols, quarter), BF))] * n_head,
                ("h", shaped((quarter, width), F32)),
                ("v", shaped((1, width), F32)),
                ("v", shaped((n_head, ff_part), F32)),
                ("v", shaped((1, width), F32)),
            ],
            scratch=[
                pltpu.VMEM((n_head, chunk, ff_part), F32),
                pltpu.VMEM((n_head, chunk, ff_part), F32),
                pltpu.VMEM((n_head, chunk, ff_part), F32),
                pltpu.VMEM((width, width), BF),
                pltpu.VMEM((quarter, width), F32),
                pltpu.VMEM((w_rows, width), BF),
                pltpu.VMEM((w_rows, width), BF),
                pltpu.SemaphoreType.DMA((4 * PIECES,)),
            ],
            margin=14,
            name="rows",
        )
        output = y_rows[None]
        dao_blocks = exchange(dao_low)


        def weights_kernel(
            need, done, gn_r, dy_r, hn_r, du_r, an_r, dhb_r, send_o, own_o, side_o, send_i, keep_i
        ):
            need(1)
            for n, o in enumerate((send_o.at[0], send_o.at[1], own_o, side_o)):
                need(0, n)
                o[...] = dot_tn(gn_r[n], dy_r[...]).astype(BF)
                done(*((0, n) if n < 2 else (n - 1, 0)))
            for i in (2, 4, 5):
                need(i)
            for n, r in enumerate(order):
                need(3, n)
                o = send_i if n < 2 else keep_i
                o[n % 2, :width] = dot_tn(hn_r[...], du_r[n]).astype(BF)
                rows = an_r[r * cols : (r + 1) * cols, :]
                o[n % 2, width:] = dot(rows, dhb_r[...]).astype(BF)
                done(3 + n // 2, n % 2)

        one = ("h", shaped((ff_part, width), BF))
        two = ("b", shaped((2, width + cols, width), BF))
        ffo_send, ffo_own, ffo_side, in_send, in_keep = call(
            weights_kernel,
            [("b", gn), ("l", dy_own), ("l", hn2), ("b", du), ("l", an_t), ("l", dhb)],
            [("b", shaped((2, ff_part, width), BF)), one, one, two, two],
            name="weight_gradients",
        )

        def plus(*terms):
            return sum(t.astype(F32) for t in terms).astype(BF)

        class Half:
            def __init__(self, terms, bit):
                self.terms = [t if isinstance(t, tuple) else (t, None) for t in terms]
                self.bit = bit
                self.size = self.terms[0][0].shape[-2] // 2

            def shapes(self):
                return [("v", shaped((self.size, width), BF))] * 2

            def buffers(self):
                return 2 * len(self.terms)

            def start(self, index, ins, outs, bufs, begin):
                upper = (index // self.bit) % 2
                for n, (_, lead) in enumerate(self.terms):
                    ref = ins[n] if lead is None else ins[n].at[lead]
                    for m, at in enumerate(((1 - upper) * self.size, upper * self.size)):
                        begin(ref.at[pl.ds(pl.multiple_of(at, 8), self.size)], bufs[2 * n + m])

            def plain(self):
                found = []
                upper = (s // self.bit) % 2
                for at in ((1 - upper) * self.size, upper * self.size):
                    parts = [t if lead is None else t[lead] for t, lead in self.terms]
                    parts = [lax.dynamic_slice_in_dim(t, at, self.size, 0) for t in parts]
                    found.append(plus(*parts))
                return found

            def finish(self, outs, bufs):
                for m in range(2):
                    parts = [bufs[2 * n + m][...].astype(F32) for n in range(len(self.terms))]
                    outs[m][...] = sum(parts[1:], parts[0]).astype(BF)

        class Joined:
            def __init__(self, own, got, bit):
                self.terms = [(own, None), (got, None)]
                self.bit = bit
                self.size = own.shape[0]

            def shapes(self):
                return [("v", shaped((2 * self.size, width), BF))]

            def buffers(self):
                return 0

            def start(self, index, ins, outs, bufs, begin):
                upper = (index // self.bit) % 2
                for ref, at in zip(ins, (upper * self.size, (1 - upper) * self.size)):
                    begin(ref, outs[0].at[pl.ds(pl.multiple_of(at, 8), self.size)])

            def plain(self):
                own, got = [t for t, _ in self.terms]
                upper = (s // self.bit) % 2 == 1
                return [
                    jnp.where(upper, jnp.concatenate([got, own], 0), jnp.concatenate([own, got], 0))
                ]

            def finish(self, outs, bufs):
                pass

        def combine(jobs):
            made = combine_tiles([job for job in jobs if job.size % 8 == 0])
            return [made.pop(0) if job.size % 8 == 0 else job.plain() for job in jobs]

        def combine_tiles(jobs):
            if not jobs:
                return []
            n_in = [len(job.terms) for job in jobs]
            n_out = [len(job.shapes()) for job in jobs]
            n_buf = [job.buffers() for job in jobs]
            total = sum(max(job.buffers(), len(job.terms)) for job in jobs)

            def kernel(need, done, s_r, *refs):
                index = s_r[0]
                ins = refs[: sum(n_in)]
                outs = refs[sum(n_in) : sum(n_in) + sum(n_out)]
                bufs = refs[sum(n_in) + sum(n_out) : -1]
                semaphores = refs[-1]
                found = []

                def begin(source, target):
                    copy = pltpu.make_async_copy(source, target, semaphores.at[len(found)])
                    copy.start()
                    found.append(copy)

                work = []
                a = b = c = 0
                for n, job in enumerate(jobs):
                    mine = (outs[b : b + n_out[n]], bufs[c : c + n_buf[n]])
                    before = len(found)
                    job.start(index, ins[a : a + n_in[n]], *mine, begin)
                    work.append((job, mine, found[before:]))
                    a, b, c = a + n_in[n], b + n_out[n], c + n_buf[n]
                for job, mine, copies in work:
                    for copy in copies:
                        copy.wait()
                    job.finish(*mine)

            results = call(
                kernel,
                [("s", s_ref), *[("a", t) for job in jobs for t, _ in job.terms]],
                [o for job in jobs for o in job.shapes()],
                scratch=[
                    *[
                        pltpu.VMEM((job.size, width), BF)
                        for job in jobs
                        for _ in range(job.buffers())
                    ],
                    pltpu.SemaphoreType.DMA((total,)),
                ],
                name="combine",
            )
            found = []
            at = 0
            for n in n_out:
                found.append(results[at : at + n])
                at += n
            return found

        n_note = 3 * heads
        note_rows = (3 * n_note + 15) // 16 * 16

        def prepare_kernel(
            need, done, h_s, d0, d1, d2, d3, ao_r, q_r, l_r, start_r, do_o, delta_o, sent_o, ddil_o, dt_s
        ):
            hv = h_s[0]
            for r, d in enumerate((d0, d1, d2, d3)):
                need(1 + r)
                base = pl.multiple_of((hv ^ r) * quarter, quarter)
                dt_s[:, pl.ds(base, quarter)] = d[...]
            dao_v = dt_s[...].astype(F32)
            grown = jnp.concatenate([dao_v, jnp.zeros((LANES - cols, tokens), F32)], 0)
            do_o[...] = grown.T.astype(BF)
            need(5)
            prod = dao_v * ao_r[...]
            sent_o[:cols, :] = q_r[...]
            for l in range(heads):
                sel = spread(hv, l)
                at = cols + l * HEAD_SIZE
                sent_o[at : at + HEAD_SIZE, :] = dot_nt(dt_s[of_head(l), :], sel).astype(BF)
                delta = jnp.sum(prod[of_head(l)], axis=0, keepdims=True)
                delta_o[l : l + 1, :] = delta
                d8 = jnp.broadcast_to(delta, (8, tokens))
                ddil_o[l : l + 1, :] = sum(dot_nt(t, sel) for t in thirds(d8))[:1]
            found = [l_r[l : l + 1, :] for l in range(heads)]
            found += [ddil_o[l : l + 1, :] for l in range(heads)]
            found += [start_r[l : l + 1, :].astype(F32) for l in range(heads)]
            row = iota((note_rows, rows_dil), 0)
            notes = jnp.zeros((note_rows, rows_dil), F32)
            for n, value in enumerate(found):
                for t, piece in enumerate(thirds(value)):
                    notes = jnp.where(row == t * n_note + n, piece.astype(F32), notes)
            sent_o[2 * cols :, :] = notes.astype(BF)

        do_a, delta_all, far_note, delta_dil = call(
            prepare_kernel,
            [
                ("s", h_ref),
                ("m", fence(dao_blocks[0], ffo_send, in_send)),
                *[("m", d) for d in dao_blocks[1:]],
                ("l", ao_t),
                ("v", dil_q),
                ("v", l_dil),
                ("v", start_dil),
            ],
            [
                ("p", shaped((tokens, LANES), BF)),
                ("v", shaped((heads, tokens), F32)),
                ("v", shaped((2 * cols + note_rows, rows_dil), BF)),
                ("v", shaped((heads, rows_dil), F32)),
            ],
            scratch=[pltpu.VMEM((cols, tokens), BF)],
            name="prepare_backward",
        )

        def near_back_kernel(part, need, done, q_r, k_r, v_r, kt_r, do_r, l_r, d_r, *rest):
            dq_o, dk_o, dv_o, token_o = rest[-4:]
            fresh = len(rest) == 4
            token_o[...] = jnp.zeros((8, 128), F32)
            for n, i in enumerate(reversed(part)):
                span = slice(i * BLOCK, (i + 1) * BLOCK)
                q_i = stack_heads(q_r[span, :])
                do_i = stack_heads(do_r[span, :])
                lse_i = jnp.concatenate([l_r[l : l + 1, span] for l in range(heads)], 1)
                del_i = jnp.concatenate([d_r[l : l + 1, span] for l in range(heads)], 1)
                dq_i = [None] * heads
                for j in range(i + 1):
                    keys = slice(j * BLOCK, (j + 1) * BLOCK)
                    pr = jnp.exp(dot_nt(k_r[keys, :], q_i) - lse_i)
                    if j == i:
                        pr = jnp.where(causal_block(), pr, 0.0)
                    dp = dot_nt(v_r[keys, :], do_i)
                    ds = (pr * (dp - del_i)).astype(BF)
                    dv = dot(pr.astype(BF), do_i)
                    dk = dot(ds, q_i)
                    if fresh and n == 0:
                        dv_o[keys, :] = dv
                        dk_o[keys, :] = dk
                    else:
                        dv_o[keys, :] += dv
                        dk_o[keys, :] += dk
                    for l in range(heads):
                        add = dot(kt_r[of_head(l), keys], ds[:, l * BLOCK : (l + 1) * BLOCK])
                        dq_i[l] = add if dq_i[l] is None else dq_i[l] + add
                for l in range(heads):
                    dq_o[of_head(l), span] = dq_i[l]

        grown_to = []

        def back_work(part):
            def work(value, *after):
                after = [value, *after]
                if part is parts[0]:
                    in_y = fence(flying["in_y"], value)
                    flying["in_got"] = swap(in_y, "seq", rising[0])
                    after += [flying["ffo_x"], in_y]
                held = [("p", a) for a in grown_to]
                *grown_to[:], token = call(
                    lambda *refs: near_back_kernel(part, *refs),
                    [
                        ("p", q_a),
                        ("p", k_a),
                        ("p", v_a),
                        ("p", k_t),
                        ("p", do_a),
                        ("v", l_all),
                        ("v", delta_all),
                        *held,
                    ],
                    [
                        ("p", shaped((cols, tokens), F32)),
                        ("p", shaped((tokens, LANES), F32)),
                        ("p", shaped((tokens, LANES), F32)),
                        ("v", shaped((8, 128), F32)),
                    ],
                    name="near_backward",
                    margin=20,
                    aliases={7 + n: n for n in range(len(held))},
                    after=after,
                )
                return None, token

            return work

        ffo_send, in_send, _ = lax.optimization_barrier((ffo_send, in_send, far_note))
        ffo_core = swap(ffo_send, "head", 1)
        in_core = swap(in_send, "head", 1)
        flying = {}

        def start_sums(value):
            flying["ffo_x"] = plus(ffo_side, ffo_core[1])
            upper = (s & rising[0]) != 0
            size = (width + cols) // 2
            away = jnp.where(upper, 0, size)
            flying["in_y"], flying["in_own"] = [
                plus(*[lax.dynamic_slice_in_dim(t, at, size, 1) for t in (in_keep, in_core)])
                for at in (away, size - away)
            ]
            flying["ffo_got"] = swap(flying["ffo_x"], "head", 2)
            return None, delta_dil

        far_q, _, tokens_back = gather_seq(
            far_note, [start_sums, *[back_work(part) for part in parts]], "v"
        )
        dq_near, dk_near, dv_near = grown_to
        ffo_got, in_got, *tokens_back = lax.optimization_barrier(
            (flying["ffo_got"], flying["in_got"], *tokens_back)
        )
        (ffo_z, ffo_kept), _ = combine([Half([ffo_own, (ffo_core, 0), ffo_got], rising[1])]) + [None]
        in_x = plus(in_got[1], flying["in_own"][1])
        ffo_z_got = swap(ffo_z, "seq", rising[1])
        in_x_got = swap(in_x, "head", 2)

        def far_back_kernel(need, done, *refs):
            p_s, kv_r, fq_r, start_r, l_r, d_r = refs[:6]
            dqn_r, dkn_r, dvn_r, w_r, x_r, g_r, send_o, keep_o, away_o, stay_o, v_o, d_o, dq_s, dk_s, dv_s = refs[6:]
            hv = p_s[0]
            sv = p_s[1]

            def rows_of(ref, b, first):
                return turned(ref[b, first : first + cols]).astype(BF)

            q_v = stack_dil(rows_of(fq_r, 0, 0))
            do_v = stack_dil(rows_of(fq_r, 0, cols))
            k_own = rows_of(kv_r, 0, 0)
            v_own = rows_of(kv_r, 0, cols)
            start_v = start_r[...]
            l_v = jnp.concatenate([l_r[l : l + 1, :] for l in range(heads)], 1)
            d_v = jnp.concatenate([d_r[l : l + 1, :] for l in range(heads)], 1)
            dq_s[...] = jnp.zeros_like(dq_s)
            dk_s[...] = jnp.zeros_like(dk_s)
            dv_s[...] = jnp.zeros_like(dv_s)

            @pl.loop(0, n_far)
            def _(b):
                owner = p_s[2 + b]

                @pl.when(owner <= sv)
                def _():
                    key, query = far_place(p_s, owner, sv)
                    keep = (key <= query) & (key >= start_v)
                    sc = dot_nt(rows_of(kv_r, b, 0), q_v)
                    pr = jnp.where(keep, jnp.exp(sc - l_v), 0.0)
                    dp = dot_nt(rows_of(kv_r, b, cols), do_v)
                    ds = (pr * (dp - d_v)).astype(BF)
                    for l in range(heads):
                        cut = slice(l * rows_dil, (l + 1) * rows_dil)
                        dq_s[of_head(l), :] += dot(kv_r[b, of_head(l)], ds[:, cut])

                @pl.when(owner >= sv)
                def _():
                    note = fq_r[b, 2 * cols :].astype(F32)

                    def row(kind):
                        found = []
                        for l in range(heads):
                            at = kind * heads + l
                            found.append(
                                sum(note[at + t * n_note : at + t * n_note + 1] for t in range(3))
                            )
                        return jnp.concatenate(found, 1)

                    key, query = far_place(p_s, sv, owner)
                    keep = (key <= query) & (key >= row(2).astype(jnp.int32))
                    q_b = stack_dil(rows_of(fq_r, b, 0))
                    do_b = stack_dil(rows_of(fq_r, b, cols))
                    sc = dot_nt(k_own, q_b)
                    pr = jnp.where(keep, jnp.exp(sc - row(0)), 0.0)
                    dp = dot_nt(v_own, do_b)
                    ds = (pr * (dp - row(1))).astype(BF)
                    dk_s[...] += dot(ds, q_b)
                    dv_s[...] += dot(pr.astype(BF), do_b)

            dk_t = turned(dk_s[...])
            dv_t = turned(dv_s[...])

            def placed(value, l):
                high, low = halves(value[of_head(l)])
                put = spread(hv, l)
                return dot(high, put) + dot(low, put)

            dk_near = dkn_r[...].T
            dv_near = dvn_r[...].T
            scale = HEAD_SIZE**-0.5
            dq_far = dq_s[...]
            for l in range(heads):
                rows = of_head(l)
                d_o[rows, :] = ((dqn_r[rows, :] + placed(dq_far, l)) * scale).astype(BF)
                at = cols + l * HEAD_SIZE
                d_o[at : at + HEAD_SIZE, :] = (dk_near[rows] + placed(dk_t, l)).astype(BF)
                at += cols
                d_o[at : at + HEAD_SIZE, :] = (dv_near[rows] + placed(dv_t, l)).astype(BF)
            for o, n, r in ((send_o, 0, 3), (send_o, 1, 1), (keep_o, 0, 2), (keep_o, 1, 0)):
                base = pl.multiple_of((hv ^ r) * quarter, quarter)
                o[n] = dot_tn(d_o[:, pl.ds(base, quarter)], w_r[...]).astype(o.dtype)
            need(10)
            part = dot(d_o[...], x_r[...])
            half = 3 * cols // 2
            for upper in (0, 1):

                @pl.when(lax.rem(sv, 2) == upper)
                def _():
                    away_o[...] = part[(1 - upper) * half : (2 - upper) * half].astype(BF)
                    stay_o[...] = part[upper * half : (1 + upper) * half].astype(BF)

            v_o[...] = jnp.sum(part * w_r[...].astype(F32), axis=0, keepdims=True) / g_r[...]

        dxn_send, dxn_keep, qkv_away, qkv_stay, v_ln1 = call(
            far_back_kernel,
            [
                ("s", place),
                ("h", far_kv),
                ("v", far_q),
                ("v", start_row),
                ("v", l_dil),
                ("v", delta_dil),
                ("p", dq_near),
                ("p", dk_near),
                ("p", dv_near),
                ("v", w_turn),
                ("l", x_all),
                ("v", g1_row),
            ],
            [
                ("v", shaped((2, quarter, width), BF)),
                ("v", shaped((2, quarter, width), F32)),
                ("v", shaped((3 * cols // 2, width), BF)),
                ("v", shaped((3 * cols // 2, width), BF)),
                ("v", shaped((1, width), F32)),
            ],
            scratch=[
                pltpu.VMEM((3 * cols, tokens), BF),
                pltpu.VMEM((cols, rows_dil), F32),
                pltpu.VMEM((rows_dil, cols), F32),
                pltpu.VMEM((rows_dil, cols), F32),
            ],
            margin=12,
            name="far_backward",
            after=(ffo_z, in_x, *tokens_back),
        )

        dxn_send, ffo_z_got, in_x_got = lax.optimization_barrier((dxn_send, ffo_z_got, in_x_got))

        def sum_rows():
            got = yield dxn_send, "head", 1, 1
            side = (dxn_keep[0] + got[0].astype(F32)).astype(BF)
            over_x = yield side, "head", 2, 3

            def last_kernel(need, done, x_r, g_r, keep_r, got_r, over_r, dh_r, o):
                xhat, rs = normed(x_r[...].astype(F32))
                dxn = keep_r[1] + got_r[1].astype(F32) + over_r[...].astype(F32)
                c = dxn * g_r[...]
                first = jnp.mean(c, axis=-1, keepdims=True)
                second = jnp.mean(c * xhat, axis=-1, keepdims=True)
                o[...] = dh_r[...] + rs * (c - first - xhat * second)

            (result,) = call(
                last_kernel,
                [("v", x_in), ("v", g1_row), ("v", dxn_keep), ("v", got), ("v", over_x), ("v", dh)],
                [("v", shaped((quarter, width), F32))],
                margin=12,
                name="first_norm_backward",
            )
            return result

        def sum_seq(terms, scatter, spread, last=1):
            for bit in scatter:
                send, kept = yield Half(terms, bit)
                terms = [kept, (yield send, "seq", bit, 1)]
            value = None
            for bit in spread:
                if value is None:
                    value = plus(*terms)
                rounds = last if bit == spread[-1] else 1
                got = yield value, "seq", bit, rounds
                (value,) = yield Joined(value, got, bit)
            return value

        def sum_ffo():
            bits = rising[2:] + rising[:1]
            terms = [ffo_kept, ffo_z_got]
            value = yield from sum_seq(terms, bits, bits[::-1] + rising[1:2])
            return value.astype(F32)

        def sum_in():
            terms = [(in_got, 0), (flying["in_own"], 0), in_x_got]
            value = yield from sum_seq(terms, rising[1:], rising[::-1])
            return value[:width].astype(F32), value[width:].astype(F32)

        def sum_qkv():
            got = yield qkv_away, "seq", rising[0], 1
            return (yield from sum_seq([qkv_stay, got], rising[1:], rising[::-1]))

        def sum_small():
            v_rel = jnp.concatenate([v_attn.reshape(n_head, cols), v_ffn], 1)
            size = v_rel.shape[1]
            common = jnp.concatenate([v_ln1.reshape(-1), v_ln2.reshape(-1), lse_sums[:2].reshape(-1)])
            got = yield jnp.concatenate([v_rel[1], v_rel[3], common]), "head", 1, 1
            mine = v_rel[0] + got[:size]
            other = v_rel[2] + got[size : 2 * size]
            common = common + got[2 * size :]
            got = yield jnp.concatenate([other, common]), "head", 2, 1
            small = jnp.concatenate([mine, common]) + got
            for bit in rising:
                small = small + (yield small, "seq", bit, 1)
            total_heads = heads * n_head
            counts = jnp.array([tokens * n_seq * total_heads, rows_dil * n_seq * total_heads], F32)
            means = jnp.sum(small[size + 2 * width :].reshape(2, 128), axis=1) / counts
            return (
                small[:cols],
                small[cols:size],
                small[size : size + width],
                small[size + width : size + 2 * width],
                means,
            )

        def in_rounds(chains):
            results = [None] * len(chains)
            large = (1, 2, 3)
            asks = {}
            flying = {}
            ended = []

            def resume(n, value):
                try:
                    asks[n] = chains[n].send(value)
                except StopIteration as stop:
                    results[n] = stop.value
                    ended.append(n)

            def settle():
                jobs = [n for n in asks if not isinstance(asks[n], tuple)]
                if jobs:
                    for n, made in zip(jobs, combine([asks.pop(n) for n in jobs])):
                        resume(n, made)

            for n in range(len(chains)):
                resume(n, None)
            number = 0
            while asks or flying:
                settle()
                for n in list(asks)[::-1] if number == 0 else list(asks):
                    value, axis, bit, rounds = asks.pop(n)
                    flying[n] = (number + rounds - 1, swap(value, axis, bit))
                due = [n for n in flying if flying[n][0] <= number]
                held = tuple(flying.pop(n)[1] for n in due)
                flat, tree = jax.tree.flatten((held, [results[n] for n in ended]))
                held, again = jax.tree.unflatten(tree, lax.optimization_barrier(tuple(flat)))
                for n, value in zip(ended, again):
                    results[n] = value
                for n, got in zip(due, held):
                    if n in large:
                        resume(n, got)
                settle()
                sent = [asks[n][0] for n in large if n in asks]
                for n, got in zip(due, held):
                    if n not in large:
                        resume(n, fence(got, sent[0]) if sent else got)
                number += 1
            return results

        dx, g_ffo, (g_in, g_out), g_qkv, (g_sub_attn, g_sub_ffn, g_ln1, g_ln2, means) = in_rounds(
            [sum_rows(), sum_ffo(), sum_in(), sum_qkv(), sum_small()]
        )
        g_qkv = g_qkv.astype(F32).reshape(3, cols, width).transpose(0, 2, 1)
        return (
            output,
            dx[None],
            g_ln1,
            g_qkv,
            g_sub_attn,
            g_out,
            g_ln2,
            g_in,
            g_sub_ffn,
            g_ffo,
            means,
        )

    return jax.shard_map(
        body,
        mesh=mesh,
        in_specs=(
            P("head", "seq", None),
            P("seq"),
            P(),
            P(None, None, "head"),
            P("head"),
            P("head", None),
            P(),
            P(None, "head"),
            P("head"),
            P("head", None),
            P("seq", None),
        ),
        out_specs=(
            P("head", "seq", None),
            P("head", "seq", None),
            P(),
            P(None, None, "head"),
            P("head"),
            P("head", None),
            P(),
            P(None, "head"),
            P("head"),
            P("head", None),
            P(),
        ),
        check_vma=False,
    )
```

```python
import math

import jax
import jax.numpy as jnp
from jax import lax
from jax.experimental import pallas as pl
from jax.experimental.pallas import tpu as pltpu
from jax.sharding import PartitionSpec as P

HEAD_SIZE = 64
DILATION_RATE = 16
EPSILON = 1e-05
NEGATIVE = -1e30
APART = -(2.0**30)
DOC_MIN = 256
GAUSS_NORM = 1.0 / math.sqrt(2.0 * math.pi)
BLOCK = 256
LANES = 256
BF = jnp.bfloat16
F32 = jnp.float32
ERF_P = 0.3275911
ERF_C = (0.254829592, -0.284496736, 1.421413741, -1.453152027, 1.061405429)
SPLIT = 3
PIECES = 2
CHUNK = 256


def dot(a, b):
    return lax.dot_general(a, b, (((1,), (0,)), ((), ())), preferred_element_type=F32)


def dot_nt(a, b):
    return lax.dot_general(a, b, (((1,), (1,)), ((), ())), preferred_element_type=F32)


def dot_tn(a, b):
    return lax.dot_general(a, b, (((0,), (0,)), ((), ())), preferred_element_type=F32)


def iota(shape, axis):
    return lax.broadcasted_iota(jnp.int32, shape, axis)


def halves(value):
    high = value.astype(BF)
    return high, (value - high.astype(F32)).astype(BF)


def thirds(value):
    high = value.astype(BF)
    rest = value - high.astype(F32)
    middle = rest.astype(BF)
    return high, middle, (rest - middle.astype(F32)).astype(BF)


def fence(value, *before):
    return lax.optimization_barrier((value, *before))[0]


def turned(value):
    return value.astype(F32).T


def room(shape, dtype):
    shape = (1,) * (2 - len(shape)) + tuple(shape)
    size = jnp.dtype(dtype).itemsize
    lanes = (shape[-1] + 127) // 128 * 128
    rows = (shape[-2] + 15) // 16 * 16
    return math.prod(shape[:-2]) * rows * lanes * size


def call(kernel, ins, outs, scratch=(), margin=8, name=None, aliases=None, after=()):
    n_in, n_out, n_after = len(ins), len(outs), len(after)
    spaces = {"s": pltpu.SMEM, "v": pltpu.VMEM, "p": pltpu.VMEM, "a": pl.ANY, "r": pltpu.HBM}
    far_in = [i for i, (kind, _) in enumerate(ins) if kind not in spaces]
    far_out = [i for i, (kind, _) in enumerate(outs) if kind not in spaces]
    n_far = len(far_in) + len(far_out)
    far = [ins[i] for i in far_in] + [outs[i] for i in far_out]
    buffers = [pltpu.VMEM(a.shape, a.dtype) for _, a in far]
    counts = [a.shape[0] if kind == "b" else 1 for kind, a in far]

    def wrapped(*refs):
        refs = (*refs[:n_in], *refs[n_in + n_after :])
        given, results, rest = list(refs[:n_in]), list(refs[n_in : n_in + n_out]), refs[n_in + n_out :]
        arriving, leaving, started = {}, {}, []

        def copies(kind, n, source, target):
            semaphores = rest[n_far]
            first = sum(counts[:n])
            if kind != "b":
                return {0: pltpu.make_async_copy(source, target, semaphores.at[first])}
            return {
                m: pltpu.make_async_copy(source.at[m], target.at[m], semaphores.at[first + m])
                for m in range(counts[n])
            }

        for n, i in enumerate(far_in):
            arriving[i] = copies(ins[i][0], n, given[i], rest[n])
            for copy in arriving[i].values():
                copy.start()
            given[i] = rest[n]
        for n, i in enumerate(far_out, len(far_in)):
            leaving[i] = copies(outs[i][0], n, rest[n], results[i])
            results[i] = rest[n]

        def need(i, m=0):
            arriving[i].pop(m).wait()

        def done(i, m=0):
            copy = leaving[i].pop(m)
            copy.start()
            started.append(copy)

        for i in far_in:
            if ins[i][0] == "h":
                need(i)
        own = rest[n_far + 1 :] if n_far else rest
        kernel(need, done, *given, *results, *own)
        for i in far_in:
            for m in list(arriving[i]):
                need(i, m)
        for i in far_out:
            for m in list(leaving[i]):
                done(i, m)
        for copy in started:
            copy.wait()

    held = [(a.shape, a.dtype) for kind, a in ins if kind not in "spar"]
    held += [(a.shape, a.dtype) for kind, a in outs if kind != "p"]
    held += [(a.shape, a.dtype) for a in scratch if jnp.issubdtype(a.dtype, jnp.number)]
    limit = sum(room(*a) for a in held) + (margin << 20)

    def placed(kind, a):
        if kind in "svam":
            return a
        return pltpu.with_memory_space_constraint(a, spaces.get(kind, pltpu.HBM))

    def shape_of(kind, a):
        if kind == "v":
            return a
        return spaces.get(kind, pltpu.HBM)(a.shape, a.dtype)

    return pl.pallas_call(
        wrapped,
        out_shape=tuple(shape_of(*o) for o in outs),
        in_specs=[
            pl.BlockSpec(memory_space=pl.ANY if kind == "m" else spaces.get(kind, pltpu.HBM))
            for kind, _ in ins
        ]
        + [pl.BlockSpec(memory_space=pl.ANY)] * n_after,
        out_specs=tuple(pl.BlockSpec(memory_space=spaces.get(kind, pltpu.HBM)) for kind, _ in outs),
        scratch_shapes=[
            *buffers,
            *([pltpu.SemaphoreType.DMA((sum(counts),))] if n_far else []),
            *scratch,
        ],
        input_output_aliases=aliases or {},
        compiler_params=pltpu.CompilerParams(vmem_limit_bytes=limit),
        cost_estimate=pl.CostEstimate(flops=0, transcendentals=0, bytes_accessed=0),
        name=name,
    )(*[placed(*a) for a in ins], *after)


def solution(mesh):
    n_head = mesh.shape["head"]
    n_seq = mesh.shape["seq"]

    def swap(value, axis, bit):
        size = n_head if axis == "head" else n_seq
        return lax.ppermute(value, axis, [(i, i ^ bit) for i in range(size)])

    rising = []
    bit = 1
    while bit < n_seq:
        rising.append(bit)
        bit *= 2
    seq_bits = rising[:1] + rising[:0:-1]

    offsets = [0]
    for bit in seq_bits:
        offsets = offsets + [o ^ bit for o in offsets]

    def body(
        layer_input,
        document_start,
        ln1_gain,
        w_qkv,
        sub_gain_attn,
        w_out,
        ln2_gain,
        w_in,
        sub_gain_ffn,
        w_ffo,
        dy,
    ):
        tokens, width = dy.shape
        quarter = layer_input.shape[1]
        cols = w_qkv.shape[2]
        heads = cols // HEAD_SIZE
        rows_dil = tokens // DILATION_RATE
        ff_part = w_in.shape[1]
        n_blocks = tokens // BLOCK
        n_far = n_seq
        h = lax.axis_index("head")
        s = lax.axis_index("seq")
        h_ref = jnp.reshape(h, (1,)).astype(jnp.int32)
        s_ref = jnp.reshape(s, (1,)).astype(jnp.int32)
        far_index = (s ^ jnp.array(offsets, jnp.int32)).astype(jnp.int32)
        place = jnp.concatenate([jnp.stack([h, s]).astype(jnp.int32), far_index])
        shaped = jax.ShapeDtypeStruct

        parts = [[] for _ in range(SPLIT)]
        for i in reversed(range(n_blocks)):
            min(parts, key=lambda part: sum(k + 1 for k in part)).append(i)
        parts = [sorted(part) for part in parts if part]
        n_parts = len(parts)
        home = {i: (p, n) for p, part in enumerate(parts) for n, i in enumerate(part)}

        def stacked(value, got, kind):
            size = value.shape[0]

            def stack_kernel(need, done, v_r, g_r, o_r, semaphores):
                copies = [
                    pltpu.make_async_copy(v_r, o_r.at[:size], semaphores.at[0]),
                    pltpu.make_async_copy(g_r, o_r.at[size:], semaphores.at[1]),
                ]
                for copy in copies:
                    copy.start()
                for copy in copies:
                    copy.wait()

            return call(
                stack_kernel,
                [("a", value), ("a", got)],
                [(kind, shaped((2 * size, *value.shape[1:]), value.dtype))],
                scratch=[pltpu.SemaphoreType.DMA((2,))],
                name="stack",
            )[0]

        def gather_seq(value, works, kind):
            value = value[None]
            results = []
            tokens = ()
            for n in range(max(len(seq_bits), len(works))):
                got = swap(value, "seq", seq_bits[n]) if n < len(seq_bits) else None
                if n < len(works):
                    result, token = works[n](value, *tokens)
                    results.append(result)
                    tokens = (token,)
                    if got is not None:
                        got, *tokens = lax.optimization_barrier((got, token))
                if got is not None:
                    value = stacked(value, got, kind if n == len(seq_bits) - 1 else "v")
            return value, results, tokens

        x_in = layer_input[0]

        def normed(value):
            mu = jnp.mean(value, axis=-1, keepdims=True)
            centred = value - mu
            rs = lax.rsqrt(jnp.mean(centred * centred, axis=-1, keepdims=True) + EPSILON)
            return centred * rs, rs

        def norm_kernel(need, done, x_r, g_r, o):
            o[...] = (normed(x_r[...].astype(F32))[0] * g_r[...]).astype(BF)

        g1_row = ln1_gain.reshape(1, -1)
        (xn,) = call(
            norm_kernel,
            [("h", x_in), ("v", g1_row)],
            [("h", shaped((quarter, width), BF))],
            margin=8,
            name="first_norm",
        )
        xn_core = swap(xn, "head", 1)
        xn_x = swap(xn, "head", 2)

        gain_part = fence(jnp.concatenate([sub_gain_attn, sub_gain_ffn]).reshape(1, -1), xn)
        gain_pair = jnp.concatenate([gain_part, swap(gain_part, "head", 1)], 0)
        gain_rel = jnp.concatenate([gain_pair, swap(gain_pair, "head", 2)], 0)
        gain_attn = gain_rel[:, :cols].reshape(1, width)
        g2_row = ln2_gain.reshape(1, -1)
        gain_ffn = gain_rel[:, cols:]
        w_own = jnp.concatenate([w_out, w_in, w_ffo], 0)
        w_core = swap(w_own, "head", 1)
        dy_own = lax.dynamic_slice_in_dim(dy, h * quarter, quarter, 0)

        seg_begin = s * tokens
        doc = jnp.clip((document_start - seg_begin) // DOC_MIN + 1, 0, tokens // DOC_MIN)
        lane = jnp.arange(LANES, dtype=jnp.int32)[None, :]
        same = lane - cols == doc[:, None]
        feature_lane = lane >= cols
        k_feat = jnp.where(same, 1.0, 0.0).astype(BF)
        q_feat = jnp.where(feature_lane & ~same, APART, 0.0).astype(BF)
        shift = (h * heads + jnp.arange(heads, dtype=jnp.int32)) % DILATION_RATE
        start_grid = document_start.reshape(rows_dil, DILATION_RATE)
        pick = jnp.arange(DILATION_RATE, dtype=jnp.int32)[:, None] == shift[None, :]
        start_dil = jnp.sum(jnp.where(pick[None], start_grid[:, :, None], 0), axis=1).T
        start_row = start_dil.reshape(1, heads * rows_dil)

        w_pad = jnp.pad(w_qkv, ((0, 0), (0, 0), (0, LANES - cols)))
        w_turn = w_qkv.transpose(0, 2, 1).reshape(3 * cols, width)
        w_rows = w_own.shape[0]
        piece = w_rows // (2 * PIECES)
        my_half = (s % 2) * (w_rows // 2)
        w_cut = [
            lax.dynamic_slice_in_dim(w_own, my_half + n * piece, piece, 0) for n in range(PIECES)
        ]
        xn_x = fence(
            xn_x, w_pad, w_turn, q_feat, k_feat, *w_cut, dy_own, start_row, gain_attn, gain_ffn, g2_row
        )
        xn_diag = swap(xn_x, "head", 1)
        w_half = [swap(w, "head", 2) for w in lax.optimization_barrier((*w_cut, xn_x))[:PIECES]]

        def head_shift(h_value, l):
            return lax.rem(h_value * heads + l, DILATION_RATE)

        def spread(h_value, l):
            a = iota((rows_dil, tokens), 0)
            p = iota((rows_dil, tokens), 1)
            return jnp.where(p == a * DILATION_RATE + head_shift(h_value, l), 1.0, 0.0).astype(BF)

        def of_head(l):
            return slice(l * HEAD_SIZE, (l + 1) * HEAD_SIZE)

        def project_kernel(
            need, done, h_s, b0, b1, b2, b3, w_r, qf, kf,
            q_o, k_o, v_o, kt_o, vt_o, x_o, dil_kv, dil_q, qt_s,
        ):
            hv = h_s[0]
            for i in (5, 6, 7):
                need(i)
            for r, b in enumerate((b0, b1, b2, b3)):
                base = pl.multiple_of((hv ^ r) * quarter, quarter)
                span = pl.ds(base, quarter)
                need(1 + r)
                xb = b[...]
                x_o[span, :] = xb
                qv = dot(xb, w_r[0]).astype(BF) * BF(HEAD_SIZE**-0.5)
                q_o[span, :] = qv + qf[span, :]
                kv = dot(xb, w_r[1]).astype(BF)
                k_o[span, :] = kv + kf[span, :]
                vv = dot(xb, w_r[2]).astype(BF)
                v_o[span, :] = vv
                qt_s[:, span] = turned(qv)[:cols].astype(BF)
                kt_o[:, span] = turned(kv)[:cols].astype(BF)
                vt_o[:, span] = turned(vv)[:cols].astype(BF)
            done(5)
            for l in range(heads):
                sel = spread(hv, l)
                dil_q[of_head(l), :] = dot_nt(qt_s[of_head(l), :], sel).astype(BF)
                dil_kv[of_head(l), :] = dot_nt(kt_o[of_head(l), :], sel).astype(BF)
                dil_kv[cols + l * HEAD_SIZE : cols + (l + 1) * HEAD_SIZE, :] = dot_nt(
                    vt_o[of_head(l), :], sel
                ).astype(BF)

        q_a, k_a, v_a, k_t, v_t, x_all, dil_kv, dil_q = call(
            project_kernel,
            [
                ("s", h_ref),
                ("m", xn),
                ("m", xn_core),
                ("m", xn_x),
                ("m", xn_diag),
                ("l", w_pad),
                ("l", q_feat),
                ("l", k_feat),
            ],
            [
                ("p", shaped((tokens, LANES), BF)),
                ("p", shaped((tokens, LANES), BF)),
                ("p", shaped((tokens, LANES), BF)),
                ("p", shaped((cols, tokens), BF)),
                ("v", shaped((cols, tokens), BF)),
                ("h", shaped((tokens, width), BF)),
                ("v", shaped((2 * cols, rows_dil), BF)),
                ("v", shaped((cols, rows_dil), BF)),
            ],
            scratch=[pltpu.VMEM((cols, tokens), BF)],
            name="project",
        )

        def stack_heads(value, size=heads):
            keep = iota(value.shape, 1) // HEAD_SIZE
            zero = jnp.zeros_like(value)
            return jnp.concatenate(
                [jnp.where((keep == l) | (keep >= size), value, zero) for l in range(size)], 0
            )

        wide = heads * BLOCK

        def causal_block():
            return iota((BLOCK, wide), 0) <= iota((BLOCK, wide), 1) % BLOCK

        def near_kernel(part, need, done, q_r, k_r, vt_r, o_o, lse_o):
            for n, i in enumerate(part):
                q_i = stack_heads(q_r[i * BLOCK : (i + 1) * BLOCK, :])
                top = total = None
                outs = None
                for j in [i] + list(range(i)):
                    sc = dot_nt(k_r[j * BLOCK : (j + 1) * BLOCK, :], q_i)
                    if j == i:
                        sc = jnp.where(causal_block(), sc, NEGATIVE)
                    part_top = jnp.max(sc, axis=0, keepdims=True)
                    new_top = part_top if top is None else jnp.maximum(top, part_top)
                    pr = jnp.exp(sc - new_top)
                    part_sum = jnp.sum(pr, axis=0, keepdims=True)
                    pb = pr.astype(BF)
                    fresh = [
                        dot(
                            vt_r[of_head(l), j * BLOCK : (j + 1) * BLOCK],
                            pb[:, l * BLOCK : (l + 1) * BLOCK],
                        )
                        for l in range(heads)
                    ]
                    if top is None:
                        total, outs = part_sum, fresh
                    else:
                        shrink = jnp.exp(top - new_top)
                        total = total * shrink + part_sum
                        outs = [
                            o * shrink[:, l * BLOCK : (l + 1) * BLOCK] + f
                            for l, (o, f) in enumerate(zip(outs, fresh))
                        ]
                    top = new_top
                lse = top + jnp.log(total)
                inv = 1.0 / total
                for l in range(heads):
                    cut = slice(l * BLOCK, (l + 1) * BLOCK)
                    o_o[of_head(l), n * BLOCK : (n + 1) * BLOCK] = outs[l] * inv[:, cut]
                    lse_o[l : l + 1, n * BLOCK : (n + 1) * BLOCK] = lse[:, cut]

        near_lse = []

        def near_work(part):
            def work(*after):
                size = len(part) * BLOCK
                after = [*after, *w_half[len(near_lse) - 1 : len(near_lse)]]
                result = call(
                    lambda *refs: near_kernel(part, *refs),
                    [("p", q_a), ("p", k_a), ("v", v_t)],
                    [("v", shaped((cols, size), F32)), ("v", shaped((heads, size), F32))],
                    name="near_forward",
                    margin=24,
                    after=after,
                )
                near_lse.append(result[1])
                return result, result[1]

            return work

        far_kv, near_out, _ = gather_seq(dil_kv, [near_work(part) for part in parts], "h")
        w_other = [
            swap(fence(w, near_lse[min(n, n_parts - 1)]), "seq", 1) for n, w in enumerate(w_half)
        ]
        near_o = [o for o, _ in near_out]

        def joined(refs, rows):
            pieces = []
            for i in range(n_blocks):
                p, n = home[i]
                pieces.append(refs[p][rows, n * BLOCK : (n + 1) * BLOCK])
            return jnp.concatenate(pieces, 1)

        def stack_dil(value):
            keep = iota(value.shape, 1) // HEAD_SIZE
            zero = jnp.zeros_like(value)
            return jnp.concatenate([jnp.where(keep == l, value, zero) for l in range(heads)], 0)

        far_wide = heads * rows_dil

        def far_place(p_s, key_owner, query_owner):
            col = iota((rows_dil, far_wide), 1)
            off = lax.rem(p_s[0] * heads + col // rows_dil, DILATION_RATE)
            key = key_owner * tokens + iota((rows_dil, far_wide), 0) * DILATION_RATE + off
            query = query_owner * tokens + (col % rows_dil) * DILATION_RATE + off
            return key, query

        def far_kernel(need, done, *refs):
            p_s, q_r, kv_r, start_r = refs[:4]
            o_r = refs[4 : 4 + n_parts]
            lse_r = refs[4 + n_parts : 4 + 2 * n_parts]
            ao_o, l_o, ldil_o, sum_o, *aob, top_s, total_s, out_s, low_s = refs[4 + 2 * n_parts :]
            hv = p_s[0]
            sv = p_s[1]
            q_v = stack_dil(turned(q_r[...]).astype(BF))
            start_v = start_r[...]
            top_s[...] = jnp.full((8, far_wide), NEGATIVE, F32)
            total_s[...] = jnp.zeros((8, far_wide), F32)
            out_s[...] = jnp.zeros((HEAD_SIZE, far_wide), F32)

            @pl.loop(0, n_far)
            def _(b):
                owner = p_s[2 + b]

                @pl.when(owner <= sv)
                def _():
                    top = top_s[:1]
                    sc = dot_nt(turned(kv_r[b, :cols]).astype(BF), q_v)
                    key, query = far_place(p_s, owner, sv)
                    sc = jnp.where((key <= query) & (key >= start_v), sc, NEGATIVE)
                    new_top = jnp.maximum(top, jnp.max(sc, axis=0, keepdims=True))
                    pr = jnp.exp(sc - new_top)
                    shrink = jnp.exp(top - new_top)
                    total_s[:1] = total_s[:1] * shrink + jnp.sum(pr, axis=0, keepdims=True)
                    pb = pr.astype(BF)
                    fresh = jnp.concatenate(
                        [
                            dot(
                                kv_r[b, cols + l * HEAD_SIZE : cols + (l + 1) * HEAD_SIZE],
                                pb[:, l * rows_dil : (l + 1) * rows_dil],
                            )
                            for l in range(heads)
                        ],
                        1,
                    )
                    out_s[...] = out_s[...] * shrink + fresh
                    top_s[:1] = new_top

            sum_o[...] = jnp.zeros((8, 128), F32)
            total = total_s[:1]
            lse_far = top_s[:1] + jnp.log(total)
            out = out_s[...] / total
            for l in range(heads):
                cut = slice(l * rows_dil, (l + 1) * rows_dil)
                rows = of_head(l)
                lf = lse_far[:, cut]
                sum_o[1:2, :] += lf
                put = spread(hv, l)
                l8 = jnp.broadcast_to(lf, (8, rows_dil))
                full_lf = sum(dot(t, put) for t in thirds(l8))[:1]
                high, low = halves(out[:, cut])
                full_o = dot(high, put) + dot(low, put)
                dilated = iota((1, tokens), 1) % DILATION_RATE == head_shift(hv, l)
                ln = joined(lse_r, slice(l, l + 1))
                for part in range(tokens // 128):
                    sum_o[:1, :] += ln[:, part * 128 : (part + 1) * 128]
                peak = jnp.maximum(ln, full_lf)
                both = peak + jnp.log(jnp.exp(ln - peak) + jnp.exp(full_lf - peak))
                tot = jnp.where(dilated, both, ln)
                w_near = jnp.exp(ln - tot)
                w_far = jnp.where(dilated, jnp.exp(full_lf - tot), 0.0)
                ao = joined(o_r, rows) * w_near + full_o * w_far
                ao_o[rows, :] = ao
                low_s[rows, :] = ao.astype(BF)
                l_o[l : l + 1, :] = tot
                t8 = jnp.broadcast_to(tot, (8, tokens))
                ldil_o[l : l + 1, :] = sum(dot_nt(t, put) for t in thirds(t8))[:1]
            for r, o in enumerate(aob):
                base = pl.multiple_of((hv ^ r) * quarter, quarter)
                o[...] = low_s[:, pl.ds(base, quarter)]

        ao_t, l_all, l_dil, lse_sums, *ao_low = call(
            far_kernel,
            [
                ("s", place),
                ("v", dil_q),
                ("h", far_kv),
                ("v", start_row),
                *[("v", o) for o in near_o],
                *[("v", lse) for lse in near_lse],
            ],
            [
                ("h", shaped((cols, tokens), F32)),
                ("h", shaped((heads, tokens), F32)),
                ("h", shaped((heads, rows_dil), F32)),
                ("h", shaped((8, 128), F32)),
                ("h", shaped((cols, quarter), BF)),
                *[("v", shaped((cols, quarter), BF))] * (n_head - 1),
            ],
            scratch=[
                pltpu.VMEM((8, far_wide), F32),
                pltpu.VMEM((8, far_wide), F32),
                pltpu.VMEM((HEAD_SIZE, far_wide), F32),
                pltpu.VMEM((cols, tokens), BF),
            ],
            name="far_forward",
            after=w_other[:1],
        )

        def exchange(pieces):
            return [pieces[0]] + [swap(pieces[r], "head", r) for r in range(1, n_head)]

        ao_rows = exchange(ao_low)
        *w_side, _ = lax.optimization_barrier((*w_half, *w_other, ao_low[0]))
        w_diag = [swap(w, "head", 1) for w in w_side]

        full_ff = ff_part * n_head
        chunk = min(CHUNK, quarter)
        order = (1, 3, 0, 2)
        slot = {r: n for n, r in enumerate(order)}

        def row_kernel(
            need, done, s_r, x_r, a0, a1, a2, a3, w0, w1, dy_r, ga_r, gf_r, g2_r, *refs
        ):
            side, refs = refs[: 4 * PIECES], refs[4 * PIECES :]
            (
            y_o, an_o, dhb_o, hn_o, gn_o, du_o, dao0, dao1, dao2, dao3, dh_o, va_o, vf_o, v2_o,
            gu_s, slope_s, dgn_s, w_out_s, hid_s, w2, w3, semaphores,
            ) = refs
            ws = (w0, w1, w2, w3)
            copies = []
            for n, ref in enumerate(side):
                half = (s_r[0] + n // PIECES) % 2
                at = pl.multiple_of(half * (w_rows // 2) + n % PIECES * piece, 8)
                copy = pltpu.make_async_copy(
                    ref, ws[2 + n // (2 * PIECES)].at[pl.ds(at, piece)], semaphores.at[n]
                )
                copy.start()
                copies.append(copy)
            for i in range(2, 6):
                need(i)
            ao = jnp.concatenate([a[...].astype(F32) for a in (a0, a1, a2, a3)], 0)
            mu_a = jnp.mean(ao, axis=0, keepdims=True)
            power = jnp.mean(ao * ao, axis=0, keepdims=True)
            rs_a = lax.rsqrt(power - mu_a * mu_a + EPSILON)
            ahat = (ao - mu_a) * rs_a
            ga = jnp.broadcast_to(ga_r[...], (128, width)).T[:, :1]
            an_t = (ahat * ga).astype(BF)
            an_o[...] = an_t
            for r, w in enumerate(ws):
                if r < 2:
                    need(6 + r)
                elif r == 2:
                    for copy in copies:
                        copy.wait()
                w_out_s[r * cols : (r + 1) * cols, :] = w[:cols, :]
            hid_s[...] = x_r[...].astype(F32) + dot(turned(an_t).astype(BF), w_out_s[...])
            g2 = g2_r[...]
            vf_o[...] = jnp.zeros((n_head, ff_part), F32)
            v2_o[...] = jnp.zeros((1, width), F32)
            for c in range(quarter // chunk):
                span = slice(c * chunk, (c + 1) * chunk)
                hid = hid_s[span, :]
                mu2 = jnp.mean(hid, axis=-1, keepdims=True)
                centred = hid - mu2
                rs2 = lax.rsqrt(jnp.mean(centred * centred, axis=-1, keepdims=True) + EPSILON)
                xhat2 = centred * rs2
                hn = (xhat2 * g2).astype(BF)
                hn_o[span, :] = hn
                if c == 0:
                    need(8)
                dy_c = dy_r[span, :]
                sums = [jnp.zeros((chunk, 1), F32)] * 4
                for r, w in enumerate(ws):
                    u = dot(hn, w[cols : cols + width, :])
                    bell = jnp.exp(u * u * -0.5)
                    t = 1.0 / (1.0 + jnp.abs(u) * (ERF_P / math.sqrt(2.0)))
                    poly = ERF_C[4]
                    for coefficient in ERF_C[3::-1]:
                        poly = poly * t + coefficient
                    tail = poly * t * bell * 0.5
                    phi = jnp.where(u >= 0.0, 1.0 - tail, tail)
                    gu = u * phi
                    dgn = dot_nt(dy_c, w[cols + width :, :])
                    c_g = dgn * gf_r[r : r + 1, :]
                    gu_s[r] = gu
                    slope_s[r] = phi + u * bell * GAUSS_NORM
                    dgn_s[r] = dgn
                    terms = (gu, gu * gu, c_g, c_g * gu)
                    sums = [a + jnp.sum(b, axis=-1, keepdims=True) for a, b in zip(sums, terms)]
                mu_g = sums[0] / full_ff
                rs_g = lax.rsqrt(sums[1] / full_ff - mu_g * mu_g + EPSILON)
                m1 = sums[2] / full_ff
                m2 = (sums[3] - mu_g * sums[2]) * rs_g / full_ff
                y = hid
                dhn = jnp.zeros((chunk, width), F32)
                for r, w in enumerate(ws):
                    gf = gf_r[r : r + 1, :]
                    ghat = (gu_s[r] - mu_g) * rs_g
                    dgn = dgn_s[r]
                    gn = (ghat * gf).astype(BF)
                    du = (rs_g * (dgn * gf - m1 - ghat * m2) * slope_s[r]).astype(BF)
                    gn_o[slot[r], span, :] = gn
                    du_o[slot[r], span, :] = du
                    vf_o[r : r + 1, :] += jnp.sum(dgn * ghat, axis=0, keepdims=True)
                    y = y + dot(gn, w[cols + width :, :])
                    dhn = dhn + dot_nt(du, w[cols : cols + width, :])
                y_o[span, :] = y.astype(BF)
                v2_o[...] += jnp.sum(dhn * xhat2, axis=0, keepdims=True)
                c2 = dhn * g2
                dh = dy_c.astype(F32) + rs2 * (
                    c2
                    - jnp.mean(c2, axis=-1, keepdims=True)
                    - xhat2 * jnp.mean(c2 * xhat2, axis=-1, keepdims=True)
                )
                dh_o[span, :] = dh
                dhb_o[span, :] = dh.astype(BF)
            for k in (0, 1, 2, 3, 4, 5, 10):
                done(k)
            dan = dot_nt(w_out_s[...], dhb_o[...])
            column = jnp.sum(dan * ahat, axis=-1, keepdims=True)
            va_o[...] = jnp.broadcast_to(column, (width, 128)).T[:1]
            c_a = dan * ga
            dao = rs_a * (
                c_a
                - jnp.mean(c_a, axis=0, keepdims=True)
                - ahat * jnp.mean(c_a * ahat, axis=0, keepdims=True)
            )
            for r, o in enumerate((dao0, dao1, dao2, dao3)):
                o[...] = dao[r * cols : (r + 1) * cols].astype(BF)

        y_rows, an_t, dhb, hn2, gn, du, *dao_low, dh, v_attn, v_ffn, v_ln2 = call(
            row_kernel,
            [
                ("s", s_ref),
                ("h", x_in),
                *[("l", a) for a in ao_rows],
                ("l", w_own),
                ("l", w_core),
                ("l", dy_own),
                ("v", gain_attn),
                ("v", gain_ffn),
                ("v", g2_row),
                *[("r", w) for w in (*w_side, *w_diag)],
            ],
            [
                ("h", shaped((quarter, width), BF)),
                ("h", shaped((width, quarter), BF)),
                ("h", shaped((quarter, width), BF)),
                ("h", shaped((quarter, width), BF)),
                ("h", shaped((n_head, quarter, ff_part), BF)),
                ("h", shaped((n_head, quarter, ff_part), BF)),
                *[("v", shaped((cols, quarter), BF))] * n_head,
                ("h", shaped((quarter, width), F32)),
                ("v", shaped((1, width), F32)),
                ("v", shaped((n_head, ff_part), F32)),
                ("v", shaped((1, width), F32)),
            ],
            scratch=[
                pltpu.VMEM((n_head, chunk, ff_part), F32),
                pltpu.VMEM((n_head, chunk, ff_part), F32),
                pltpu.VMEM((n_head, chunk, ff_part), F32),
                pltpu.VMEM((width, width), BF),
                pltpu.VMEM((quarter, width), F32),
                pltpu.VMEM((w_rows, width), BF),
                pltpu.VMEM((w_rows, width), BF),
                pltpu.SemaphoreType.DMA((4 * PIECES,)),
            ],
            margin=14,
            name="rows",
        )
        output = y_rows[None]
        dao_blocks = exchange(dao_low)


        def weights_kernel(
            need, done, gn_r, dy_r, hn_r, du_r, an_r, dhb_r, send_o, own_o, side_o, send_i, keep_i
        ):
            need(1)
            for n, o in enumerate((send_o.at[0], send_o.at[1], own_o, side_o)):
                need(0, n)
                o[...] = dot_tn(gn_r[n], dy_r[...]).astype(BF)
                done(*((0, n) if n < 2 else (n - 1, 0)))
            for i in (2, 4, 5):
                need(i)
            for n, r in enumerate(order):
                need(3, n)
                o = send_i if n < 2 else keep_i
                o[n % 2, :width] = dot_tn(hn_r[...], du_r[n]).astype(BF)
                rows = an_r[r * cols : (r + 1) * cols, :]
                o[n % 2, width:] = dot(rows, dhb_r[...]).astype(BF)
                done(3 + n // 2, n % 2)

        one = ("h", shaped((ff_part, width), BF))
        two = ("b", shaped((2, width + cols, width), BF))
        ffo_send, ffo_own, ffo_side, in_send, in_keep = call(
            weights_kernel,
            [("b", gn), ("l", dy_own), ("l", hn2), ("b", du), ("l", an_t), ("l", dhb)],
            [("b", shaped((2, ff_part, width), BF)), one, one, two, two],
            name="weight_gradients",
        )

        def plus(*terms):
            return sum(t.astype(F32) for t in terms).astype(BF)

        class Half:
            def __init__(self, terms, bit):
                self.terms = [t if isinstance(t, tuple) else (t, None) for t in terms]
                self.bit = bit
                self.size = self.terms[0][0].shape[-2] // 2

            def shapes(self):
                return [("v", shaped((self.size, width), BF))] * 2

            def buffers(self):
                return 2 * len(self.terms)

            def start(self, index, ins, outs, bufs, begin):
                upper = (index // self.bit) % 2
                for n, (_, lead) in enumerate(self.terms):
                    ref = ins[n] if lead is None else ins[n].at[lead]
                    for m, at in enumerate(((1 - upper) * self.size, upper * self.size)):
                        begin(ref.at[pl.ds(pl.multiple_of(at, 8), self.size)], bufs[2 * n + m])

            def plain(self):
                found = []
                upper = (s // self.bit) % 2
                for at in ((1 - upper) * self.size, upper * self.size):
                    parts = [t if lead is None else t[lead] for t, lead in self.terms]
                    parts = [lax.dynamic_slice_in_dim(t, at, self.size, 0) for t in parts]
                    found.append(plus(*parts))
                return found

            def finish(self, outs, bufs):
                for m in range(2):
                    parts = [bufs[2 * n + m][...].astype(F32) for n in range(len(self.terms))]
                    outs[m][...] = sum(parts[1:], parts[0]).astype(BF)

        class Joined:
            def __init__(self, own, got, bit):
                self.terms = [(own, None), (got, None)]
                self.bit = bit
                self.size = own.shape[0]

            def shapes(self):
                return [("v", shaped((2 * self.size, width), BF))]

            def buffers(self):
                return 0

            def start(self, index, ins, outs, bufs, begin):
                upper = (index // self.bit) % 2
                for ref, at in zip(ins, (upper * self.size, (1 - upper) * self.size)):
                    begin(ref, outs[0].at[pl.ds(pl.multiple_of(at, 8), self.size)])

            def plain(self):
                own, got = [t for t, _ in self.terms]
                upper = (s // self.bit) % 2 == 1
                return [
                    jnp.where(upper, jnp.concatenate([got, own], 0), jnp.concatenate([own, got], 0))
                ]

            def finish(self, outs, bufs):
                pass

        def combine(jobs):
            made = combine_tiles([job for job in jobs if job.size % 8 == 0])
            return [made.pop(0) if job.size % 8 == 0 else job.plain() for job in jobs]

        def combine_tiles(jobs):
            if not jobs:
                return []
            n_in = [len(job.terms) for job in jobs]
            n_out = [len(job.shapes()) for job in jobs]
            n_buf = [job.buffers() for job in jobs]
            total = sum(max(job.buffers(), len(job.terms)) for job in jobs)

            def kernel(need, done, s_r, *refs):
                index = s_r[0]
                ins = refs[: sum(n_in)]
                outs = refs[sum(n_in) : sum(n_in) + sum(n_out)]
                bufs = refs[sum(n_in) + sum(n_out) : -1]
                semaphores = refs[-1]
                found = []

                def begin(source, target):
                    copy = pltpu.make_async_copy(source, target, semaphores.at[len(found)])
                    copy.start()
                    found.append(copy)

                work = []
                a = b = c = 0
                for n, job in enumerate(jobs):
                    mine = (outs[b : b + n_out[n]], bufs[c : c + n_buf[n]])
                    before = len(found)
                    job.start(index, ins[a : a + n_in[n]], *mine, begin)
                    work.append((job, mine, found[before:]))
                    a, b, c = a + n_in[n], b + n_out[n], c + n_buf[n]
                for job, mine, copies in work:
                    for copy in copies:
                        copy.wait()
                    job.finish(*mine)

            results = call(
                kernel,
                [("s", s_ref), *[("a", t) for job in jobs for t, _ in job.terms]],
                [o for job in jobs for o in job.shapes()],
                scratch=[
                    *[
                        pltpu.VMEM((job.size, width), BF)
                        for job in jobs
                        for _ in range(job.buffers())
                    ],
                    pltpu.SemaphoreType.DMA((total,)),
                ],
                name="combine",
            )
            found = []
            at = 0
            for n in n_out:
                found.append(results[at : at + n])
                at += n
            return found

        n_note = 3 * heads
        note_rows = (3 * n_note + 15) // 16 * 16

        def prepare_kernel(
            need, done, h_s, d0, d1, d2, d3, ao_r, q_r, l_r, start_r, do_o, delta_o, sent_o, ddil_o, dt_s
        ):
            hv = h_s[0]
            for r, d in enumerate((d0, d1, d2, d3)):
                need(1 + r)
                base = pl.multiple_of((hv ^ r) * quarter, quarter)
                dt_s[:, pl.ds(base, quarter)] = d[...]
            dao_v = dt_s[...].astype(F32)
            grown = jnp.concatenate([dao_v, jnp.zeros((LANES - cols, tokens), F32)], 0)
            do_o[...] = grown.T.astype(BF)
            need(5)
            prod = dao_v * ao_r[...]
            sent_o[:cols, :] = q_r[...]
            for l in range(heads):
                sel = spread(hv, l)
                at = cols + l * HEAD_SIZE
                sent_o[at : at + HEAD_SIZE, :] = dot_nt(dt_s[of_head(l), :], sel).astype(BF)
                delta = jnp.sum(prod[of_head(l)], axis=0, keepdims=True)
                delta_o[l : l + 1, :] = delta
                d8 = jnp.broadcast_to(delta, (8, tokens))
                ddil_o[l : l + 1, :] = sum(dot_nt(t, sel) for t in thirds(d8))[:1]
            found = [l_r[l : l + 1, :] for l in range(heads)]
            found += [ddil_o[l : l + 1, :] for l in range(heads)]
            found += [start_r[l : l + 1, :].astype(F32) for l in range(heads)]
            row = iota((note_rows, rows_dil), 0)
            notes = jnp.zeros((note_rows, rows_dil), F32)
            for n, value in enumerate(found):
                for t, piece in enumerate(thirds(value)):
                    notes = jnp.where(row == t * n_note + n, piece.astype(F32), notes)
            sent_o[2 * cols :, :] = notes.astype(BF)

        do_a, delta_all, far_note, delta_dil = call(
            prepare_kernel,
            [
                ("s", h_ref),
                ("m", fence(dao_blocks[0], ffo_send, in_send)),
                *[("m", d) for d in dao_blocks[1:]],
                ("l", ao_t),
                ("v", dil_q),
                ("v", l_dil),
                ("v", start_dil),
            ],
            [
                ("p", shaped((tokens, LANES), BF)),
                ("v", shaped((heads, tokens), F32)),
                ("v", shaped((2 * cols + note_rows, rows_dil), BF)),
                ("v", shaped((heads, rows_dil), F32)),
            ],
            scratch=[pltpu.VMEM((cols, tokens), BF)],
            name="prepare_backward",
        )

        def near_back_kernel(part, need, done, q_r, k_r, v_r, kt_r, do_r, l_r, d_r, *rest):
            dq_o, dk_o, dv_o, token_o = rest[-4:]
            fresh = len(rest) == 4
            token_o[...] = jnp.zeros((8, 128), F32)
            for n, i in enumerate(reversed(part)):
                span = slice(i * BLOCK, (i + 1) * BLOCK)
                q_i = stack_heads(q_r[span, :])
                do_i = stack_heads(do_r[span, :])
                lse_i = jnp.concatenate([l_r[l : l + 1, span] for l in range(heads)], 1)
                del_i = jnp.concatenate([d_r[l : l + 1, span] for l in range(heads)], 1)
                dq_i = [None] * heads
                for j in range(i + 1):
                    keys = slice(j * BLOCK, (j + 1) * BLOCK)
                    pr = jnp.exp(dot_nt(k_r[keys, :], q_i) - lse_i)
                    if j == i:
                        pr = jnp.where(causal_block(), pr, 0.0)
                    dp = dot_nt(v_r[keys, :], do_i)
                    ds = (pr * (dp - del_i)).astype(BF)
                    dv = dot(pr.astype(BF), do_i)
                    dk = dot(ds, q_i)
                    if fresh and n == 0:
                        dv_o[keys, :] = dv
                        dk_o[keys, :] = dk
                    else:
                        dv_o[keys, :] += dv
                        dk_o[keys, :] += dk
                    for l in range(heads):
                        add = dot(kt_r[of_head(l), keys], ds[:, l * BLOCK : (l + 1) * BLOCK])
                        dq_i[l] = add if dq_i[l] is None else dq_i[l] + add
                for l in range(heads):
                    dq_o[of_head(l), span] = dq_i[l]

        grown_to = []

        def back_work(part):
            def work(value, *after):
                after = [value, *after]
                if part is parts[0]:
                    in_y = fence(flying["in_y"], value)
                    flying["in_got"] = swap(in_y, "seq", rising[0])
                    after += [flying["ffo_x"], in_y]
                held = [("p", a) for a in grown_to]
                *grown_to[:], token = call(
                    lambda *refs: near_back_kernel(part, *refs),
                    [
                        ("p", q_a),
                        ("p", k_a),
                        ("p", v_a),
                        ("p", k_t),
                        ("p", do_a),
                        ("v", l_all),
                        ("v", delta_all),
                        *held,
                    ],
                    [
                        ("p", shaped((cols, tokens), F32)),
                        ("p", shaped((tokens, LANES), F32)),
                        ("p", shaped((tokens, LANES), F32)),
                        ("v", shaped((8, 128), F32)),
                    ],
                    name="near_backward",
                    margin=20,
                    aliases={7 + n: n for n in range(len(held))},
                    after=after,
                )
                return None, token

            return work

        ffo_send, in_send, _ = lax.optimization_barrier((ffo_send, in_send, far_note))
        ffo_core = swap(ffo_send, "head", 1)
        in_core = swap(in_send, "head", 1)
        flying = {}

        def start_sums(value):
            flying["ffo_x"] = plus(ffo_side, ffo_core[1])
            upper = (s & rising[0]) != 0
            size = (width + cols) // 2
            away = jnp.where(upper, 0, size)
            flying["in_y"], flying["in_own"] = [
                plus(*[lax.dynamic_slice_in_dim(t, at, size, 1) for t in (in_keep, in_core)])
                for at in (away, size - away)
            ]
            flying["ffo_got"] = swap(flying["ffo_x"], "head", 2)
            return None, delta_dil

        far_q, _, tokens_back = gather_seq(
            far_note, [start_sums, *[back_work(part) for part in parts]], "v"
        )
        dq_near, dk_near, dv_near = grown_to
        ffo_got, in_got, *tokens_back = lax.optimization_barrier(
            (flying["ffo_got"], flying["in_got"], *tokens_back)
        )
        (ffo_z, ffo_kept), _ = combine([Half([ffo_own, (ffo_core, 0), ffo_got], rising[1])]) + [None]
        in_x = plus(in_got[1], flying["in_own"][1])
        ffo_z_got = swap(ffo_z, "seq", rising[1])
        in_x_got = swap(in_x, "head", 2)

        def far_back_kernel(need, done, *refs):
            p_s, kv_r, fq_r, start_r, l_r, d_r = refs[:6]
            dqn_r, dkn_r, dvn_r, w_r, x_r, g_r, send_o, keep_o, away_o, stay_o, v_o, d_o, dq_s, dk_s, dv_s = refs[6:]
            hv = p_s[0]
            sv = p_s[1]

            def rows_of(ref, b, first):
                return turned(ref[b, first : first + cols]).astype(BF)

            q_v = stack_dil(rows_of(fq_r, 0, 0))
            do_v = stack_dil(rows_of(fq_r, 0, cols))
            k_own = rows_of(kv_r, 0, 0)
            v_own = rows_of(kv_r, 0, cols)
            start_v = start_r[...]
            l_v = jnp.concatenate([l_r[l : l + 1, :] for l in range(heads)], 1)
            d_v = jnp.concatenate([d_r[l : l + 1, :] for l in range(heads)], 1)
            dq_s[...] = jnp.zeros_like(dq_s)
            dk_s[...] = jnp.zeros_like(dk_s)
            dv_s[...] = jnp.zeros_like(dv_s)

            @pl.loop(0, n_far)
            def _(b):
                owner = p_s[2 + b]

                @pl.when(owner <= sv)
                def _():
                    key, query = far_place(p_s, owner, sv)
                    keep = (key <= query) & (key >= start_v)
                    sc = dot_nt(rows_of(kv_r, b, 0), q_v)
                    pr = jnp.where(keep, jnp.exp(sc - l_v), 0.0)
                    dp = dot_nt(rows_of(kv_r, b, cols), do_v)
                    ds = (pr * (dp - d_v)).astype(BF)
                    for l in range(heads):
                        cut = slice(l * rows_dil, (l + 1) * rows_dil)
                        dq_s[of_head(l), :] += dot(kv_r[b, of_head(l)], ds[:, cut])

                @pl.when(owner >= sv)
                def _():
                    note = fq_r[b, 2 * cols :].astype(F32)

                    def row(kind):
                        found = []
                        for l in range(heads):
                            at = kind * heads + l
                            found.append(
                                sum(note[at + t * n_note : at + t * n_note + 1] for t in range(3))
                            )
                        return jnp.concatenate(found, 1)

                    key, query = far_place(p_s, sv, owner)
                    keep = (key <= query) & (key >= row(2).astype(jnp.int32))
                    q_b = stack_dil(rows_of(fq_r, b, 0))
                    do_b = stack_dil(rows_of(fq_r, b, cols))
                    sc = dot_nt(k_own, q_b)
                    pr = jnp.where(keep, jnp.exp(sc - row(0)), 0.0)
                    dp = dot_nt(v_own, do_b)
                    ds = (pr * (dp - row(1))).astype(BF)
                    dk_s[...] += dot(ds, q_b)
                    dv_s[...] += dot(pr.astype(BF), do_b)

            dk_t = turned(dk_s[...])
            dv_t = turned(dv_s[...])

            def placed(value, l):
                high, low = halves(value[of_head(l)])
                put = spread(hv, l)
                return dot(high, put) + dot(low, put)

            dk_near = dkn_r[...].T
            dv_near = dvn_r[...].T
            scale = HEAD_SIZE**-0.5
            dq_far = dq_s[...]
            for l in range(heads):
                rows = of_head(l)
                d_o[rows, :] = ((dqn_r[rows, :] + placed(dq_far, l)) * scale).astype(BF)
                at = cols + l * HEAD_SIZE
                d_o[at : at + HEAD_SIZE, :] = (dk_near[rows] + placed(dk_t, l)).astype(BF)
                at += cols
                d_o[at : at + HEAD_SIZE, :] = (dv_near[rows] + placed(dv_t, l)).astype(BF)
            for o, n, r in ((send_o, 0, 3), (send_o, 1, 1), (keep_o, 0, 2), (keep_o, 1, 0)):
                base = pl.multiple_of((hv ^ r) * quarter, quarter)
                o[n] = dot_tn(d_o[:, pl.ds(base, quarter)], w_r[...]).astype(o.dtype)
            need(10)
            part = dot(d_o[...], x_r[...])
            half = 3 * cols // 2
            for upper in (0, 1):

                @pl.when(lax.rem(sv, 2) == upper)
                def _():
                    away_o[...] = part[(1 - upper) * half : (2 - upper) * half].astype(BF)
                    stay_o[...] = part[upper * half : (1 + upper) * half].astype(BF)

            v_o[...] = jnp.sum(part * w_r[...].astype(F32), axis=0, keepdims=True) / g_r[...]

        dxn_send, dxn_keep, qkv_away, qkv_stay, v_ln1 = call(
            far_back_kernel,
            [
                ("s", place),
                ("h", far_kv),
                ("v", far_q),
                ("v", start_row),
                ("v", l_dil),
                ("v", delta_dil),
                ("p", dq_near),
                ("p", dk_near),
                ("p", dv_near),
                ("v", w_turn),
                ("l", x_all),
                ("v", g1_row),
            ],
            [
                ("v", shaped((2, quarter, width), BF)),
                ("v", shaped((2, quarter, width), F32)),
                ("v", shaped((3 * cols // 2, width), BF)),
                ("v", shaped((3 * cols // 2, width), BF)),
                ("v", shaped((1, width), F32)),
            ],
            scratch=[
                pltpu.VMEM((3 * cols, tokens), BF),
                pltpu.VMEM((cols, rows_dil), F32),
                pltpu.VMEM((rows_dil, cols), F32),
                pltpu.VMEM((rows_dil, cols), F32),
            ],
            margin=12,
            name="far_backward",
            after=(ffo_z, in_x, *tokens_back),
        )

        dxn_send, ffo_z_got, in_x_got = lax.optimization_barrier((dxn_send, ffo_z_got, in_x_got))

        def sum_rows():
            got = yield dxn_send, "head", 1, 1
            side = (dxn_keep[0] + got[0].astype(F32)).astype(BF)
            over_x = yield side, "head", 2, 3

            def last_kernel(need, done, x_r, g_r, keep_r, got_r, over_r, dh_r, o):
                xhat, rs = normed(x_r[...].astype(F32))
                dxn = keep_r[1] + got_r[1].astype(F32) + over_r[...].astype(F32)
                c = dxn * g_r[...]
                first = jnp.mean(c, axis=-1, keepdims=True)
                second = jnp.mean(c * xhat, axis=-1, keepdims=True)
                o[...] = dh_r[...] + rs * (c - first - xhat * second)

            (result,) = call(
                last_kernel,
                [("v", x_in), ("v", g1_row), ("v", dxn_keep), ("v", got), ("v", over_x), ("v", dh)],
                [("v", shaped((quarter, width), F32))],
                margin=12,
                name="first_norm_backward",
            )
            return result

        def sum_seq(terms, scatter, spread, slow=()):
            for bit in scatter:
                send, kept = yield Half(terms, bit)
                terms = [kept, (yield send, "seq", bit, 1)]
            value = None
            for bit in spread:
                if value is None:
                    value = plus(*terms)
                rounds = 2 if bit in slow else 1
                got = yield value, "seq", bit, rounds
                (value,) = yield Joined(value, got, bit)
            return value

        def sum_ffo():
            bits = rising[2:] + rising[:1]
            terms = [ffo_kept, ffo_z_got]
            value = yield from sum_seq(terms, bits, bits[::-1] + rising[1:2], rising[2:3])
            return value.astype(F32)

        def sum_in():
            terms = [(in_got, 0), (flying["in_own"], 0), in_x_got]
            value = yield from sum_seq(terms, rising[1:], rising[::-1], rising[:1])
            return value[:width].astype(F32), value[width:].astype(F32)

        def sum_qkv():
            got = yield qkv_away, "seq", rising[0], 1
            return (yield from sum_seq([qkv_stay, got], rising[1:], rising[::-1]))

        def sum_small():
            v_rel = jnp.concatenate([v_attn.reshape(n_head, cols), v_ffn], 1)
            size = v_rel.shape[1]
            common = jnp.concatenate([v_ln1.reshape(-1), v_ln2.reshape(-1), lse_sums[:2].reshape(-1)])
            got = yield jnp.concatenate([v_rel[1], v_rel[3], common]), "head", 1, 1
            mine = v_rel[0] + got[:size]
            other = v_rel[2] + got[size : 2 * size]
            common = common + got[2 * size :]
            got = yield jnp.concatenate([other, common]), "head", 2, 1
            small = jnp.concatenate([mine, common]) + got
            for bit in rising:
                small = small + (yield small, "seq", bit, 1)
            total_heads = heads * n_head
            counts = jnp.array([tokens * n_seq * total_heads, rows_dil * n_seq * total_heads], F32)
            means = jnp.sum(small[size + 2 * width :].reshape(2, 128), axis=1) / counts
            return (
                small[:cols],
                small[cols:size],
                small[size : size + width],
                small[size + width : size + 2 * width],
                means,
            )

        def in_rounds(chains):
            results = [None] * len(chains)
            large = (1, 2, 3)
            asks = {}
            flying = {}
            ended = []

            def resume(n, value):
                try:
                    asks[n] = chains[n].send(value)
                except StopIteration as stop:
                    results[n] = stop.value
                    ended.append(n)

            def settle():
                jobs = [n for n in asks if not isinstance(asks[n], tuple)]
                if jobs:
                    for n, made in zip(jobs, combine([asks.pop(n) for n in jobs])):
                        resume(n, made)

            for n in range(len(chains)):
                resume(n, None)
            number = 0
            while asks or flying:
                settle()
                quick = [asks[n][0] for n in large if n in asks and asks[n][3] == 1]
                for n in list(asks)[::-1] if number == 0 else list(asks):
                    value, axis, bit, rounds = asks.pop(n)
                    if n in large and rounds > 1 and quick:
                        value = fence(value, quick[-1])
                    flying[n] = (number + rounds - 1, swap(value, axis, bit))
                due = [n for n in flying if flying[n][0] <= number]
                held = tuple(flying.pop(n)[1] for n in due)
                flat, tree = jax.tree.flatten((held, [results[n] for n in ended]))
                held, again = jax.tree.unflatten(tree, lax.optimization_barrier(tuple(flat)))
                for n, value in zip(ended, again):
                    results[n] = value
                for n, got in zip(due, held):
                    if n in large:
                        resume(n, got)
                settle()
                sent = [asks[n][0] for n in large if n in asks]
                for n, got in zip(due, held):
                    if n not in large:
                        resume(n, fence(got, sent[0]) if sent else got)
                number += 1
            return results

        dx, g_ffo, (g_in, g_out), g_qkv, (g_sub_attn, g_sub_ffn, g_ln1, g_ln2, means) = in_rounds(
            [sum_rows(), sum_ffo(), sum_in(), sum_qkv(), sum_small()]
        )
        g_qkv = g_qkv.astype(F32).reshape(3, cols, width).transpose(0, 2, 1)
        return (
            output,
            dx[None],
            g_ln1,
            g_qkv,
            g_sub_attn,
            g_out,
            g_ln2,
            g_in,
            g_sub_ffn,
            g_ffo,
            means,
        )

    return jax.shard_map(
        body,
        mesh=mesh,
        in_specs=(
            P("head", "seq", None),
            P("seq"),
            P(),
            P(None, None, "head"),
            P("head"),
            P("head", None),
            P(),
            P(None, "head"),
            P("head"),
            P("head", None),
            P("seq", None),
        ),
        out_specs=(
            P("head", "seq", None),
            P("head", "seq", None),
            P(),
            P(None, None, "head"),
            P("head"),
            P("head", None),
            P(),
            P(None, "head"),
            P("head"),
            P("head", None),
            P(),
        ),
        check_vma=False,
    )
```

```python
import math

import jax
import jax.numpy as jnp
from jax import lax
from jax.experimental import pallas as pl
from jax.experimental.pallas import tpu as pltpu
from jax.sharding import PartitionSpec as P

HEAD_SIZE = 64
DILATION_RATE = 16
EPSILON = 1e-05
NEGATIVE = -1e30
APART = -(2.0**30)
DOC_MIN = 256
GAUSS_NORM = 1.0 / math.sqrt(2.0 * math.pi)
BLOCK = 256
LANES = 256
BF = jnp.bfloat16
F32 = jnp.float32
ERF_P = 0.3275911
ERF_C = (0.254829592, -0.284496736, 1.421413741, -1.453152027, 1.061405429)
SPLIT = 3
PIECES = 2
CHUNK = 256


def dot(a, b):
    return lax.dot_general(a, b, (((1,), (0,)), ((), ())), preferred_element_type=F32)


def dot_nt(a, b):
    return lax.dot_general(a, b, (((1,), (1,)), ((), ())), preferred_element_type=F32)


def dot_tn(a, b):
    return lax.dot_general(a, b, (((0,), (0,)), ((), ())), preferred_element_type=F32)


def iota(shape, axis):
    return lax.broadcasted_iota(jnp.int32, shape, axis)


def halves(value):
    high = value.astype(BF)
    return high, (value - high.astype(F32)).astype(BF)


def thirds(value):
    high = value.astype(BF)
    rest = value - high.astype(F32)
    middle = rest.astype(BF)
    return high, middle, (rest - middle.astype(F32)).astype(BF)


def fence(value, *before):
    return lax.optimization_barrier((value, *before))[0]


def turned(value):
    return value.astype(F32).T


def room(shape, dtype):
    shape = (1,) * (2 - len(shape)) + tuple(shape)
    size = jnp.dtype(dtype).itemsize
    lanes = (shape[-1] + 127) // 128 * 128
    rows = (shape[-2] + 15) // 16 * 16
    return math.prod(shape[:-2]) * rows * lanes * size


def call(kernel, ins, outs, scratch=(), margin=8, name=None, aliases=None, after=()):
    n_in, n_out, n_after = len(ins), len(outs), len(after)
    spaces = {"s": pltpu.SMEM, "v": pltpu.VMEM, "p": pltpu.VMEM, "a": pl.ANY, "r": pltpu.HBM}
    far_in = [i for i, (kind, _) in enumerate(ins) if kind not in spaces]
    far_out = [i for i, (kind, _) in enumerate(outs) if kind not in spaces]
    n_far = len(far_in) + len(far_out)
    far = [ins[i] for i in far_in] + [outs[i] for i in far_out]
    buffers = [pltpu.VMEM(a.shape, a.dtype) for _, a in far]
    counts = [a.shape[0] if kind == "b" else 1 for kind, a in far]

    def wrapped(*refs):
        refs = (*refs[:n_in], *refs[n_in + n_after :])
        given, results, rest = list(refs[:n_in]), list(refs[n_in : n_in + n_out]), refs[n_in + n_out :]
        arriving, leaving, started = {}, {}, []

        def copies(kind, n, source, target):
            semaphores = rest[n_far]
            first = sum(counts[:n])
            if kind != "b":
                return {0: pltpu.make_async_copy(source, target, semaphores.at[first])}
            return {
                m: pltpu.make_async_copy(source.at[m], target.at[m], semaphores.at[first + m])
                for m in range(counts[n])
            }

        for n, i in enumerate(far_in):
            arriving[i] = copies(ins[i][0], n, given[i], rest[n])
            for copy in arriving[i].values():
                copy.start()
            given[i] = rest[n]
        for n, i in enumerate(far_out, len(far_in)):
            leaving[i] = copies(outs[i][0], n, rest[n], results[i])
            results[i] = rest[n]

        def need(i, m=0):
            arriving[i].pop(m).wait()

        def done(i, m=0):
            copy = leaving[i].pop(m)
            copy.start()
            started.append(copy)

        for i in far_in:
            if ins[i][0] == "h":
                need(i)
        own = rest[n_far + 1 :] if n_far else rest
        kernel(need, done, *given, *results, *own)
        for i in far_in:
            for m in list(arriving[i]):
                need(i, m)
        for i in far_out:
            for m in list(leaving[i]):
                done(i, m)
        for copy in started:
            copy.wait()

    held = [(a.shape, a.dtype) for kind, a in ins if kind not in "spar"]
    held += [(a.shape, a.dtype) for kind, a in outs if kind != "p"]
    held += [(a.shape, a.dtype) for a in scratch if jnp.issubdtype(a.dtype, jnp.number)]
    limit = sum(room(*a) for a in held) + (margin << 20)

    def placed(kind, a):
        if kind in "svam":
            return a
        return pltpu.with_memory_space_constraint(a, spaces.get(kind, pltpu.HBM))

    def shape_of(kind, a):
        if kind == "v":
            return a
        return spaces.get(kind, pltpu.HBM)(a.shape, a.dtype)

    return pl.pallas_call(
        wrapped,
        out_shape=tuple(shape_of(*o) for o in outs),
        in_specs=[
            pl.BlockSpec(memory_space=pl.ANY if kind == "m" else spaces.get(kind, pltpu.HBM))
            for kind, _ in ins
        ]
        + [pl.BlockSpec(memory_space=pl.ANY)] * n_after,
        out_specs=tuple(pl.BlockSpec(memory_space=spaces.get(kind, pltpu.HBM)) for kind, _ in outs),
        scratch_shapes=[
            *buffers,
            *([pltpu.SemaphoreType.DMA((sum(counts),))] if n_far else []),
            *scratch,
        ],
        input_output_aliases=aliases or {},
        compiler_params=pltpu.CompilerParams(vmem_limit_bytes=limit),
        cost_estimate=pl.CostEstimate(flops=0, transcendentals=0, bytes_accessed=0),
        name=name,
    )(*[placed(*a) for a in ins], *after)


def solution(mesh):
    n_head = mesh.shape["head"]
    n_seq = mesh.shape["seq"]

    def swap(value, axis, bit):
        size = n_head if axis == "head" else n_seq
        return lax.ppermute(value, axis, [(i, i ^ bit) for i in range(size)])

    rising = []
    bit = 1
    while bit < n_seq:
        rising.append(bit)
        bit *= 2
    seq_bits = rising[:1] + rising[:0:-1]

    offsets = [0]
    for bit in seq_bits:
        offsets = offsets + [o ^ bit for o in offsets]

    def body(
        layer_input,
        document_start,
        ln1_gain,
        w_qkv,
        sub_gain_attn,
        w_out,
        ln2_gain,
        w_in,
        sub_gain_ffn,
        w_ffo,
        dy,
    ):
        tokens, width = dy.shape
        quarter = layer_input.shape[1]
        cols = w_qkv.shape[2]
        heads = cols // HEAD_SIZE
        rows_dil = tokens // DILATION_RATE
        ff_part = w_in.shape[1]
        n_blocks = tokens // BLOCK
        n_far = n_seq
        h = lax.axis_index("head")
        s = lax.axis_index("seq")
        h_ref = jnp.reshape(h, (1,)).astype(jnp.int32)
        s_ref = jnp.reshape(s, (1,)).astype(jnp.int32)
        far_index = (s ^ jnp.array(offsets, jnp.int32)).astype(jnp.int32)
        place = jnp.concatenate([jnp.stack([h, s]).astype(jnp.int32), far_index])
        shaped = jax.ShapeDtypeStruct

        parts = [[] for _ in range(SPLIT)]
        for i in reversed(range(n_blocks)):
            min(parts, key=lambda part: sum(k + 1 for k in part)).append(i)
        parts = [sorted(part) for part in parts if part]
        n_parts = len(parts)
        home = {i: (p, n) for p, part in enumerate(parts) for n, i in enumerate(part)}

        def stacked(value, got, kind):
            size = value.shape[0]

            def stack_kernel(need, done, v_r, g_r, o_r, semaphores):
                copies = [
                    pltpu.make_async_copy(v_r, o_r.at[:size], semaphores.at[0]),
                    pltpu.make_async_copy(g_r, o_r.at[size:], semaphores.at[1]),
                ]
                for copy in copies:
                    copy.start()
                for copy in copies:
                    copy.wait()

            return call(
                stack_kernel,
                [("a", value), ("a", got)],
                [(kind, shaped((2 * size, *value.shape[1:]), value.dtype))],
                scratch=[pltpu.SemaphoreType.DMA((2,))],
                name="stack",
            )[0]

        def gather_seq(value, works, kind):
            value = value[None]
            results = []
            tokens = ()
            for n in range(max(len(seq_bits), len(works))):
                got = swap(value, "seq", seq_bits[n]) if n < len(seq_bits) else None
                if n < len(works):
                    result, token = works[n](value, *tokens)
                    results.append(result)
                    tokens = (token,)
                    if got is not None:
                        got, *tokens = lax.optimization_barrier((got, token))
                if got is not None:
                    value = stacked(value, got, kind if n == len(seq_bits) - 1 else "v")
            return value, results, tokens

        x_in = layer_input[0]

        def normed(value):
            mu = jnp.mean(value, axis=-1, keepdims=True)
            centred = value - mu
            rs = lax.rsqrt(jnp.mean(centred * centred, axis=-1, keepdims=True) + EPSILON)
            return centred * rs, rs

        def norm_kernel(need, done, x_r, g_r, o):
            o[...] = (normed(x_r[...].astype(F32))[0] * g_r[...]).astype(BF)

        g1_row = ln1_gain.reshape(1, -1)
        (xn,) = call(
            norm_kernel,
            [("h", x_in), ("v", g1_row)],
            [("h", shaped((quarter, width), BF))],
            margin=8,
            name="first_norm",
        )
        xn_core = swap(xn, "head", 1)
        xn_x = swap(xn, "head", 2)

        gain_part = fence(jnp.concatenate([sub_gain_attn, sub_gain_ffn]).reshape(1, -1), xn)
        gain_pair = jnp.concatenate([gain_part, swap(gain_part, "head", 1)], 0)
        gain_rel = jnp.concatenate([gain_pair, swap(gain_pair, "head", 2)], 0)
        gain_attn = gain_rel[:, :cols].reshape(1, width)
        g2_row = ln2_gain.reshape(1, -1)
        gain_ffn = gain_rel[:, cols:]
        w_own = jnp.concatenate([w_out, w_in, w_ffo], 0)
        w_core = swap(w_own, "head", 1)
        dy_own = lax.dynamic_slice_in_dim(dy, h * quarter, quarter, 0)

        seg_begin = s * tokens
        doc = jnp.clip((document_start - seg_begin) // DOC_MIN + 1, 0, tokens // DOC_MIN)
        lane = jnp.arange(LANES, dtype=jnp.int32)[None, :]
        same = lane - cols == doc[:, None]
        feature_lane = lane >= cols
        k_feat = jnp.where(same, 1.0, 0.0).astype(BF)
        q_feat = jnp.where(feature_lane & ~same, APART, 0.0).astype(BF)
        shift = (h * heads + jnp.arange(heads, dtype=jnp.int32)) % DILATION_RATE
        start_grid = document_start.reshape(rows_dil, DILATION_RATE)
        pick = jnp.arange(DILATION_RATE, dtype=jnp.int32)[:, None] == shift[None, :]
        start_dil = jnp.sum(jnp.where(pick[None], start_grid[:, :, None], 0), axis=1).T
        start_row = start_dil.reshape(1, heads * rows_dil)

        w_pad = jnp.pad(w_qkv, ((0, 0), (0, 0), (0, LANES - cols)))
        w_turn = w_qkv.transpose(0, 2, 1).reshape(3 * cols, width)
        w_rows = w_own.shape[0]
        piece = w_rows // (2 * PIECES)
        my_half = (s % 2) * (w_rows // 2)
        w_cut = [
            lax.dynamic_slice_in_dim(w_own, my_half + n * piece, piece, 0) for n in range(PIECES)
        ]
        xn_x = fence(
            xn_x, w_pad, w_turn, q_feat, k_feat, *w_cut, dy_own, start_row, gain_attn, gain_ffn, g2_row
        )
        xn_diag = swap(xn_x, "head", 1)
        w_half = [swap(w, "head", 2) for w in lax.optimization_barrier((*w_cut, xn_x))[:PIECES]]

        def head_shift(h_value, l):
            return lax.rem(h_value * heads + l, DILATION_RATE)

        def spread(h_value, l):
            a = iota((rows_dil, tokens), 0)
            p = iota((rows_dil, tokens), 1)
            return jnp.where(p == a * DILATION_RATE + head_shift(h_value, l), 1.0, 0.0).astype(BF)

        def of_head(l):
            return slice(l * HEAD_SIZE, (l + 1) * HEAD_SIZE)

        def project_kernel(
            need, done, h_s, b0, b1, b2, b3, w_r, qf, kf,
            q_o, k_o, v_o, kt_o, vt_o, x_o, dil_kv, dil_q, qt_s,
        ):
            hv = h_s[0]
            for i in (5, 6, 7):
                need(i)
            for r, b in enumerate((b0, b1, b2, b3)):
                base = pl.multiple_of((hv ^ r) * quarter, quarter)
                span = pl.ds(base, quarter)
                need(1 + r)
                xb = b[...]
                x_o[span, :] = xb
                qv = dot(xb, w_r[0]).astype(BF) * BF(HEAD_SIZE**-0.5)
                q_o[span, :] = qv + qf[span, :]
                kv = dot(xb, w_r[1]).astype(BF)
                k_o[span, :] = kv + kf[span, :]
                vv = dot(xb, w_r[2]).astype(BF)
                v_o[span, :] = vv
                qt_s[:, span] = turned(qv)[:cols].astype(BF)
                kt_o[:, span] = turned(kv)[:cols].astype(BF)
                vt_o[:, span] = turned(vv)[:cols].astype(BF)
            done(5)
            for l in range(heads):
                sel = spread(hv, l)
                dil_q[of_head(l), :] = dot_nt(qt_s[of_head(l), :], sel).astype(BF)
                dil_kv[of_head(l), :] = dot_nt(kt_o[of_head(l), :], sel).astype(BF)
                dil_kv[cols + l * HEAD_SIZE : cols + (l + 1) * HEAD_SIZE, :] = dot_nt(
                    vt_o[of_head(l), :], sel
                ).astype(BF)

        q_a, k_a, v_a, k_t, v_t, x_all, dil_kv, dil_q = call(
            project_kernel,
            [
                ("s", h_ref),
                ("m", xn),
                ("m", xn_core),
                ("m", xn_x),
                ("m", xn_diag),
                ("l", w_pad),
                ("l", q_feat),
                ("l", k_feat),
            ],
            [
                ("p", shaped((tokens, LANES), BF)),
                ("p", shaped((tokens, LANES), BF)),
                ("p", shaped((tokens, LANES), BF)),
                ("p", shaped((cols, tokens), BF)),
                ("v", shaped((cols, tokens), BF)),
                ("h", shaped((tokens, width), BF)),
                ("v", shaped((2 * cols, rows_dil), BF)),
                ("v", shaped((cols, rows_dil), BF)),
            ],
            scratch=[pltpu.VMEM((cols, tokens), BF)],
            name="project",
        )

        def stack_heads(value, size=heads):
            keep = iota(value.shape, 1) // HEAD_SIZE
            zero = jnp.zeros_like(value)
            return jnp.concatenate(
                [jnp.where((keep == l) | (keep >= size), value, zero) for l in range(size)], 0
            )

        wide = heads * BLOCK

        def causal_block():
            return iota((BLOCK, wide), 0) <= iota((BLOCK, wide), 1) % BLOCK

        def near_kernel(part, need, done, q_r, k_r, vt_r, o_o, lse_o):
            for n, i in enumerate(part):
                q_i = stack_heads(q_r[i * BLOCK : (i + 1) * BLOCK, :])
                top = total = None
                outs = None
                for j in [i] + list(range(i)):
                    sc = dot_nt(k_r[j * BLOCK : (j + 1) * BLOCK, :], q_i)
                    if j == i:
                        sc = jnp.where(causal_block(), sc, NEGATIVE)
                    part_top = jnp.max(sc, axis=0, keepdims=True)
                    new_top = part_top if top is None else jnp.maximum(top, part_top)
                    pr = jnp.exp(sc - new_top)
                    part_sum = jnp.sum(pr, axis=0, keepdims=True)
                    pb = pr.astype(BF)
                    fresh = [
                        dot(
                            vt_r[of_head(l), j * BLOCK : (j + 1) * BLOCK],
                            pb[:, l * BLOCK : (l + 1) * BLOCK],
                        )
                        for l in range(heads)
                    ]
                    if top is None:
                        total, outs = part_sum, fresh
                    else:
                        shrink = jnp.exp(top - new_top)
                        total = total * shrink + part_sum
                        outs = [
                            o * shrink[:, l * BLOCK : (l + 1) * BLOCK] + f
                            for l, (o, f) in enumerate(zip(outs, fresh))
                        ]
                    top = new_top
                lse = top + jnp.log(total)
                inv = 1.0 / total
                for l in range(heads):
                    cut = slice(l * BLOCK, (l + 1) * BLOCK)
                    o_o[of_head(l), n * BLOCK : (n + 1) * BLOCK] = outs[l] * inv[:, cut]
                    lse_o[l : l + 1, n * BLOCK : (n + 1) * BLOCK] = lse[:, cut]

        near_lse = []

        def near_work(part):
            def work(*after):
                size = len(part) * BLOCK
                after = [*after, *w_half[len(near_lse) - 1 : len(near_lse)]]
                result = call(
                    lambda *refs: near_kernel(part, *refs),
                    [("p", q_a), ("p", k_a), ("v", v_t)],
                    [("v", shaped((cols, size), F32)), ("v", shaped((heads, size), F32))],
                    name="near_forward",
                    margin=24,
                    after=after,
                )
                near_lse.append(result[1])
                return result, result[1]

            return work

        far_kv, near_out, _ = gather_seq(dil_kv, [near_work(part) for part in parts], "h")
        w_other = [
            swap(fence(w, near_lse[min(n, n_parts - 1)]), "seq", 1) for n, w in enumerate(w_half)
        ]
        near_o = [o for o, _ in near_out]

        def joined(refs, rows):
            pieces = []
            for i in range(n_blocks):
                p, n = home[i]
                pieces.append(refs[p][rows, n * BLOCK : (n + 1) * BLOCK])
            return jnp.concatenate(pieces, 1)

        def stack_dil(value):
            keep = iota(value.shape, 1) // HEAD_SIZE
            zero = jnp.zeros_like(value)
            return jnp.concatenate([jnp.where(keep == l, value, zero) for l in range(heads)], 0)

        far_wide = heads * rows_dil

        def far_place(p_s, key_owner, query_owner):
            col = iota((rows_dil, far_wide), 1)
            off = lax.rem(p_s[0] * heads + col // rows_dil, DILATION_RATE)
            key = key_owner * tokens + iota((rows_dil, far_wide), 0) * DILATION_RATE + off
            query = query_owner * tokens + (col % rows_dil) * DILATION_RATE + off
            return key, query

        def far_kernel(need, done, *refs):
            p_s, q_r, kv_r, start_r = refs[:4]
            o_r = refs[4 : 4 + n_parts]
            lse_r = refs[4 + n_parts : 4 + 2 * n_parts]
            ao_o, l_o, ldil_o, sum_o, *aob, top_s, total_s, out_s, low_s = refs[4 + 2 * n_parts :]
            hv = p_s[0]
            sv = p_s[1]
            q_v = stack_dil(turned(q_r[...]).astype(BF))
            start_v = start_r[...]
            top_s[...] = jnp.full((8, far_wide), NEGATIVE, F32)
            total_s[...] = jnp.zeros((8, far_wide), F32)
            out_s[...] = jnp.zeros((HEAD_SIZE, far_wide), F32)

            @pl.loop(0, n_far)
            def _(b):
                owner = p_s[2 + b]

                @pl.when(owner <= sv)
                def _():
                    top = top_s[:1]
                    sc = dot_nt(turned(kv_r[b, :cols]).astype(BF), q_v)
                    key, query = far_place(p_s, owner, sv)
                    sc = jnp.where((key <= query) & (key >= start_v), sc, NEGATIVE)
                    new_top = jnp.maximum(top, jnp.max(sc, axis=0, keepdims=True))
                    pr = jnp.exp(sc - new_top)
                    shrink = jnp.exp(top - new_top)
                    total_s[:1] = total_s[:1] * shrink + jnp.sum(pr, axis=0, keepdims=True)
                    pb = pr.astype(BF)
                    fresh = jnp.concatenate(
                        [
                            dot(
                                kv_r[b, cols + l * HEAD_SIZE : cols + (l + 1) * HEAD_SIZE],
                                pb[:, l * rows_dil : (l + 1) * rows_dil],
                            )
                            for l in range(heads)
                        ],
                        1,
                    )
                    out_s[...] = out_s[...] * shrink + fresh
                    top_s[:1] = new_top

            sum_o[...] = jnp.zeros((8, 128), F32)
            total = total_s[:1]
            lse_far = top_s[:1] + jnp.log(total)
            out = out_s[...] / total
            for l in range(heads):
                cut = slice(l * rows_dil, (l + 1) * rows_dil)
                rows = of_head(l)
                lf = lse_far[:, cut]
                sum_o[1:2, :] += lf
                put = spread(hv, l)
                l8 = jnp.broadcast_to(lf, (8, rows_dil))
                full_lf = sum(dot(t, put) for t in thirds(l8))[:1]
                high, low = halves(out[:, cut])
                full_o = dot(high, put) + dot(low, put)
                dilated = iota((1, tokens), 1) % DILATION_RATE == head_shift(hv, l)
                ln = joined(lse_r, slice(l, l + 1))
                for part in range(tokens // 128):
                    sum_o[:1, :] += ln[:, part * 128 : (part + 1) * 128]
                peak = jnp.maximum(ln, full_lf)
                both = peak + jnp.log(jnp.exp(ln - peak) + jnp.exp(full_lf - peak))
                tot = jnp.where(dilated, both, ln)
                w_near = jnp.exp(ln - tot)
                w_far = jnp.where(dilated, jnp.exp(full_lf - tot), 0.0)
                ao = joined(o_r, rows) * w_near + full_o * w_far
                ao_o[rows, :] = ao
                low_s[rows, :] = ao.astype(BF)
                l_o[l : l + 1, :] = tot
                t8 = jnp.broadcast_to(tot, (8, tokens))
                ldil_o[l : l + 1, :] = sum(dot_nt(t, put) for t in thirds(t8))[:1]
            for r, o in enumerate(aob):
                base = pl.multiple_of((hv ^ r) * quarter, quarter)
                o[...] = low_s[:, pl.ds(base, quarter)]

        ao_t, l_all, l_dil, lse_sums, *ao_low = call(
            far_kernel,
            [
                ("s", place),
                ("v", dil_q),
                ("h", far_kv),
                ("v", start_row),
                *[("v", o) for o in near_o],
                *[("v", lse) for lse in near_lse],
            ],
            [
                ("h", shaped((cols, tokens), F32)),
                ("h", shaped((heads, tokens), F32)),
                ("h", shaped((heads, rows_dil), F32)),
                ("h", shaped((8, 128), F32)),
                ("h", shaped((cols, quarter), BF)),
                *[("v", shaped((cols, quarter), BF))] * (n_head - 1),
            ],
            scratch=[
                pltpu.VMEM((8, far_wide), F32),
                pltpu.VMEM((8, far_wide), F32),
                pltpu.VMEM((HEAD_SIZE, far_wide), F32),
                pltpu.VMEM((cols, tokens), BF),
            ],
            name="far_forward",
            after=w_other[:1],
        )

        def exchange(pieces):
            return [pieces[0]] + [swap(pieces[r], "head", r) for r in range(1, n_head)]

        ao_rows = exchange(ao_low)
        *w_side, _ = lax.optimization_barrier((*w_half, *w_other, ao_low[0]))
        w_diag = [swap(w, "head", 1) for w in w_side]

        full_ff = ff_part * n_head
        chunk = min(CHUNK, quarter)
        order = (1, 3, 0, 2)
        slot = {r: n for n, r in enumerate(order)}

        def row_kernel(
            need, done, s_r, x_r, a0, a1, a2, a3, w0, w1, dy_r, ga_r, gf_r, g2_r, *refs
        ):
            side, refs = refs[: 4 * PIECES], refs[4 * PIECES :]
            (
            y_o, an_o, dhb_o, hn_o, gn_o, du_o, dao0, dao1, dao2, dao3, dh_o, va_o, vf_o, v2_o,
            gu_s, slope_s, dgn_s, w_out_s, hid_s, w2, w3, semaphores,
            ) = refs
            ws = (w0, w1, w2, w3)
            copies = []
            for n, ref in enumerate(side):
                half = (s_r[0] + n // PIECES) % 2
                at = pl.multiple_of(half * (w_rows // 2) + n % PIECES * piece, 8)
                copy = pltpu.make_async_copy(
                    ref, ws[2 + n // (2 * PIECES)].at[pl.ds(at, piece)], semaphores.at[n]
                )
                copy.start()
                copies.append(copy)
            for i in range(2, 6):
                need(i)
            ao = jnp.concatenate([a[...].astype(F32) for a in (a0, a1, a2, a3)], 0)
            mu_a = jnp.mean(ao, axis=0, keepdims=True)
            power = jnp.mean(ao * ao, axis=0, keepdims=True)
            rs_a = lax.rsqrt(power - mu_a * mu_a + EPSILON)
            ahat = (ao - mu_a) * rs_a
            ga = jnp.broadcast_to(ga_r[...], (128, width)).T[:, :1]
            an_t = (ahat * ga).astype(BF)
            an_o[...] = an_t
            for r, w in enumerate(ws):
                if r < 2:
                    need(6 + r)
                elif r == 2:
                    for copy in copies:
                        copy.wait()
                w_out_s[r * cols : (r + 1) * cols, :] = w[:cols, :]
            hid_s[...] = x_r[...].astype(F32) + dot(turned(an_t).astype(BF), w_out_s[...])
            g2 = g2_r[...]
            vf_o[...] = jnp.zeros((n_head, ff_part), F32)
            v2_o[...] = jnp.zeros((1, width), F32)
            for c in range(quarter // chunk):
                span = slice(c * chunk, (c + 1) * chunk)
                hid = hid_s[span, :]
                mu2 = jnp.mean(hid, axis=-1, keepdims=True)
                centred = hid - mu2
                rs2 = lax.rsqrt(jnp.mean(centred * centred, axis=-1, keepdims=True) + EPSILON)
                xhat2 = centred * rs2
                hn = (xhat2 * g2).astype(BF)
                hn_o[span, :] = hn
                if c == 0:
                    need(8)
                dy_c = dy_r[span, :]
                sums = [jnp.zeros((chunk, 1), F32)] * 4
                for r, w in enumerate(ws):
                    u = dot(hn, w[cols : cols + width, :])
                    bell = jnp.exp(u * u * -0.5)
                    t = 1.0 / (1.0 + jnp.abs(u) * (ERF_P / math.sqrt(2.0)))
                    poly = ERF_C[4]
                    for coefficient in ERF_C[3::-1]:
                        poly = poly * t + coefficient
                    tail = poly * t * bell * 0.5
                    phi = jnp.where(u >= 0.0, 1.0 - tail, tail)
                    gu = u * phi
                    dgn = dot_nt(dy_c, w[cols + width :, :])
                    c_g = dgn * gf_r[r : r + 1, :]
                    gu_s[r] = gu
                    slope_s[r] = phi + u * bell * GAUSS_NORM
                    dgn_s[r] = dgn
                    terms = (gu, gu * gu, c_g, c_g * gu)
                    sums = [a + jnp.sum(b, axis=-1, keepdims=True) for a, b in zip(sums, terms)]
                mu_g = sums[0] / full_ff
                rs_g = lax.rsqrt(sums[1] / full_ff - mu_g * mu_g + EPSILON)
                m1 = sums[2] / full_ff
                m2 = (sums[3] - mu_g * sums[2]) * rs_g / full_ff
                y = hid
                dhn = jnp.zeros((chunk, width), F32)
                for r, w in enumerate(ws):
                    gf = gf_r[r : r + 1, :]
                    ghat = (gu_s[r] - mu_g) * rs_g
                    dgn = dgn_s[r]
                    gn = (ghat * gf).astype(BF)
                    du = (rs_g * (dgn * gf - m1 - ghat * m2) * slope_s[r]).astype(BF)
                    gn_o[slot[r], span, :] = gn
                    du_o[slot[r], span, :] = du
                    vf_o[r : r + 1, :] += jnp.sum(dgn * ghat, axis=0, keepdims=True)
                    y = y + dot(gn, w[cols + width :, :])
                    dhn = dhn + dot_nt(du, w[cols : cols + width, :])
                y_o[span, :] = y.astype(BF)
                v2_o[...] += jnp.sum(dhn * xhat2, axis=0, keepdims=True)
                c2 = dhn * g2
                dh = dy_c.astype(F32) + rs2 * (
                    c2
                    - jnp.mean(c2, axis=-1, keepdims=True)
                    - xhat2 * jnp.mean(c2 * xhat2, axis=-1, keepdims=True)
                )
                dh_o[span, :] = dh
                dhb_o[span, :] = dh.astype(BF)
            for k in (0, 1, 2, 3, 4, 5, 10):
                done(k)
            dan = dot_nt(w_out_s[...], dhb_o[...])
            column = jnp.sum(dan * ahat, axis=-1, keepdims=True)
            va_o[...] = jnp.broadcast_to(column, (width, 128)).T[:1]
            c_a = dan * ga
            dao = rs_a * (
                c_a
                - jnp.mean(c_a, axis=0, keepdims=True)
                - ahat * jnp.mean(c_a * ahat, axis=0, keepdims=True)
            )
            for r, o in enumerate((dao0, dao1, dao2, dao3)):
                o[...] = dao[r * cols : (r + 1) * cols].astype(BF)

        y_rows, an_t, dhb, hn2, gn, du, *dao_low, dh, v_attn, v_ffn, v_ln2 = call(
            row_kernel,
            [
                ("s", s_ref),
                ("h", x_in),
                *[("l", a) for a in ao_rows],
                ("l", w_own),
                ("l", w_core),
                ("l", dy_own),
                ("v", gain_attn),
                ("v", gain_ffn),
                ("v", g2_row),
                *[("r", w) for w in (*w_side, *w_diag)],
            ],
            [
                ("h", shaped((quarter, width), BF)),
                ("h", shaped((width, quarter), BF)),
                ("h", shaped((quarter, width), BF)),
                ("h", shaped((quarter, width), BF)),
                ("h", shaped((n_head, quarter, ff_part), BF)),
                ("h", shaped((n_head, quarter, ff_part), BF)),
                *[("v", shaped((cols, quarter), BF))] * n_head,
                ("h", shaped((quarter, width), F32)),
                ("v", shaped((1, width), F32)),
                ("v", shaped((n_head, ff_part), F32)),
                ("v", shaped((1, width), F32)),
            ],
            scratch=[
                pltpu.VMEM((n_head, chunk, ff_part), F32),
                pltpu.VMEM((n_head, chunk, ff_part), F32),
                pltpu.VMEM((n_head, chunk, ff_part), F32),
                pltpu.VMEM((width, width), BF),
                pltpu.VMEM((quarter, width), F32),
                pltpu.VMEM((w_rows, width), BF),
                pltpu.VMEM((w_rows, width), BF),
                pltpu.SemaphoreType.DMA((4 * PIECES,)),
            ],
            margin=14,
            name="rows",
        )
        output = y_rows[None]
        dao_blocks = exchange(dao_low)


        def weights_kernel(
            need, done, gn_r, dy_r, hn_r, du_r, an_r, dhb_r, send_o, own_o, side_o, send_i, keep_i
        ):
            need(1)
            for n, o in enumerate((send_o.at[0], send_o.at[1], own_o, side_o)):
                need(0, n)
                o[...] = dot_tn(gn_r[n], dy_r[...]).astype(BF)
                done(*((0, n) if n < 2 else (n - 1, 0)))
            for i in (2, 4, 5):
                need(i)
            for n, r in enumerate(order):
                need(3, n)
                o = send_i if n < 2 else keep_i
                o[n % 2, :width] = dot_tn(hn_r[...], du_r[n]).astype(BF)
                rows = an_r[r * cols : (r + 1) * cols, :]
                o[n % 2, width:] = dot(rows, dhb_r[...]).astype(BF)
                done(3 + n // 2, n % 2)

        one = ("h", shaped((ff_part, width), BF))
        two = ("b", shaped((2, width + cols, width), BF))
        ffo_send, ffo_own, ffo_side, in_send, in_keep = call(
            weights_kernel,
            [("b", gn), ("l", dy_own), ("l", hn2), ("b", du), ("l", an_t), ("l", dhb)],
            [("b", shaped((2, ff_part, width), BF)), one, one, two, two],
            name="weight_gradients",
        )

        def plus(*terms):
            return sum(t.astype(F32) for t in terms).astype(BF)

        class Half:
            def __init__(self, terms, bit):
                self.terms = [t if isinstance(t, tuple) else (t, None) for t in terms]
                self.bit = bit
                self.size = self.terms[0][0].shape[-2] // 2

            def shapes(self):
                return [("v", shaped((self.size, width), BF))] * 2

            def buffers(self):
                return 2 * len(self.terms)

            def start(self, index, ins, outs, bufs, begin):
                upper = (index // self.bit) % 2
                for n, (_, lead) in enumerate(self.terms):
                    ref = ins[n] if lead is None else ins[n].at[lead]
                    for m, at in enumerate(((1 - upper) * self.size, upper * self.size)):
                        begin(ref.at[pl.ds(pl.multiple_of(at, 8), self.size)], bufs[2 * n + m])

            def plain(self):
                found = []
                upper = (s // self.bit) % 2
                for at in ((1 - upper) * self.size, upper * self.size):
                    parts = [t if lead is None else t[lead] for t, lead in self.terms]
                    parts = [lax.dynamic_slice_in_dim(t, at, self.size, 0) for t in parts]
                    found.append(plus(*parts))
                return found

            def finish(self, outs, bufs):
                for m in range(2):
                    parts = [bufs[2 * n + m][...].astype(F32) for n in range(len(self.terms))]
                    outs[m][...] = sum(parts[1:], parts[0]).astype(BF)

        class Joined:
            def __init__(self, own, got, bit):
                self.terms = [(own, None), (got, None)]
                self.bit = bit
                self.size = own.shape[0]

            def shapes(self):
                return [("v", shaped((2 * self.size, width), BF))]

            def buffers(self):
                return 0

            def start(self, index, ins, outs, bufs, begin):
                upper = (index // self.bit) % 2
                for ref, at in zip(ins, (upper * self.size, (1 - upper) * self.size)):
                    begin(ref, outs[0].at[pl.ds(pl.multiple_of(at, 8), self.size)])

            def plain(self):
                own, got = [t for t, _ in self.terms]
                upper = (s // self.bit) % 2 == 1
                return [
                    jnp.where(upper, jnp.concatenate([got, own], 0), jnp.concatenate([own, got], 0))
                ]

            def finish(self, outs, bufs):
                pass

        def combine(jobs):
            made = combine_tiles([job for job in jobs if job.size % 8 == 0])
            return [made.pop(0) if job.size % 8 == 0 else job.plain() for job in jobs]

        def combine_tiles(jobs):
            if not jobs:
                return []
            n_in = [len(job.terms) for job in jobs]
            n_out = [len(job.shapes()) for job in jobs]
            n_buf = [job.buffers() for job in jobs]
            total = sum(max(job.buffers(), len(job.terms)) for job in jobs)

            def kernel(need, done, s_r, *refs):
                index = s_r[0]
                ins = refs[: sum(n_in)]
                outs = refs[sum(n_in) : sum(n_in) + sum(n_out)]
                bufs = refs[sum(n_in) + sum(n_out) : -1]
                semaphores = refs[-1]
                found = []

                def begin(source, target):
                    copy = pltpu.make_async_copy(source, target, semaphores.at[len(found)])
                    copy.start()
                    found.append(copy)

                work = []
                a = b = c = 0
                for n, job in enumerate(jobs):
                    mine = (outs[b : b + n_out[n]], bufs[c : c + n_buf[n]])
                    before = len(found)
                    job.start(index, ins[a : a + n_in[n]], *mine, begin)
                    work.append((job, mine, found[before:]))
                    a, b, c = a + n_in[n], b + n_out[n], c + n_buf[n]
                for job, mine, copies in work:
                    for copy in copies:
                        copy.wait()
                    job.finish(*mine)

            results = call(
                kernel,
                [("s", s_ref), *[("a", t) for job in jobs for t, _ in job.terms]],
                [o for job in jobs for o in job.shapes()],
                scratch=[
                    *[
                        pltpu.VMEM((job.size, width), BF)
                        for job in jobs
                        for _ in range(job.buffers())
                    ],
                    pltpu.SemaphoreType.DMA((total,)),
                ],
                name="combine",
            )
            found = []
            at = 0
            for n in n_out:
                found.append(results[at : at + n])
                at += n
            return found

        n_note = 3 * heads
        note_rows = (3 * n_note + 15) // 16 * 16

        def prepare_kernel(
            need, done, h_s, d0, d1, d2, d3, ao_r, q_r, l_r, start_r, do_o, delta_o, sent_o, ddil_o, dt_s
        ):
            hv = h_s[0]
            for r, d in enumerate((d0, d1, d2, d3)):
                need(1 + r)
                base = pl.multiple_of((hv ^ r) * quarter, quarter)
                dt_s[:, pl.ds(base, quarter)] = d[...]
            dao_v = dt_s[...].astype(F32)
            grown = jnp.concatenate([dao_v, jnp.zeros((LANES - cols, tokens), F32)], 0)
            do_o[...] = grown.T.astype(BF)
            need(5)
            prod = dao_v * ao_r[...]
            sent_o[:cols, :] = q_r[...]
            for l in range(heads):
                sel = spread(hv, l)
                at = cols + l * HEAD_SIZE
                sent_o[at : at + HEAD_SIZE, :] = dot_nt(dt_s[of_head(l), :], sel).astype(BF)
                delta = jnp.sum(prod[of_head(l)], axis=0, keepdims=True)
                delta_o[l : l + 1, :] = delta
                d8 = jnp.broadcast_to(delta, (8, tokens))
                ddil_o[l : l + 1, :] = sum(dot_nt(t, sel) for t in thirds(d8))[:1]
            found = [l_r[l : l + 1, :] for l in range(heads)]
            found += [ddil_o[l : l + 1, :] for l in range(heads)]
            found += [start_r[l : l + 1, :].astype(F32) for l in range(heads)]
            row = iota((note_rows, rows_dil), 0)
            notes = jnp.zeros((note_rows, rows_dil), F32)
            for n, value in enumerate(found):
                for t, piece in enumerate(thirds(value)):
                    notes = jnp.where(row == t * n_note + n, piece.astype(F32), notes)
            sent_o[2 * cols :, :] = notes.astype(BF)

        do_a, delta_all, far_note, delta_dil = call(
            prepare_kernel,
            [
                ("s", h_ref),
                ("m", fence(dao_blocks[0], ffo_send, in_send)),
                *[("m", d) for d in dao_blocks[1:]],
                ("l", ao_t),
                ("v", dil_q),
                ("v", l_dil),
                ("v", start_dil),
            ],
            [
                ("p", shaped((tokens, LANES), BF)),
                ("v", shaped((heads, tokens), F32)),
                ("v", shaped((2 * cols + note_rows, rows_dil), BF)),
                ("v", shaped((heads, rows_dil), F32)),
            ],
            scratch=[pltpu.VMEM((cols, tokens), BF)],
            name="prepare_backward",
        )

        def near_back_kernel(part, need, done, q_r, k_r, v_r, kt_r, do_r, l_r, d_r, *rest):
            dq_o, dk_o, dv_o, token_o = rest[-4:]
            fresh = len(rest) == 4
            token_o[...] = jnp.zeros((8, 128), F32)
            for n, i in enumerate(reversed(part)):
                span = slice(i * BLOCK, (i + 1) * BLOCK)
                q_i = stack_heads(q_r[span, :])
                do_i = stack_heads(do_r[span, :])
                lse_i = jnp.concatenate([l_r[l : l + 1, span] for l in range(heads)], 1)
                del_i = jnp.concatenate([d_r[l : l + 1, span] for l in range(heads)], 1)
                dq_i = [None] * heads
                for j in range(i + 1):
                    keys = slice(j * BLOCK, (j + 1) * BLOCK)
                    pr = jnp.exp(dot_nt(k_r[keys, :], q_i) - lse_i)
                    if j == i:
                        pr = jnp.where(causal_block(), pr, 0.0)
                    dp = dot_nt(v_r[keys, :], do_i)
                    ds = (pr * (dp - del_i)).astype(BF)
                    dv = dot(pr.astype(BF), do_i)
                    dk = dot(ds, q_i)
                    if fresh and n == 0:
                        dv_o[keys, :] = dv
                        dk_o[keys, :] = dk
                    else:
                        dv_o[keys, :] += dv
                        dk_o[keys, :] += dk
                    for l in range(heads):
                        add = dot(kt_r[of_head(l), keys], ds[:, l * BLOCK : (l + 1) * BLOCK])
                        dq_i[l] = add if dq_i[l] is None else dq_i[l] + add
                for l in range(heads):
                    dq_o[of_head(l), span] = dq_i[l]

        grown_to = []

        def back_work(part):
            def work(value, *after):
                after = [value, *after]
                if part is parts[0]:
                    in_y = fence(flying["in_y"], value)
                    flying["in_got"] = swap(in_y, "seq", rising[0])
                    after += [flying["ffo_x"], in_y]
                held = [("p", a) for a in grown_to]
                *grown_to[:], token = call(
                    lambda *refs: near_back_kernel(part, *refs),
                    [
                        ("p", q_a),
                        ("p", k_a),
                        ("p", v_a),
                        ("p", k_t),
                        ("p", do_a),
                        ("v", l_all),
                        ("v", delta_all),
                        *held,
                    ],
                    [
                        ("p", shaped((cols, tokens), F32)),
                        ("p", shaped((tokens, LANES), F32)),
                        ("p", shaped((tokens, LANES), F32)),
                        ("v", shaped((8, 128), F32)),
                    ],
                    name="near_backward",
                    margin=20,
                    aliases={7 + n: n for n in range(len(held))},
                    after=after,
                )
                return None, token

            return work

        ffo_send, in_send, _ = lax.optimization_barrier((ffo_send, in_send, far_note))
        ffo_core = swap(ffo_send, "head", 1)
        in_core = swap(in_send, "head", 1)
        flying = {}

        def start_sums(value):
            flying["ffo_x"] = plus(ffo_side, ffo_core[1])
            upper = (s & rising[0]) != 0
            size = (width + cols) // 2
            away = jnp.where(upper, 0, size)
            flying["in_y"], flying["in_own"] = [
                plus(*[lax.dynamic_slice_in_dim(t, at, size, 1) for t in (in_keep, in_core)])
                for at in (away, size - away)
            ]
            flying["ffo_got"] = swap(flying["ffo_x"], "head", 2)
            return None, delta_dil

        far_q, _, tokens_back = gather_seq(
            far_note, [start_sums, *[back_work(part) for part in parts]], "v"
        )
        dq_near, dk_near, dv_near = grown_to
        ffo_got, in_got, *tokens_back = lax.optimization_barrier(
            (flying["ffo_got"], flying["in_got"], *tokens_back)
        )
        (ffo_z, ffo_kept), _ = combine([Half([ffo_own, (ffo_core, 0), ffo_got], rising[1])]) + [None]
        in_x = plus(in_got[1], flying["in_own"][1])
        ffo_z_got = swap(ffo_z, "seq", rising[1])
        in_x_got = swap(in_x, "head", 2)

        def far_back_kernel(need, done, *refs):
            p_s, kv_r, fq_r, start_r, l_r, d_r = refs[:6]
            dqn_r, dkn_r, dvn_r, w_r, x_r, g_r, send_o, keep_o, away_o, stay_o, v_o, d_o, dq_s, dk_s, dv_s = refs[6:]
            hv = p_s[0]
            sv = p_s[1]

            def rows_of(ref, b, first):
                return turned(ref[b, first : first + cols]).astype(BF)

            q_v = stack_dil(rows_of(fq_r, 0, 0))
            do_v = stack_dil(rows_of(fq_r, 0, cols))
            k_own = rows_of(kv_r, 0, 0)
            v_own = rows_of(kv_r, 0, cols)
            start_v = start_r[...]
            l_v = jnp.concatenate([l_r[l : l + 1, :] for l in range(heads)], 1)
            d_v = jnp.concatenate([d_r[l : l + 1, :] for l in range(heads)], 1)
            dq_s[...] = jnp.zeros_like(dq_s)
            dk_s[...] = jnp.zeros_like(dk_s)
            dv_s[...] = jnp.zeros_like(dv_s)

            @pl.loop(0, n_far)
            def _(b):
                owner = p_s[2 + b]

                @pl.when(owner <= sv)
                def _():
                    key, query = far_place(p_s, owner, sv)
                    keep = (key <= query) & (key >= start_v)
                    sc = dot_nt(rows_of(kv_r, b, 0), q_v)
                    pr = jnp.where(keep, jnp.exp(sc - l_v), 0.0)
                    dp = dot_nt(rows_of(kv_r, b, cols), do_v)
                    ds = (pr * (dp - d_v)).astype(BF)
                    for l in range(heads):
                        cut = slice(l * rows_dil, (l + 1) * rows_dil)
                        dq_s[of_head(l), :] += dot(kv_r[b, of_head(l)], ds[:, cut])

                @pl.when(owner >= sv)
                def _():
                    note = fq_r[b, 2 * cols :].astype(F32)

                    def row(kind):
                        found = []
                        for l in range(heads):
                            at = kind * heads + l
                            found.append(
                                sum(note[at + t * n_note : at + t * n_note + 1] for t in range(3))
                            )
                        return jnp.concatenate(found, 1)

                    key, query = far_place(p_s, sv, owner)
                    keep = (key <= query) & (key >= row(2).astype(jnp.int32))
                    q_b = stack_dil(rows_of(fq_r, b, 0))
                    do_b = stack_dil(rows_of(fq_r, b, cols))
                    sc = dot_nt(k_own, q_b)
                    pr = jnp.where(keep, jnp.exp(sc - row(0)), 0.0)
                    dp = dot_nt(v_own, do_b)
                    ds = (pr * (dp - row(1))).astype(BF)
                    dk_s[...] += dot(ds, q_b)
                    dv_s[...] += dot(pr.astype(BF), do_b)

            dk_t = turned(dk_s[...])
            dv_t = turned(dv_s[...])

            def placed(value, l):
                high, low = halves(value[of_head(l)])
                put = spread(hv, l)
                return dot(high, put) + dot(low, put)

            dk_near = dkn_r[...].T
            dv_near = dvn_r[...].T
            scale = HEAD_SIZE**-0.5
            dq_far = dq_s[...]
            for l in range(heads):
                rows = of_head(l)
                d_o[rows, :] = ((dqn_r[rows, :] + placed(dq_far, l)) * scale).astype(BF)
                at = cols + l * HEAD_SIZE
                d_o[at : at + HEAD_SIZE, :] = (dk_near[rows] + placed(dk_t, l)).astype(BF)
                at += cols
                d_o[at : at + HEAD_SIZE, :] = (dv_near[rows] + placed(dv_t, l)).astype(BF)
            for o, n, r in ((send_o, 0, 3), (send_o, 1, 1), (keep_o, 0, 2), (keep_o, 1, 0)):
                base = pl.multiple_of((hv ^ r) * quarter, quarter)
                o[n] = dot_tn(d_o[:, pl.ds(base, quarter)], w_r[...]).astype(o.dtype)
            need(10)
            part = dot(d_o[...], x_r[...])
            half = 3 * cols // 2
            for upper in (0, 1):

                @pl.when(lax.rem(sv, 2) == upper)
                def _():
                    away_o[...] = part[(1 - upper) * half : (2 - upper) * half].astype(BF)
                    stay_o[...] = part[upper * half : (1 + upper) * half].astype(BF)

            v_o[...] = jnp.sum(part * w_r[...].astype(F32), axis=0, keepdims=True) / g_r[...]

        dxn_send, dxn_keep, qkv_away, qkv_stay, v_ln1 = call(
            far_back_kernel,
            [
                ("s", place),
                ("h", far_kv),
                ("v", far_q),
                ("v", start_row),
                ("v", l_dil),
                ("v", delta_dil),
                ("p", dq_near),
                ("p", dk_near),
                ("p", dv_near),
                ("v", w_turn),
                ("l", x_all),
                ("v", g1_row),
            ],
            [
                ("v", shaped((2, quarter, width), BF)),
                ("v", shaped((2, quarter, width), F32)),
                ("v", shaped((3 * cols // 2, width), BF)),
                ("v", shaped((3 * cols // 2, width), BF)),
                ("v", shaped((1, width), F32)),
            ],
            scratch=[
                pltpu.VMEM((3 * cols, tokens), BF),
                pltpu.VMEM((cols, rows_dil), F32),
                pltpu.VMEM((rows_dil, cols), F32),
                pltpu.VMEM((rows_dil, cols), F32),
            ],
            margin=12,
            name="far_backward",
            after=(ffo_z, in_x, *tokens_back),
        )

        dxn_send, ffo_z_got, in_x_got = lax.optimization_barrier((dxn_send, ffo_z_got, in_x_got))

        def sum_rows():
            got = yield dxn_send, "head", 1, 1
            side = (dxn_keep[0] + got[0].astype(F32)).astype(BF)
            over_x = yield side, "head", 2, 3

            def last_kernel(need, done, x_r, g_r, keep_r, got_r, over_r, dh_r, o):
                xhat, rs = normed(x_r[...].astype(F32))
                dxn = keep_r[1] + got_r[1].astype(F32) + over_r[...].astype(F32)
                c = dxn * g_r[...]
                first = jnp.mean(c, axis=-1, keepdims=True)
                second = jnp.mean(c * xhat, axis=-1, keepdims=True)
                o[...] = dh_r[...] + rs * (c - first - xhat * second)

            (result,) = call(
                last_kernel,
                [("v", x_in), ("v", g1_row), ("v", dxn_keep), ("v", got), ("v", over_x), ("v", dh)],
                [("v", shaped((quarter, width), F32))],
                margin=12,
                name="first_norm_backward",
            )
            return result

        def sum_seq(terms, scatter, spread, slow=()):
            for bit in scatter:
                send, kept = yield Half(terms, bit)
                terms = [kept, (yield send, "seq", bit, 1)]
            value = None
            for bit in spread:
                if value is None:
                    value = plus(*terms)
                rounds = 2 if bit in slow else 1
                got = yield value, "seq", bit, rounds
                (value,) = yield Joined(value, got, bit)
            return value

        def sum_ffo():
            bits = rising[2:] + rising[:1]
            terms = [ffo_kept, ffo_z_got]
            value = yield from sum_seq(terms, bits, bits[::-1] + rising[1:2], rising[2:3])
            return value.astype(F32)

        def sum_in():
            terms = [(in_got, 0), (flying["in_own"], 0), in_x_got]
            value = yield from sum_seq(terms, rising[1:], rising[::-1], rising[:1])
            return value[:width].astype(F32), value[width:].astype(F32)

        def sum_qkv():
            got = yield qkv_away, "seq", rising[0], 1
            return (yield from sum_seq([qkv_stay, got], rising[1:], rising[::-1]))

        def sum_small():
            v_rel = jnp.concatenate([v_attn.reshape(n_head, cols), v_ffn], 1)
            size = v_rel.shape[1]
            common = jnp.concatenate([v_ln1.reshape(-1), v_ln2.reshape(-1), lse_sums[:2].reshape(-1)])
            got = yield jnp.concatenate([v_rel[1], v_rel[3], common]), "head", 1, 1
            mine = v_rel[0] + got[:size]
            other = v_rel[2] + got[size : 2 * size]
            common = common + got[2 * size :]
            got = yield jnp.concatenate([other, common]), "head", 2, 1
            small = jnp.concatenate([mine, common]) + got
            for bit in rising:
                small = small + (yield small, "seq", bit, 1)
            total_heads = heads * n_head
            counts = jnp.array([tokens * n_seq * total_heads, rows_dil * n_seq * total_heads], F32)
            means = jnp.sum(small[size + 2 * width :].reshape(2, 128), axis=1) / counts
            return (
                small[:cols],
                small[cols:size],
                small[size : size + width],
                small[size + width : size + 2 * width],
                means,
            )

        def in_rounds(chains):
            results = [None] * len(chains)
            large = (1, 2, 3)
            asks = {}
            flying = {}
            ended = []

            def resume(n, value):
                try:
                    asks[n] = chains[n].send(value)
                except StopIteration as stop:
                    results[n] = stop.value
                    ended.append(n)

            def settle():
                jobs = [n for n in asks if not isinstance(asks[n], tuple)]
                if jobs:
                    for n, made in zip(jobs, combine([asks.pop(n) for n in jobs])):
                        resume(n, made)

            for n in range(len(chains)):
                resume(n, None)
            number = 0
            while asks or flying:
                settle()
                quick = [asks[n][0] for n in (*large, 4) if n in asks and asks[n][3] == 1]
                for n in list(asks)[::-1] if number == 0 else list(asks):
                    value, axis, bit, rounds = asks.pop(n)
                    if n in large and rounds > 1 and quick:
                        value = fence(value, *quick[-2:])
                    flying[n] = (number + rounds - 1, swap(value, axis, bit))
                due = [n for n in flying if flying[n][0] <= number]
                held = tuple(flying.pop(n)[1] for n in due)
                flat, tree = jax.tree.flatten((held, [results[n] for n in ended]))
                held, again = jax.tree.unflatten(tree, lax.optimization_barrier(tuple(flat)))
                for n, value in zip(ended, again):
                    results[n] = value
                for n, got in zip(due, held):
                    if n in large:
                        resume(n, got)
                settle()
                sent = [asks[n][0] for n in large if n in asks]
                for n, got in zip(due, held):
                    if n not in large:
                        resume(n, fence(got, sent[0]) if sent else got)
                number += 1
            return results

        dx, g_ffo, (g_in, g_out), g_qkv, (g_sub_attn, g_sub_ffn, g_ln1, g_ln2, means) = in_rounds(
            [sum_rows(), sum_ffo(), sum_in(), sum_qkv(), sum_small()]
        )
        g_qkv = g_qkv.astype(F32).reshape(3, cols, width).transpose(0, 2, 1)
        return (
            output,
            dx[None],
            g_ln1,
            g_qkv,
            g_sub_attn,
            g_out,
            g_ln2,
            g_in,
            g_sub_ffn,
            g_ffo,
            means,
        )

    return jax.shard_map(
        body,
        mesh=mesh,
        in_specs=(
            P("head", "seq", None),
            P("seq"),
            P(),
            P(None, None, "head"),
            P("head"),
            P("head", None),
            P(),
            P(None, "head"),
            P("head"),
            P("head", None),
            P("seq", None),
        ),
        out_specs=(
            P("head", "seq", None),
            P("head", "seq", None),
            P(),
            P(None, None, "head"),
            P("head"),
            P("head", None),
            P(),
            P(None, "head"),
            P("head"),
            P("head", None),
            P(),
        ),
        check_vma=False,
    )
```
